32 devices in a mesh: grp: 2 (over y), gx: 4 (over z), gy: 2 (over x), gz: 2 (over core).
Axes of the slice: x: 2, y: 2, z: 4, core: 2. Of those that a mesh axis runs over, the one named last changes fastest.
Arguments:
- pressure: float32 [64, 128, 256], P(('grp', 'gx'), 'gy', 'gz'), parts along dimension 0, may hold values from -3 to 3
- previous: float32 [64, 128, 256], P(('grp', 'gx'), 'gy', 'gz'), parts along dimension 0, may hold values from -3 to 3
- material: int32 [64, 128, 256], P(('grp', 'gx'), 'gy', 'gz'), parts along dimension 0, may hold values from 0 to 7
- stiffness: float32 [8], replicated, may hold values from 0.05 to 0.2
- density: float32 [8], replicated, may hold values from 1 to 2
- nonlinear: float32 [8], replicated, may hold values from 0.005 to 0.025
- lift_weight: float32 [4, 20], replicated, may hold values from -3 to 3
- lift_bias: float32 [20], replicated, may hold values from -3 to 3
- mode_weight: float32 [2, 8, 20, 20], replicated, may hold values from -2 to 2
- local_weight: bfloat16 [20, 20], replicated, may hold values from -1.25 to 1.25
Outputs:
- wave_field: float32 [64, 128, 256], P(('grp', 'gx'), 'gy', 'gz'), parts along dimension 0
- features: bfloat16 [64, 128, 20, 256], P(('grp', 'gx', 'gz'), 'gy'), parts along dimension 0
The draws below stay inside these ranges and needn't reach their ends.
There are 2 independent parts, one for each index of `grp`. The reference program is written for one: setup_inputs(seed, part) draws one part's arguments, and reference() takes and returns one part's arrays. A program takes and returns all parts, laid end to end along the dimension named above; an argument that names none is the same for every part. Nothing has to cross between parts.
All inputs are finite; a program needn't handle non-finite values.
Results may differ from the reference program's by a relative error of at most 0.0079.
Values may be sent and summed in bfloat16 or wider, within the bound.
No kernel may reach another device: no remote copies, remote signals or barrier semaphores. Data moves between devices by JAX's collectives and lax.ppermute only.
A program may use at most 64 MiB of HBM per device.

```python
import math
import jax
import jax.numpy as jnp
from jax import lax

BX = 8
C = 20
STEPS = 4
NMAT = 8
NX = 32
NY = 128
NZ = 256
MX = 8
MY = 32
MZ = 64


def plant(array, rng, low, largest):
    place = [jax.random.randint(jax.random.fold_in(rng, axis), (), 0, length) for axis, length in enumerate(array.shape)]
    longest = array.shape.index(max(array.shape))
    next_to = place[:longest] + [(place[longest] + 1) % array.shape[longest]] + place[longest + 1:]
    return array.at[tuple(place)].set(low).at[tuple(next_to)].set(largest)


def block_scale(stream_key, extent, cuts, smallest, top_value):
    loudness, own = 1.0, jax.random.fold_in(stream_key, 6)
    for dim, shards_of in cuts:
        heights = jnp.exp(jax.random.uniform(jax.random.fold_in(own, dim), (shards_of,), jnp.float32, smallest / len(cuts), top_value / len(cuts)))
        loudness = loudness * jnp.repeat(heights, extent[dim] // shards_of).reshape([-1 if axis == dim else 1 for axis in range(len(extent))])
    return loudness


def centred(stream_key, dims, scale, limit, shards=(), kind=jnp.bfloat16):
    result = scale * jax.random.normal(stream_key, dims, jnp.float32)
    if shards:
        result = result * block_scale(stream_key, dims, shards, -0.22, 0.18)
    return jnp.clip(result, -limit, limit).astype(kind)


def setup_inputs(seed: int = 0, part: int = 0) -> dict:
    splits = jax.random.split(jax.random.key(seed), 11)
    part_splits = jax.random.split(jax.random.fold_in(splits[10], part), 11)
    pressure = centred(part_splits[0], (NX, NY, NZ), 0.5, 3.0, ((0, 4), (1, 2), (2, 2)), jnp.float32)
    previous = centred(part_splits[1], (NX, NY, NZ), 0.5, 3.0, ((0, 4), (1, 2), (2, 2)), jnp.float32)
    material = plant(jax.random.randint(part_splits[2], (NX, NY, NZ), 0, NMAT), jax.random.fold_in(part_splits[2], 1), 0, NMAT - 1).astype(jnp.int32)
    stiffness = jnp.clip(jnp.exp(jax.random.uniform(splits[3], (NMAT,), jnp.float32, math.log(0.05), math.log(0.2))), 0.05, 0.2)
    density = jnp.clip(jnp.exp(jax.random.uniform(splits[4], (NMAT,), jnp.float32, math.log(1.0), math.log(2.0))), 1.0, 2.0)
    nonlinear = jnp.clip(jax.random.uniform(splits[5], (NMAT,), jnp.float32, 0.005, 0.025), 0.005, 0.025)
    lift_weight = centred(splits[6], (4, C), 0.5, 3.0, (), jnp.float32)
    lift_bias = centred(splits[7], (C,), 0.5, 3.0, (), jnp.float32)
    mode_weight = centred(splits[8], (2, MX, C, C), 0.3, 2.0, (), jnp.float32)
    local_weight = centred(splits[9], (C, C), C ** -0.5, 1.25)
    return {"pressure": pressure, "previous": previous, "material": material, "stiffness": stiffness, "density": density, "nonlinear": nonlinear, "lift_weight": lift_weight, "lift_bias": lift_bias, "mode_weight": mode_weight, "local_weight": local_weight}


stencil_taps = (-205.0 / 72.0, 8.0 / 5.0, -1.0 / 5.0, 8.0 / 315.0, -1.0 / 560.0)


def shifted(padded, dimension, offset):
    starts = [4, 4, 4]
    starts[dimension] = 4 + offset
    limits = [starts[position] + padded.shape[position] - 8 for position in range(3)]
    return lax.slice(padded, starts, limits)


def laplace(padded, center):
    running = (3.0 * stencil_taps[0]) * center
    for offset in range(1, 5):
        for dimension in range(3):
            running = running + stencil_taps[offset] * (shifted(padded, dimension, offset) + shifted(padded, dimension, -offset))
    return running


def advance(padded, before, ratio_inner, bend_inner):
    center = shifted(padded, 0, 0)
    change = center - before
    updated = 2.0 * center - before + ratio_inner * laplace(padded, center) + bend_inner * change * change
    return updated, center


def lift_features(pieces, lift_weight, lift_bias):
    running = lift_bias[None, :, None]
    for feature_id in range(4):
        running = running + pieces[feature_id][:, :, None, :] * lift_weight[feature_id][None, :, None]
    return running.astype(jnp.bfloat16)


def kept_modes(length, mode_count):
    position = jnp.arange(mode_count, dtype=jnp.int32)
    return jnp.where(position < mode_count // 2, position, length - mode_count + position).astype(jnp.int32)


def angle_of(source, target, length):
    product = (source[:, None] * target[None, :]) % length
    return (2.0 * math.pi / length) * product.astype(jnp.float32)


def twiddle(source, target, length, direction):
    phases = angle_of(source, target, length)
    cosine = jnp.cos(phases)
    sine = direction * jnp.sin(phases)
    return jnp.stack([jnp.stack([cosine, sine], -1), jnp.stack([-sine, cosine], -1)], 1).astype(jnp.bfloat16)


def depth_table(length, mode_count):
    phases = angle_of(jnp.arange(length, dtype=jnp.int32), jnp.arange(mode_count, dtype=jnp.int32), length)
    return jnp.stack([jnp.cos(phases), -jnp.sin(phases)], -1).astype(jnp.bfloat16)


def depth_inverse(length, mode_count):
    phases = angle_of(jnp.arange(mode_count, dtype=jnp.int32), jnp.arange(length, dtype=jnp.int32), length)
    weight = jnp.where(jnp.arange(mode_count, dtype=jnp.int32) == 0, 1.0, 2.0)[:, None]
    return jnp.stack([weight * jnp.cos(phases), -weight * jnp.sin(phases)], 1).astype(jnp.bfloat16)


def mode_mixer(mode_weight):
    real_part = mode_weight[0]
    imag_part = mode_weight[1]
    return jnp.stack([jnp.stack([real_part, imag_part], -1), jnp.stack([-imag_part, real_part], -1)], 2)


def reference(pressure, previous, material, stiffness, density, nonlinear, lift_weight, lift_bias, mode_weight, local_weight):
    ratio_field = (stiffness / density)[material]
    bend_field = nonlinear[material]
    stiff_field = stiffness[material]
    dense_field = density[material]
    current, before = pressure, previous
    for repeat in range(STEPS):
        current, before = advance(jnp.pad(current, 4), before, ratio_field, bend_field)
    forward_depth = depth_table(NZ, MZ).astype(jnp.float32)
    offsets = (jnp.arange(NX // BX, dtype=jnp.int32) * BX).astype(jnp.int32)

    def lifted_block(offset):
        pieces = [lax.dynamic_slice_in_dim(source, offset, BX, 0) for source in (current, before, stiff_field, dense_field)]
        return lift_features(pieces, lift_weight, lift_bias)

    def depth_block(offset):
        lifted = lifted_block(offset)
        return jnp.einsum("xycz,zkq->xyckq", lifted.astype(jnp.float32), forward_depth).astype(jnp.bfloat16)

    depth_modes = lax.map(depth_block, offsets).reshape(NX, NY, C, MZ, 2)
    kept_second = kept_modes(NY, MY)
    kept_first = kept_modes(NX, MX)
    second_table = twiddle(jnp.arange(NY, dtype=jnp.int32), kept_second, NY, -1.0).astype(jnp.float32)
    second_modes = jnp.einsum("xyckp,ypmq->xmckq", depth_modes.astype(jnp.float32), second_table).astype(jnp.bfloat16)
    first_table = twiddle(jnp.arange(NX, dtype=jnp.int32), kept_first, NX, -1.0).astype(jnp.float32)
    first_modes = jnp.einsum("xmckp,xpnq->nmckq", second_modes.astype(jnp.float32), first_table)
    mixed = jnp.einsum("nmckp,ncpoq->nmokq", first_modes, mode_mixer(mode_weight), precision=lax.Precision.HIGHEST).astype(jnp.bfloat16)
    first_inverse = twiddle(kept_first, jnp.arange(NX, dtype=jnp.int32), NX, 1.0).astype(jnp.float32)
    back_first = jnp.einsum("nmokp,npxq->xmokq", mixed.astype(jnp.float32), first_inverse).astype(jnp.bfloat16)
    second_inverse = twiddle(kept_second, jnp.arange(NY, dtype=jnp.int32), NY, 1.0).astype(jnp.float32)
    back_second = jnp.einsum("xmokp,mpyq->xyokq", back_first.astype(jnp.float32), second_inverse).astype(jnp.bfloat16)
    inverse_depth = depth_inverse(NZ, MZ).astype(jnp.float32)
    scale = 1.0 / (NX * NY * NZ)

    def output_block(offset):
        lifted = lifted_block(offset)
        mode_rows = lax.dynamic_slice_in_dim(back_second, offset, BX, 0)
        spectral = jnp.einsum("xyckq,kqz->xycz", mode_rows.astype(jnp.float32), inverse_depth) * scale
        local_part = jnp.einsum("xycz,co->xyoz", lifted.astype(jnp.float32), local_weight.astype(jnp.float32))
        return jax.nn.gelu(local_part + spectral, approximate=True).astype(jnp.bfloat16)

    features = lax.map(output_block, offsets).reshape(NX, NY, C, NZ)
    return (current, features)
```

```python
import math

import numpy as np
import jax
import jax.numpy as jnp
from jax import lax
from jax.experimental import pallas as pl
from jax.experimental.pallas import tpu as pltpu
from jax.sharding import PartitionSpec as P
import ml_dtypes

STEPS = 4
FIELDS = 4
REACH = 4
EDGE = 8
stencil_taps = (-205.0 / 72.0, 8.0 / 5.0, -1.0 / 5.0, 8.0 / 315.0, -1.0 / 560.0)
F32 = jnp.float32
BF16 = jnp.bfloat16
HIGHEST = lax.Precision.HIGHEST

VMEM = pl.BlockSpec(memory_space=pltpu.VMEM)
SMEM = pl.BlockSpec(memory_space=pltpu.SMEM)


def rounded(table):
    return table.astype(ml_dtypes.bfloat16)


def kept_modes(length, mode_count):
    position = np.arange(mode_count)
    return np.where(position < mode_count // 2, position, length - mode_count + position)


def cos_sin(source, target, length):
    product = (source[:, None] * target[None, :]) % length
    phases = np.float32(2.0 * math.pi / length) * product.astype(np.float32)
    return rounded(np.cos(phases)), rounded(np.sin(phases))


def call(body, outs, in_specs, scratch=(), flops=0, moved=0):
    return pl.pallas_call(
        body,
        out_shape=outs,
        in_specs=in_specs,
        out_specs=jax.tree.map(lambda _: VMEM, outs),
        scratch_shapes=list(scratch),
        compiler_params=pltpu.CompilerParams(vmem_limit_bytes=32 * 1024 * 1024),
        cost_estimate=pl.CostEstimate(flops=flops, bytes_accessed=moved, transcendentals=0),
    )


def high_low(value):
    high = value.astype(BF16)
    return high, (value - high.astype(F32)).astype(BF16)


def turned(value, half, sign):
    lane = lax.broadcasted_iota(jnp.int32, value.shape, value.ndim - 1)
    swapped = pltpu.roll(value, half, value.ndim - 1)
    return jnp.where(lane < half, sign * swapped, -sign * swapped)


def pack_body(where_ref, pressure, previous, material, send):
    core = where_ref[0] % 2
    rows = send.shape[1]
    start = (1 - core) * rows
    send[0] = pressure[pl.ds(start, rows)]
    send[1] = previous[pl.ds(start, rows)]
    send[2] = material[pl.ds(start, rows)].astype(F32)


def looked_up(material, table, entries):
    result = jnp.full(material.shape, table(0), F32)
    for entry in range(1, entries):
        result = jnp.where(material == float(entry), table(entry), result)
    return result


def edges(value_of, outs, row_parity, brick_y):
    for position, out in enumerate(outs):
        upper = row_parity == position
        out[...] = jnp.where(upper, value_of(brick_y - EDGE, brick_y), value_of(0, EDGE))


def assemble_body(where_ref, stiffness, density, nonlinear, pressure, previous, material, got, *outs):
    p_out, q_out, ratio, bend, stiff, dense = outs[:6]
    core = where_ref[0] % 2
    column = where_ref[1]
    rows, brick_y, half = got.shape[1:]
    start = core * rows
    entries = stiffness.shape[0]

    def whole(own, other):
        return jnp.concatenate(
            [jnp.where(core == 0, own, other), jnp.where(core == 0, other, own)], axis=-1
        )

    for row in range(rows):
        p_out[row] = whole(pressure[start + row], got[0, row])
        q_out[row] = whole(previous[start + row], got[1, row])
        cell = whole(material[start + row].astype(F32), got[2, row])
        ratio[row] = looked_up(cell, lambda e: stiffness[e] / density[e], entries)
        bend[row] = looked_up(cell, lambda e: nonlinear[e], entries)
        stiff[row] = looked_up(cell, lambda e: stiffness[e], entries)
        dense[row] = looked_up(cell, lambda e: density[e], entries)
    edges(lambda a, b: p_out[:, a:b, :], outs[6:], column % 2, brick_y)


def step_body(two_sided, last, where_ref, p_ref, q_ref, ratio, bend, mate, far, *rest):
    count = 2 if two_sided else 1
    halos = rest[:count]
    new_ref = rest[count]
    edge_outs = rest[count + 1 : -1]
    padded = rest[-1]
    core = where_ref[0] % 2
    parity = where_ref[1] % 2
    rows, brick_y, depth = p_ref.shape
    lane = lax.broadcasted_iota(jnp.int32, (brick_y, depth), 1)
    zero_edge = jnp.zeros((EDGE, depth), F32)

    def line(index):
        if 0 <= index < rows:
            return p_ref[index]
        if index < 0:
            return jnp.where(core == 0, far[index + rows], mate[index + rows])
        return jnp.where(core == 0, mate[index - rows], far[index - rows])

    for row in range(rows):
        first = halos[0][row]
        second = halos[1][row] if two_sided else zero_edge
        center = p_ref[row]
        padded[0:EDGE, :] = jnp.where(parity == 0, second, first)
        padded[EDGE : EDGE + brick_y, :] = center
        padded[EDGE + brick_y :, :] = jnp.where(parity == 0, first, second)
        total = (3.0 * stencil_taps[0]) * center
        for offset in range(1, REACH + 1):
            low, high = EDGE - offset, EDGE + offset
            pair = padded[low : low + brick_y, :] + padded[high : high + brick_y, :]
            pair = pair + (line(row - offset) + line(row + offset))
            pair = pair + jnp.where(lane >= offset, pltpu.roll(center, offset, 1), 0.0)
            pair = pair + jnp.where(
                lane < depth - offset, pltpu.roll(center, depth - offset, 1), 0.0
            )
            total = total + stencil_taps[offset] * pair
        change = center - q_ref[row]
        new_ref[row] = (center + change) + ratio[row] * total + bend[row] * change * change
    if last:
        half = depth // 2
        edge_outs[0][...] = jnp.where(core == 0, new_ref[:, :, half:], new_ref[:, :, :half])
    else:
        edges(lambda a, b: new_ref[:, a:b, :], edge_outs, parity, brick_y)


def spectrum_body(where_ref, twiddle_x, p_ref, q_ref, stiff, dense, table_z, table_y, keep, send, lines, grid):
    core = where_ref[0] % 2
    column = where_ref[1]
    rows, brick_y, depth = p_ref.shape
    modes_x, modes_y, width = keep.shape[1:]
    half = width // 2
    for field, ref in enumerate((p_ref, q_ref, stiff, dense)):
        for row in range(rows):
            high, low = high_low(ref[row])
            modes = jnp.dot(high, table_z[...], preferred_element_type=F32)
            modes = modes + jnp.dot(low, table_z[...], preferred_element_type=F32)
            back = turned(modes, half, 1.0)
            high, low = high_low(modes)
            back_high, back_low = high_low(back)
            lanes = slice((field * rows + row) * width, (field * rows + row + 1) * width)
            for index, part in enumerate((high, back_high, low, back_low)):
                lines[index * brick_y : (index + 1) * brick_y, lanes] = part
    grid[...] = jnp.dot(table_y[column], lines[...], preferred_element_type=F32)
    first = (where_ref[0] * rows) * modes_x * 2

    def sums(base_field, out, index):
        values, backs = [], []
        for row in range(rows):
            lanes = pl.ds(pl.multiple_of((base_field * rows + row) * width, width), width)
            value = grid[:, lanes]
            values.append(value)
            backs.append(turned(value, half, 1.0))

        @pl.loop(0, modes_x)
        def _(mode):
            total = jnp.zeros((modes_y, width), F32)
            for row in range(rows):
                at = first + (row * modes_x + mode) * 2
                total = total + twiddle_x[at] * values[row] + twiddle_x[at + 1] * backs[row]
            out[index, mode] = total

    for index in range(2):
        sums(core * 2 + index, keep, index)
        sums((1 - core) * 2 + index, send, index)


def prepare_body(where_ref, mode_ref, lift_ref, bias_ref, local_ref, spread_ref, place_ref, owner_ref, turn_ref, left, offset):
    block = where_ref[0]
    modes = spread_ref.shape[0]
    total = left.shape[1]
    half = place_ref.shape[1]
    spread = owner_ref[...]
    channels = lift_ref.shape[1]

    def dot(a, b, dims=((1,), (0,))):
        return lax.dot_general(a, b, (dims, ((), ())), precision=HIGHEST, preferred_element_type=F32)

    lifted = dot(dot(spread_ref[:, :channels], lift_ref[...], ((1,), (1,))), place_ref[...])
    same = spread_ref[:, channels : channels + half]
    lifted = lifted * same
    real = dot(dot(spread, mode_ref[0], ((1,), (1,))), lifted)
    imag = dot(dot(spread, mode_ref[1], ((1,), (1,))), lifted)
    cosine = turn_ref[block, 0]
    sine = turn_ref[block, 1]
    first = cosine * real - sine * imag
    second = -(cosine * imag + sine * real)
    left[...] = jnp.zeros_like(left)
    coupled = jnp.concatenate([first, second], axis=1).astype(BF16)
    width = 2 * half
    left[:, 0:width] = coupled
    left[:, width : 2 * width] = coupled
    constant = dot(spread, mode_ref[0, 0:channels, :], ((1,), (1,)))
    offset[...] = jnp.sum(constant * bias_ref[...], axis=1, keepdims=True)


def kernel_sizes(rows, channels, modes_x):
    padded_channels = -(-channels // 8) * 8
    height = rows * padded_channels
    coupled = FIELDS * modes_x * 2
    depth = -(-(2 * coupled + height) // 256) * 256
    return padded_channels, height, coupled, depth


def output_body(
    where_ref, mine, other, p_ref, q_ref, stiff, dense, lift_ref, left, offset, table_y, table_z,
    wave_ref, wave_other, features, wave_out, modes, right,
):
    step = pl.program_id(0)
    core = where_ref[0] % 2
    column = where_ref[1]
    modes_x, modes_y, width = mine.shape[1:]
    half = width // 2
    rows, group, depth = p_ref.shape
    brick_y = modes.shape[0]
    channels = features.shape[2]
    padded_channels = lift_ref.shape[0]
    height = rows * padded_channels
    coupled = FIELDS * modes_x

    @pl.when(step == 0)
    def _():
        chunk = 4
        left_y = table_y[column]
        for field in range(FIELDS):
            index = field % 2
            for start in range(0, modes_x, chunk):
                parts = [[], [], [], []]
                for mode in range(start, start + chunk):
                    own, far = mine[index, mode], other[index, mode]
                    value = jnp.where(core == field // 2, own, far)
                    high, low = high_low(value)
                    back_high, back_low = high_low(turned(value, half, -1.0))
                    for position, part in enumerate((high, back_high, low, back_low)):
                        parts[position].append(part)
                stacked = jnp.concatenate([jnp.concatenate(part, axis=1) for part in parts], axis=0)
                result = jnp.dot(left_y, stacked, preferred_element_type=F32)
                for mode in range(start, start + chunk):
                    lanes = slice((mode - start) * width, (mode - start + 1) * width)
                    modes[:, mode * FIELDS + field, :] = result[:, lanes]
        right[...] = jnp.zeros_like(right)
        z_half = depth // 2
        for row in range(rows):
            own = jnp.where(core == 0, wave_ref[row, :, :z_half], wave_ref[row, :, z_half:])
            wave_out[core * rows + row] = own
            wave_out[(1 - core) * rows + row] = wave_other[row]

    base = pl.multiple_of(step * group, group)
    high, low = high_low(modes[pl.ds(base, group)].reshape(group * coupled, width))
    waves = jnp.dot(high, table_z[...], preferred_element_type=F32)
    waves = waves + jnp.dot(low, table_z[...], preferred_element_type=F32)
    high, low = high_low(waves)
    weights = [lift_ref[:, index : index + 1] for index in range(FIELDS + 1)]
    for y in range(group):
        lines = slice(y * coupled, (y + 1) * coupled)
        position = 0
        for part in (high, low):
            for lanes in (slice(0, depth), slice(depth, 2 * depth)):
                right[y, position : position + coupled, :] = part[lines, lanes]
                position += coupled
        lifted = []
        for row in range(rows):
            total = jnp.broadcast_to(weights[FIELDS], (padded_channels, depth))
            for index, ref in enumerate((p_ref, q_ref, stiff, dense)):
                total = total + ref[row, y : y + 1, :] * weights[index]
            lifted.append(total)
        right[y, position : position + height, :] = jnp.concatenate(lifted, axis=0).astype(BF16)
        total = jnp.dot(left[...], right[y], preferred_element_type=F32) + offset[...]
        inner = math.sqrt(2.0 / math.pi) * (total + 0.044715 * (total * total * total))
        total = (0.5 * total) * (1.0 + jnp.tanh(inner))
        total = total.astype(BF16)
        for row in range(rows):
            at = row * padded_channels
            features[row, y] = total[at : at + channels]


def xor_pairs(count, distance):
    return [(index, index ^ distance) for index in range(count)]


def odd_pairs(count):
    pairs = [(index, index + 1) for index in range(1, count - 1, 2)]
    return pairs + [(target, source) for source, target in pairs]


def per_device(
    pressure,
    previous,
    material,
    stiffness,
    density,
    nonlinear,
    lift_weight,
    lift_bias,
    mode_weight,
    local_weight,
):
    brick_x, brick_y, brick_z = pressure.shape
    cycle_count = lax.axis_size("gx")
    column_count = lax.axis_size("gy")
    core_count = lax.axis_size("gz")
    total_x = brick_x * cycle_count
    total_y = brick_y * column_count
    total_z = brick_z * core_count
    modes_x = total_x // 4
    modes_y = total_y // 4
    modes_z = total_z // 4
    width = 2 * modes_z
    channels = lift_bias.shape[0]
    rows = brick_x // core_count
    assert core_count == 2 and rows >= REACH
    blocks = cycle_count * core_count
    padded_channels, height, coupled, right_depth = kernel_sizes(rows, channels, modes_x)
    two_sided = column_count > 2

    kept_first = kept_modes(total_x, modes_x)
    kept_second = kept_modes(total_y, modes_y)
    kept_third = np.arange(modes_z)
    cz, sz = cos_sin(np.arange(total_z), kept_third, total_z)
    forward_z = np.concatenate([cz, -sz], 1)
    weight = np.where(kept_third == 0, 1.0, 2.0) / (total_x * total_y * total_z)
    wc, ws = [rounded((t.astype(np.float32) * weight).T.astype(np.float32)) for t in (cz, sz)]
    inverse_z = np.concatenate(
        [np.concatenate([wc, ws], 1), np.concatenate([-ws.astype(np.float32), wc.astype(np.float32)], 1)], 0
    )
    inverse_z = rounded(inverse_z)
    cy, sy = cos_sin(kept_second, np.arange(total_y), total_y)
    cy3, sy3 = [t.reshape(modes_y, column_count, brick_y).transpose(1, 0, 2) for t in (cy, sy)]
    forward_y = np.concatenate([cy3, sy3, cy3, sy3], 2)
    cy3, sy3 = [t.transpose(0, 2, 1) for t in (cy3, sy3)]
    inverse_y = np.concatenate([cy3, sy3, cy3, sy3], 2)
    cx, sx = [t.astype(np.float32) for t in cos_sin(np.arange(total_x), kept_first, total_x)]
    twiddle_x = np.stack([cx, sx], -1).reshape(-1)
    owner = np.zeros((height, channels), np.float32)
    turn = np.zeros((blocks, 2, height, modes_x * FIELDS), np.float32)
    for row in range(rows):
        owner[row * padded_channels : row * padded_channels + channels] = np.eye(channels)
    for source, table in enumerate((cx, sx)):
        turn[:, source] = np.repeat(
            np.repeat(table.reshape(blocks, rows, modes_x), padded_channels, 1), FIELDS, 2
        )
    spread = np.tile(np.eye(channels, dtype=np.float32), (modes_x, 1))
    same = np.repeat(
        np.repeat(np.eye(modes_x, dtype=np.float32), channels, 0), FIELDS, 1
    )
    spread = np.concatenate([spread, same], 1)
    place = np.tile(np.eye(FIELDS, dtype=np.float32), (1, modes_x))

    core = lax.axis_index("gz")
    where = jnp.array([1, 0], jnp.int32) * (lax.axis_index("gx") * core_count + core) + jnp.array(
        [0, 1], jnp.int32
    ) * lax.axis_index("gy")

    def shape(*dims, dtype=F32):
        return jax.ShapeDtypeStruct(dims, dtype)

    cells = rows * brick_y * total_z
    field = shape(rows, brick_y, total_z)
    edge = [shape(rows, EDGE, total_z)] * (2 if two_sided else 1)
    half = shape(rows, brick_y, brick_z)

    send = call(pack_body, shape(3, rows, brick_y, brick_z), [SMEM] + [VMEM] * 3, moved=cells * 24)(
        where, pressure, previous, material
    )
    swap_core = xor_pairs(core_count, 1)
    got = lax.ppermute(send, "gz", swap_core)
    current, before, ratio, bend, stiff, dense, *edge_values = call(
        assemble_body, [field] * 6 + edge, [SMEM] * 4 + [VMEM] * 4, moved=cells * 36
    )(where, stiffness, density, nonlinear, pressure, previous, material, got)

    left, offset = call(
        prepare_body, [shape(height, right_depth, dtype=BF16), shape(height, 1)], [SMEM] + [VMEM] * 8
    )(
        where, mode_weight.reshape(2, modes_x * channels, channels), lift_weight,
        lift_bias.reshape(1, channels), local_weight, spread, place, owner, turn,
    )
    wide = jnp.zeros((rows, padded_channels, rows, padded_channels), BF16)
    small = jnp.pad(local_weight.T, ((0, padded_channels - channels),) * 2)
    wide = (np.eye(rows, dtype=ml_dtypes.bfloat16)[:, None, :, None] * small[None, :, None, :]).reshape(height, height)
    left = left.at[:, 2 * coupled : 2 * coupled + height].set(wide)
    lift_table = jnp.pad(
        jnp.concatenate([lift_weight, lift_bias[None]], 0).T, ((0, padded_channels - channels), (0, 0))
    )

    for repeat in range(STEPS):
        last = repeat == STEPS - 1
        far = lax.ppermute(current, ("gx", "gz"), odd_pairs(blocks))
        mate = lax.ppermute(current, "gz", swap_core)
        halos = [lax.ppermute(edge_values[0], "gy", xor_pairs(column_count, 1))]
        if two_sided:
            halos.append(lax.ppermute(edge_values[1], "gy", odd_pairs(column_count)))
        outs = [field] + ([half] if last else edge)
        body = lambda *refs, last=last: step_body(two_sided, last, *refs)
        new, *edge_values = call(
            body, outs, [SMEM] + [VMEM] * (6 + len(halos)),
            [pltpu.VMEM((brick_y + 2 * EDGE, total_z), F32)], flops=cells * 60, moved=cells * 28,
        )(where, current, before, ratio, bend, mate, far, *halos)
        current, before = new, current

    wave_other = lax.ppermute(edge_values[0], "gz", swap_core)
    part = shape(2, modes_x, modes_y, width)
    keep, send = call(
        spectrum_body, [part, part], [SMEM] * 2 + [VMEM] * 6,
        [pltpu.VMEM((4 * brick_y, FIELDS * rows * width), BF16), pltpu.VMEM((modes_y, FIELDS * rows * width), F32)],
        flops=cells * 2048, moved=cells * 32,
    )(where, twiddle_x, current, before, stiff, dense, forward_z, forward_y)
    total = keep + lax.ppermute(send, "gz", swap_core)
    for axis, count in (("gy", column_count), ("gx", cycle_count)):
        distance = 1
        while distance < count:
            total = total + lax.ppermute(total, axis, xor_pairs(count, distance))
            distance *= 2
    other = lax.ppermute(total, "gz", swap_core)

    group = 8
    whole = lambda array: pl.BlockSpec(array.shape, lambda i: (0,) * len(array.shape))
    slab = pl.BlockSpec((rows, group, total_z), lambda i: (0, i, 0))
    features, wave = pl.pallas_call(
        output_body,
        grid=(brick_y // group,),
        out_shape=[shape(rows, brick_y, channels, total_z, dtype=BF16), shape(*pressure.shape)],
        in_specs=[SMEM, whole(part), whole(part), slab, slab, slab, slab, whole(lift_table), whole(left),
                  whole(offset), whole(inverse_y), whole(inverse_z), whole(field), whole(half)],
        out_specs=[pl.BlockSpec((rows, group, channels, total_z), lambda i: (0, i, 0, 0)), whole(pressure)],
        scratch_shapes=[
            pltpu.VMEM((brick_y, FIELDS * modes_x, width), F32),
            pltpu.VMEM((group, right_depth, total_z), BF16),
        ],
        compiler_params=pltpu.CompilerParams(vmem_limit_bytes=56 * 1024 * 1024),
        cost_estimate=pl.CostEstimate(flops=cells * 2000, bytes_accessed=cells * 60, transcendentals=cells * 20),
    )(where, total, other, current, before, stiff, dense, lift_table, left, offset, inverse_y, inverse_z, current, wave_other)
    return (wave, features)


def solution(mesh):
    placed = (
        P(("grp", "gx"), "gy", "gz"),
        P(("grp", "gx"), "gy", "gz"),
        P(("grp", "gx"), "gy", "gz"),
        P(),
        P(),
        P(),
        P(),
        P(),
        P(),
        P(),
    )
    return jax.shard_map(
        per_device,
        mesh=mesh,
        in_specs=placed,
        out_specs=(P(("grp", "gx"), "gy", "gz"), P(("grp", "gx", "gz"), "gy", None, None)),
        check_vma=False,
    )
```

```python
import math

import numpy as np
import jax
import jax.numpy as jnp
from jax import lax
from jax.experimental import pallas as pl
from jax.experimental.pallas import tpu as pltpu
from jax.sharding import PartitionSpec as P
import ml_dtypes

STEPS = 4
FIELDS = 4
REACH = 4
EDGE = 8
stencil_taps = (-205.0 / 72.0, 8.0 / 5.0, -1.0 / 5.0, 8.0 / 315.0, -1.0 / 560.0)
F32 = jnp.float32
BF16 = jnp.bfloat16
HIGHEST = lax.Precision.HIGHEST

VMEM = pl.BlockSpec(memory_space=pltpu.VMEM)
SMEM = pl.BlockSpec(memory_space=pltpu.SMEM)


def rounded(table):
    return table.astype(ml_dtypes.bfloat16)


def kept_modes(length, mode_count):
    position = np.arange(mode_count)
    return np.where(position < mode_count // 2, position, length - mode_count + position)


def cos_sin(source, target, length):
    product = (source[:, None] * target[None, :]) % length
    phases = np.float32(2.0 * math.pi / length) * product.astype(np.float32)
    return rounded(np.cos(phases)), rounded(np.sin(phases))


def call(body, outs, in_specs, scratch=(), flops=0, moved=0):
    return pl.pallas_call(
        body,
        out_shape=outs,
        in_specs=in_specs,
        out_specs=jax.tree.map(lambda _: VMEM, outs),
        scratch_shapes=list(scratch),
        compiler_params=pltpu.CompilerParams(vmem_limit_bytes=16 * 1024 * 1024),
        cost_estimate=pl.CostEstimate(flops=flops, bytes_accessed=moved, transcendentals=0),
    )


def high_low(value):
    high = value.astype(BF16)
    return high, (value - high.astype(F32)).astype(BF16)


def turned(value, half, sign):
    lane = lax.broadcasted_iota(jnp.int32, value.shape, value.ndim - 1)
    swapped = pltpu.roll(value, half, value.ndim - 1)
    return jnp.where(lane < half, sign * swapped, -sign * swapped)


def looked_up(material, table, entries):
    result = jnp.full(material.shape, table(0), F32)
    for entry in range(1, entries):
        result = jnp.where(material == entry, table(entry), result)
    return result


def edges(value_of, outs, row_parity, brick_y):
    for position, out in enumerate(outs):
        upper = row_parity == position
        out[...] = jnp.where(upper, value_of(brick_y - EDGE, brick_y), value_of(0, EDGE))


def assemble_body(where_ref, stiffness, density, nonlinear, pressure, previous, material, got_p, got_q, got_m, *outs):
    p_out, q_out, ratio, bend, stiff, dense = outs[:6]
    core = where_ref[0] % 2
    column = where_ref[1]
    rows, brick_y = p_out.shape[:2]
    start = core * rows
    entries = stiffness.shape[0]

    def whole(own, other):
        return jnp.concatenate(
            [jnp.where(core == 0, own, other), jnp.where(core == 0, other, own)], axis=-1
        )

    for row in range(rows):
        p_out[row] = whole(pressure[start + row], got_p[start + row])
        q_out[row] = whole(previous[start + row], got_q[start + row])
        cell = whole(material[start + row], got_m[start + row])
        ratio[row] = looked_up(cell, lambda e: stiffness[e] / density[e], entries)
        bend[row] = looked_up(cell, lambda e: nonlinear[e], entries)
        stiff[row] = looked_up(cell, lambda e: stiffness[e], entries)
        dense[row] = looked_up(cell, lambda e: density[e], entries)
    edges(lambda a, b: p_out[:, a:b, :], outs[6:], column % 2, brick_y)


def step_body(two_sided, last, where_ref, p_ref, q_ref, ratio, bend, mate, far, *rest):
    count = 2 if two_sided else 1
    halos = rest[:count]
    new_ref = rest[count]
    edge_outs = rest[count + 1 : -1]
    padded = rest[-1]
    core = where_ref[0] % 2
    parity = where_ref[1] % 2
    rows, brick_y, depth = p_ref.shape
    lane = lax.broadcasted_iota(jnp.int32, (brick_y, depth), 1)
    zero_edge = jnp.zeros((EDGE, depth), F32)

    def line(index):
        if 0 <= index < rows:
            return p_ref[index]
        if index < 0:
            return jnp.where(core == 0, far[index + rows], mate[index + rows])
        return jnp.where(core == 0, mate[index - rows], far[index - rows])

    for row in range(rows):
        first = halos[0][row]
        second = halos[1][row] if two_sided else zero_edge
        center = p_ref[row]
        padded[0:EDGE, :] = jnp.where(parity == 0, second, first)
        padded[EDGE : EDGE + brick_y, :] = center
        padded[EDGE + brick_y :, :] = jnp.where(parity == 0, first, second)
        total = (3.0 * stencil_taps[0]) * center
        for offset in range(1, REACH + 1):
            low, high = EDGE - offset, EDGE + offset
            pair = padded[low : low + brick_y, :] + padded[high : high + brick_y, :]
            pair = pair + (line(row - offset) + line(row + offset))
            pair = pair + jnp.where(lane >= offset, pltpu.roll(center, offset, 1), 0.0)
            pair = pair + jnp.where(
                lane < depth - offset, pltpu.roll(center, depth - offset, 1), 0.0
            )
            total = total + stencil_taps[offset] * pair
        change = center - q_ref[row]
        new_ref[row] = (center + change) + ratio[row] * total + bend[row] * change * change
    if last:
        half = depth // 2
        edge_outs[0][...] = jnp.where(core == 0, new_ref[:, :, half:], new_ref[:, :, :half])
    else:
        edges(lambda a, b: new_ref[:, a:b, :], edge_outs, parity, brick_y)


def spectrum_body(where_ref, twiddle_x, p_ref, q_ref, stiff, dense, table_z, table_y, keep, send, lines, grid):
    core = where_ref[0] % 2
    column = where_ref[1]
    rows, brick_y, depth = p_ref.shape
    modes_x, modes_y, width = keep.shape[1:]
    half = width // 2
    for field, ref in enumerate((p_ref, q_ref, stiff, dense)):
        for row in range(rows):
            high, low = high_low(ref[row])
            modes = jnp.dot(high, table_z[...], preferred_element_type=F32)
            modes = modes + jnp.dot(low, table_z[...], preferred_element_type=F32)
            back = turned(modes, half, 1.0)
            high, low = high_low(modes)
            back_high, back_low = high_low(back)
            lanes = slice((field * rows + row) * width, (field * rows + row + 1) * width)
            for index, part in enumerate((high, back_high, low, back_low)):
                lines[index * brick_y : (index + 1) * brick_y, lanes] = part
    grid[...] = jnp.dot(table_y[column], lines[...], preferred_element_type=F32)
    first = (where_ref[0] * rows) * modes_x * 2

    def sums(base_field, out, index):
        values, backs = [], []
        for row in range(rows):
            lanes = pl.ds(pl.multiple_of((base_field * rows + row) * width, width), width)
            value = grid[:, lanes]
            values.append(value)
            backs.append(turned(value, half, 1.0))

        @pl.loop(0, modes_x)
        def _(mode):
            total = jnp.zeros((modes_y, width), F32)
            for row in range(rows):
                at = first + (row * modes_x + mode) * 2
                total = total + twiddle_x[at] * values[row] + twiddle_x[at + 1] * backs[row]
            out[index, mode] = total

    for index in range(2):
        sums(core * 2 + index, keep, index)
        sums((1 - core) * 2 + index, send, index)


def prepare_body(
    where_ref, mode_ref, lift_ref, bias_ref, local_ref, spread_ref, place_ref, owner_ref, turn_ref,
    wide_ref, mixing, pointwise, lift_table, offset,
):
    block = where_ref[0]
    half = place_ref.shape[1]
    channels = lift_ref.shape[1]
    spread = owner_ref[...]

    def dot(a, b, dims=((1,), (0,))):
        return lax.dot_general(a, b, (dims, ((), ())), precision=HIGHEST, preferred_element_type=F32)

    across = ((1,), (1,))
    lifted = dot(dot(spread_ref[:, :channels], lift_ref[...], across), place_ref[...])
    lifted = lifted * spread_ref[:, channels : channels + half]
    real = dot(dot(spread, mode_ref[0], across), lifted)
    imag = dot(dot(spread, mode_ref[1], across), lifted)
    cosine = turn_ref[block, 0]
    sine = turn_ref[block, 1]
    coupled = jnp.concatenate([cosine * real - sine * imag, -(cosine * imag + sine * real)], axis=1)
    coupled = coupled.astype(BF16)
    mixing[...] = jnp.concatenate([coupled, coupled], axis=1)
    constant = dot(spread, mode_ref[0, 0:channels, :], across)
    offset[...] = jnp.sum(constant * bias_ref[...], axis=1, keepdims=True)
    height = spread.shape[0]
    widest = wide_ref[0:channels, :]
    repeated = dot(dot(spread, local_ref[...].astype(F32), across), widest)
    pointwise[...] = (repeated * wide_ref[channels : channels + height, :]).astype(BF16)
    padded = wide_ref[channels + height :, 0:channels]
    lift_table[:, 0:FIELDS] = dot(padded, lift_ref[...], across)
    lift_table[:, FIELDS : FIELDS + 1] = dot(padded, bias_ref[...], across)


def pointwise_body(p_ref, q_ref, stiff, dense, lift_ref, left, offset, out, right):
    rows, group, depth = p_ref.shape
    padded_channels = lift_ref.shape[0]
    height = rows * padded_channels

    @pl.when(pl.program_id(0) == 0)
    def _():
        right[...] = jnp.zeros_like(right)

    weights = [lift_ref[:, index : index + 1] for index in range(FIELDS + 1)]
    for y in range(group):
        lifted = []
        for row in range(rows):
            total = jnp.broadcast_to(weights[FIELDS], (padded_channels, depth))
            for index, ref in enumerate((p_ref, q_ref, stiff, dense)):
                total = total + ref[row, y : y + 1, :] * weights[index]
            lifted.append(total)
        right[y, 0:height, :] = jnp.concatenate(lifted, axis=0).astype(BF16)
        out[:, y, :] = jnp.dot(left[...], right[y], preferred_element_type=F32) + offset[...]


def output_body(
    where_ref, mine, other, local, left, table_y, table_z, wave_ref, wave_other,
    features, wave_out, modes, right, sums,
):
    step = pl.program_id(0)
    core = where_ref[0] % 2
    column = where_ref[1]
    modes_x, modes_y, width = mine.shape[1:]
    half = width // 2
    rows, channels, group, depth = features.shape
    coupled = FIELDS * modes_x

    @pl.when(step == 0)
    def _():
        chunk = 4
        left_y = table_y[column]
        for field in range(FIELDS):
            index = field % 2
            for start in range(0, modes_x, chunk):
                parts = [[], [], [], []]
                for mode in range(start, start + chunk):
                    own, far = mine[index, mode], other[index, mode]
                    value = jnp.where(core == field // 2, own, far)
                    high, low = high_low(value)
                    back_high, back_low = high_low(turned(value, half, -1.0))
                    for position, part in enumerate((high, back_high, low, back_low)):
                        parts[position].append(part)
                stacked = jnp.concatenate([jnp.concatenate(part, axis=1) for part in parts], axis=0)
                result = jnp.dot(left_y, stacked, preferred_element_type=F32)
                for mode in range(start, start + chunk):
                    lanes = slice((mode - start) * width, (mode - start + 1) * width)
                    modes[:, mode * FIELDS + field, :] = result[:, lanes]
        z_half = depth // 2
        for row in range(rows):
            own = jnp.where(core == 0, wave_ref[row, :, :z_half], wave_ref[row, :, z_half:])
            wave_out[core * rows + row] = own
            wave_out[(1 - core) * rows + row] = wave_other[row]

    base = pl.multiple_of(step * group, group)
    high, low = high_low(modes[pl.ds(base, group)].reshape(group * coupled, width))
    waves = jnp.dot(high, table_z[...], preferred_element_type=F32)
    waves = waves + jnp.dot(low, table_z[...], preferred_element_type=F32)
    high, low = high_low(waves)
    for y in range(group):
        lines = slice(y * coupled, (y + 1) * coupled)
        position = 0
        for part in (high, low):
            for lanes in (slice(0, depth), slice(depth, 2 * depth)):
                right[y, position : position + coupled, :] = part[lines, lanes]
                position += coupled
        sums[:, y, :] = jnp.dot(left[...], right[y], preferred_element_type=F32)
    for row in range(rows):
        for channel in range(channels):
            at = row * channels + channel
            total = sums[at] + local[at]
            inner = math.sqrt(2.0 / math.pi) * (total + 0.044715 * (total * total * total))
            total = (0.5 * total) * (1.0 + jnp.tanh(inner))
            features[row, channel] = total.astype(BF16)


def xor_pairs(count, distance):
    return [(index, index ^ distance) for index in range(count)]


def odd_pairs(count):
    pairs = [(index, index + 1) for index in range(1, count - 1, 2)]
    return pairs + [(target, source) for source, target in pairs]


def per_device(
    pressure,
    previous,
    material,
    stiffness,
    density,
    nonlinear,
    lift_weight,
    lift_bias,
    mode_weight,
    local_weight,
):
    brick_x, brick_y, brick_z = pressure.shape
    cycle_count = lax.axis_size("gx")
    column_count = lax.axis_size("gy")
    core_count = lax.axis_size("gz")
    total_x = brick_x * cycle_count
    total_y = brick_y * column_count
    total_z = brick_z * core_count
    modes_x = total_x // 4
    modes_y = total_y // 4
    modes_z = total_z // 4
    width = 2 * modes_z
    channels = lift_bias.shape[0]
    rows = brick_x // core_count
    assert core_count == 2 and rows >= REACH
    blocks = cycle_count * core_count
    padded_channels = -(-channels // 8) * 8
    height = rows * channels
    coupled = FIELDS * modes_x
    right_depth = -(-rows * padded_channels // 128) * 128
    two_sided = column_count > 2

    kept_first = kept_modes(total_x, modes_x)
    kept_second = kept_modes(total_y, modes_y)
    kept_third = np.arange(modes_z)
    cz, sz = cos_sin(np.arange(total_z), kept_third, total_z)
    forward_z = np.concatenate([cz, -sz], 1)
    weight = np.where(kept_third == 0, 1.0, 2.0) / (total_x * total_y * total_z)
    wc, ws = [rounded((t.astype(np.float32) * weight).T.astype(np.float32)) for t in (cz, sz)]
    inverse_z = np.concatenate(
        [np.concatenate([wc, ws], 1), np.concatenate([-ws.astype(np.float32), wc.astype(np.float32)], 1)], 0
    )
    inverse_z = rounded(inverse_z)
    cy, sy = cos_sin(kept_second, np.arange(total_y), total_y)
    cy3, sy3 = [t.reshape(modes_y, column_count, brick_y).transpose(1, 0, 2) for t in (cy, sy)]
    forward_y = np.concatenate([cy3, sy3, cy3, sy3], 2)
    cy3, sy3 = [t.transpose(0, 2, 1) for t in (cy3, sy3)]
    inverse_y = np.concatenate([cy3, sy3, cy3, sy3], 2)
    cx, sx = [t.astype(np.float32) for t in cos_sin(np.arange(total_x), kept_first, total_x)]
    twiddle_x = np.stack([cx, sx], -1).reshape(-1)
    owner = np.tile(np.eye(channels, dtype=np.float32), (rows, 1))
    turn = np.zeros((blocks, 2, height, coupled), np.float32)
    for source, table in enumerate((cx, sx)):
        turn[:, source] = np.repeat(
            np.repeat(table.reshape(blocks, rows, modes_x), channels, 1), FIELDS, 2
        )
    padded_eye = np.eye(channels, padded_channels, dtype=np.float32)
    wide = np.zeros((channels + height + padded_channels, right_depth), np.float32)
    wide[:channels, : rows * padded_channels] = np.tile(padded_eye, (1, rows))
    wide[channels : channels + height, : rows * padded_channels] = np.kron(
        np.eye(rows), np.ones((channels, padded_channels))
    )
    wide[channels + height :, :channels] = padded_eye.T
    spread = np.tile(np.eye(channels, dtype=np.float32), (modes_x, 1))
    same = np.repeat(
        np.repeat(np.eye(modes_x, dtype=np.float32), channels, 0), FIELDS, 1
    )
    spread = np.concatenate([spread, same], 1)
    place = np.tile(np.eye(FIELDS, dtype=np.float32), (1, modes_x))

    core = lax.axis_index("gz")
    where = jnp.array([1, 0], jnp.int32) * (lax.axis_index("gx") * core_count + core) + jnp.array(
        [0, 1], jnp.int32
    ) * lax.axis_index("gy")

    def shape(*dims, dtype=F32):
        return jax.ShapeDtypeStruct(dims, dtype)

    cells = rows * brick_y * total_z
    field = shape(rows, brick_y, total_z)
    edge = [shape(rows, EDGE, total_z)] * (2 if two_sided else 1)
    half = shape(rows, brick_y, brick_z)

    swap_core = xor_pairs(core_count, 1)
    got = [lax.ppermute(array, "gz", swap_core) for array in (pressure, previous, material)]
    current, before, ratio, bend, stiff, dense, *edge_values = call(
        assemble_body, [field] * 6 + edge, [SMEM] * 4 + [VMEM] * 6, moved=cells * 36
    )(where, stiffness, density, nonlinear, pressure, previous, material, *got)

    mixing, pointwise, lift_table, offset = call(
        prepare_body,
        [shape(height, 4 * coupled, dtype=BF16), shape(height, right_depth, dtype=BF16),
         shape(padded_channels, FIELDS + 1), shape(height, 1)],
        [SMEM] + [VMEM] * 9, flops=2_000_000_000, moved=4_000_000,
    )(
        where, mode_weight.reshape(2, modes_x * channels, channels), lift_weight,
        lift_bias.reshape(1, channels), local_weight, spread, place, owner, turn, wide,
    )

    for repeat in range(STEPS):
        last = repeat == STEPS - 1
        far = lax.ppermute(current, ("gx", "gz"), odd_pairs(blocks))
        mate = lax.ppermute(current, "gz", swap_core)
        halos = [lax.ppermute(edge_values[0], "gy", xor_pairs(column_count, 1))]
        if two_sided:
            halos.append(lax.ppermute(edge_values[1], "gy", odd_pairs(column_count)))
        outs = [field] + ([half] if last else edge)
        body = lambda *refs, last=last: step_body(two_sided, last, *refs)
        new, *edge_values = call(
            body, outs, [SMEM] + [VMEM] * (6 + len(halos)),
            [pltpu.VMEM((brick_y + 2 * EDGE, total_z), F32)], flops=cells * 60, moved=cells * 28,
        )(where, current, before, ratio, bend, mate, far, *halos)
        current, before = new, current

    wave_other = lax.ppermute(edge_values[0], "gz", swap_core)
    part = shape(2, modes_x, modes_y, width)
    keep, send = call(
        spectrum_body, [part, part], [SMEM] * 2 + [VMEM] * 6,
        [pltpu.VMEM((4 * brick_y, FIELDS * rows * width), BF16), pltpu.VMEM((modes_y, FIELDS * rows * width), F32)],
        flops=cells * 2048, moved=cells * 32,
    )(where, twiddle_x, current, before, stiff, dense, forward_z, forward_y)
    total = keep + lax.ppermute(send, "gz", swap_core)
    group = 8
    whole = lambda array: pl.BlockSpec(array.shape, lambda i: (0,) * len(array.shape))
    slab = pl.BlockSpec((rows, group, total_z), lambda i: (0, i, 0))
    strip = pl.BlockSpec((height, group, total_z), lambda i: (0, i, 0))
    stages = [(axis, count, 2**bit) for axis, count in (("gy", column_count), ("gx", cycle_count))
              for bit in range((count - 1).bit_length())]
    for index, (axis, count, distance) in enumerate(stages):
        arrived = lax.ppermute(total, axis, xor_pairs(count, distance))
        if index == 0:
            arrived, mixing, pointwise, lift_table, offset = lax.optimization_barrier(
                (arrived, mixing, pointwise, lift_table, offset)
            )
        if index == len(stages) - 1:
            local = pl.pallas_call(
                pointwise_body,
                grid=(brick_y // group,),
                out_shape=shape(height, brick_y, total_z),
                in_specs=[slab] * 4 + [whole(lift_table), whole(pointwise), whole(offset)],
                out_specs=strip,
                scratch_shapes=[pltpu.VMEM((group, right_depth, total_z), BF16)],
                compiler_params=pltpu.CompilerParams(vmem_limit_bytes=24 * 1024 * 1024),
                cost_estimate=pl.CostEstimate(flops=cells * 40000, bytes_accessed=cells * 100, transcendentals=0),
            )(current, before, stiff, dense, lift_table, pointwise, offset)
            arrived, local = lax.optimization_barrier((arrived, local))
        total = total + arrived
    other = lax.ppermute(total, "gz", swap_core)

    scoped = 12 * 2**20 + 4 * (6 * 2 * modes_x * modes_y * width + brick_y * coupled * width + 6 * group * coupled * total_z)
    features, wave = pl.pallas_call(
        output_body,
        grid=(brick_y // group,),
        out_shape=[shape(rows, channels, brick_y, total_z, dtype=BF16), shape(*pressure.shape)],
        in_specs=[SMEM, whole(part), whole(part), strip, whole(mixing), whole(inverse_y), whole(inverse_z),
                  whole(field), whole(half)],
        out_specs=[pl.BlockSpec((rows, channels, group, total_z), lambda i: (0, 0, i, 0)), whole(pressure)],
        scratch_shapes=[
            pltpu.VMEM((brick_y, coupled, width), F32),
            pltpu.VMEM((group, 4 * coupled, total_z), BF16),
            pltpu.VMEM((height, group, total_z), F32),
        ],
        compiler_params=pltpu.CompilerParams(vmem_limit_bytes=scoped),
        cost_estimate=pl.CostEstimate(flops=cells * 2000, bytes_accessed=cells * 60, transcendentals=cells * 20),
    )(where, total, other, local, mixing, inverse_y, inverse_z, current, wave_other)
    features = features.transpose(0, 2, 1, 3)
    return (wave, features)


def solution(mesh):
    placed = (
        P(("grp", "gx"), "gy", "gz"),
        P(("grp", "gx"), "gy", "gz"),
        P(("grp", "gx"), "gy", "gz"),
        P(),
        P(),
        P(),
        P(),
        P(),
        P(),
        P(),
    )
    return jax.shard_map(
        per_device,
        mesh=mesh,
        in_specs=placed,
        out_specs=(P(("grp", "gx"), "gy", "gz"), P(("grp", "gx", "gz"), "gy", None, None)),
        check_vma=False,
    )
```

```python
import math

import numpy as np
import jax
import jax.numpy as jnp
from jax import lax
from jax.experimental import pallas as pl
from jax.experimental.pallas import tpu as pltpu
from jax.sharding import PartitionSpec as P
import ml_dtypes

STEPS = 4
FIELDS = 4
REACH = 4
EDGE = 8
stencil_taps = (-205.0 / 72.0, 8.0 / 5.0, -1.0 / 5.0, 8.0 / 315.0, -1.0 / 560.0)
F32 = jnp.float32
BF16 = jnp.bfloat16
HIGHEST = lax.Precision.HIGHEST

VMEM = pl.BlockSpec(memory_space=pltpu.VMEM)
SMEM = pl.BlockSpec(memory_space=pltpu.SMEM)
HBM = pl.BlockSpec(memory_space=pltpu.HBM)


def rounded(table):
    return table.astype(ml_dtypes.bfloat16)


def kept_modes(length, mode_count):
    position = np.arange(mode_count)
    return np.where(position < mode_count // 2, position, length - mode_count + position)


def cos_sin(source, target, length):
    product = (source[:, None] * target[None, :]) % length
    phases = np.float32(2.0 * math.pi / length) * product.astype(np.float32)
    return rounded(np.cos(phases)), rounded(np.sin(phases))


def call(body, outs, in_specs, scratch=(), flops=0, moved=0):
    return pl.pallas_call(
        body,
        out_shape=outs,
        in_specs=in_specs,
        out_specs=jax.tree.map(lambda _: VMEM, outs),
        scratch_shapes=list(scratch),
        compiler_params=pltpu.CompilerParams(vmem_limit_bytes=16 * 1024 * 1024),
        cost_estimate=pl.CostEstimate(flops=flops, bytes_accessed=moved, transcendentals=0),
    )


def high_low(value):
    high = value.astype(BF16)
    return high, (value - high.astype(F32)).astype(BF16)


def turned(value, half, sign):
    lane = lax.broadcasted_iota(jnp.int32, value.shape, value.ndim - 1)
    swapped = pltpu.roll(value, half, value.ndim - 1)
    return jnp.where(lane < half, sign * swapped, -sign * swapped)


def looked_up(material, table, entries):
    result = jnp.full(material.shape, table(0), F32)
    for entry in range(1, entries):
        result = jnp.where(material == entry, table(entry), result)
    return result


def middle(table):
    total = table[0]
    for entry in range(1, table.shape[0]):
        total = total + table[entry]
    return total * (1.0 / table.shape[0])


def edges(value_of, outs, row_parity, brick_y):
    for position, out in enumerate(outs):
        upper = row_parity == position
        out[...] = jnp.where(upper, value_of(brick_y - EDGE, brick_y), value_of(0, EDGE))


def assemble_body(count, *refs):
    tables_in, own_in, got = refs[:3], refs[3:6], refs[6:9]
    p_out, q_out, ratio, bend, stiff, dense, sent = refs[9:16]
    edge_outs = refs[16 : 16 + count]
    tables, own, semaphores = refs[16 + count : 19 + count], refs[19 + count : 22 + count], refs[22 + count]
    core, column = lax.axis_index("gz"), lax.axis_index("gy")
    rows, brick_y = p_out.shape[:2]
    start = core * rows
    copies = [
        pltpu.make_async_copy(source, target, semaphores.at[index])
        for index, (source, target) in enumerate(zip(tables_in, tables))
    ] + [
        pltpu.make_async_copy(source.at[pl.ds(start, rows)], target, semaphores.at[3 + index])
        for index, (source, target) in enumerate(zip(own_in, own))
    ]
    for copy in copies:
        copy.start()
    for copy in copies:
        copy.wait()
    stiffness, density, nonlinear = tables
    entries = stiffness.shape[0]

    def whole(mine, other):
        return jnp.concatenate(
            [jnp.where(core == 0, mine, other), jnp.where(core == 0, other, mine)], axis=-1
        )

    stiff_middle, dense_middle = middle(stiffness), middle(density)
    for row in range(rows):
        value = whole(own[0][row], got[0][start + row])
        p_out[row] = value
        sent[row] = value.astype(BF16)
        q_out[row] = whole(own[1][row], got[1][start + row])
        cell = whole(own[2][row], got[2][start + row])
        ratio[row] = looked_up(cell, lambda e: stiffness[e] / density[e], entries)
        bend[row] = looked_up(cell, lambda e: nonlinear[e], entries)
        stiff[row] = looked_up(cell, lambda e: stiffness[e] - stiff_middle, entries)
        dense[row] = looked_up(cell, lambda e: density[e] - dense_middle, entries)
    edges(lambda a, b: p_out[:, a:b, :], edge_outs, column % 2, brick_y)


def step_body(two_sided, last, p_ref, q_ref, ratio, bend, mate, far, *rest):
    count = 2 if two_sided else 1
    halos = rest[:count]
    new_ref, sent = rest[count : count + 2]
    edge_outs = rest[count + 2 : -1]
    padded = rest[-1]
    core = lax.axis_index("gz")
    parity = lax.axis_index("gy") % 2
    rows, brick_y, depth = p_ref.shape
    lane = lax.broadcasted_iota(jnp.int32, (brick_y, depth), 1)
    zero_edge = jnp.zeros((EDGE, depth), F32)

    def line(index):
        if 0 <= index < rows:
            return p_ref[index]
        if index < 0:
            return jnp.where(core == 0, far[index + rows], mate[index + rows]).astype(F32)
        return jnp.where(core == 0, mate[index - rows], far[index - rows]).astype(F32)

    for row in range(rows):
        first = halos[0][row]
        second = halos[1][row] if two_sided else zero_edge
        center = p_ref[row]
        padded[0:EDGE, :] = jnp.where(parity == 0, second, first)
        padded[EDGE : EDGE + brick_y, :] = center
        padded[EDGE + brick_y :, :] = jnp.where(parity == 0, first, second)
        total = (3.0 * stencil_taps[0]) * center
        for offset in range(1, REACH + 1):
            low, high = EDGE - offset, EDGE + offset
            pair = padded[low : low + brick_y, :] + padded[high : high + brick_y, :]
            pair = pair + (line(row - offset) + line(row + offset))
            pair = pair + jnp.where(lane >= offset, pltpu.roll(center, offset, 1), 0.0)
            pair = pair + jnp.where(
                lane < depth - offset, pltpu.roll(center, depth - offset, 1), 0.0
            )
            total = total + stencil_taps[offset] * pair
        change = center - q_ref[row]
        value = (center + change) + ratio[row] * total + bend[row] * change * change
        new_ref[row] = value
        if not last:
            sent[row] = value.astype(BF16)
    if last:
        half = depth // 2
        sent[...] = jnp.where(core == 0, new_ref[:, :, half:], new_ref[:, :, :half])
    else:
        edges(lambda a, b: new_ref[:, a:b, :], edge_outs, parity, brick_y)


def spectrum_body(twiddle_x, *refs):
    count = (len(refs) - 6) or 1
    sources = refs[:count]
    table_z, table_y, keep, send, lines, grid = refs[count:]
    core, column = lax.axis_index("gz"), lax.axis_index("gy")
    rows, brick_y, depth = sources[0].shape
    modes_x, modes_y, width = keep.shape[1:]
    half = width // 2
    for field, ref in enumerate(sources):
        for row in range(rows):
            high, low = high_low(ref[row])
            modes = jnp.dot(high, table_z[...], preferred_element_type=F32)
            modes = modes + jnp.dot(low, table_z[...], preferred_element_type=F32)
            back = turned(modes, half, 1.0)
            high, low = high_low(modes)
            back_high, back_low = high_low(back)
            lanes = slice((field * rows + row) * width, (field * rows + row + 1) * width)
            for index, part in enumerate((high, back_high, low, back_low)):
                lines[index * brick_y : (index + 1) * brick_y, lanes] = part
    grid[...] = jnp.dot(table_y[column], lines[...], preferred_element_type=F32)
    block = lax.axis_index("gx") * 2 + core
    first = block * (rows * modes_x * 4)

    for field in range(count):
        values, backs = [], []
        for row in range(rows):
            lanes = slice((field * rows + row) * width, (field * rows + row + 1) * width)
            values.append(grid[:, lanes])
            backs.append(turned(values[-1], half, 1.0))

        def summed(mode):
            total = jnp.zeros((modes_y, width), F32)
            for row in range(rows):
                at = first + (row * modes_x * 2 + mode) * 2
                total = total + twiddle_x[at] * values[row] + twiddle_x[at + 1] * backs[row]
            return total

        @pl.loop(0, modes_x)
        def _(mode):
            keep[field, mode] = summed(core * modes_x + mode)
            send[field, mode] = summed((1 - core) * modes_x + mode).astype(BF16)


def prepare_body(
    stiffness, density, mode_ref, lift_ref, bias_ref, local_ref, spread_ref, place_ref, owner_ref, turn_ref,
    wide_ref, mixing, pointwise, lift_table, offset,
):
    block = lax.axis_index("gx") * 2 + lax.axis_index("gz")
    half = place_ref.shape[1]
    channels = lift_ref.shape[1]
    spread = owner_ref[...]

    def dot(a, b, dims=((1,), (0,))):
        return lax.dot_general(a, b, (dims, ((), ())), precision=HIGHEST, preferred_element_type=F32)

    across = ((1,), (1,))
    lifted = dot(dot(spread_ref[:, :channels], lift_ref[...], across), place_ref[...])
    lifted = lifted * spread_ref[:, channels : channels + half]
    real = dot(dot(spread, mode_ref[0], across), lifted)
    imag = dot(dot(spread, mode_ref[1], across), lifted)
    cosine = turn_ref[block, 0]
    sine = turn_ref[block, 1]
    coupled = jnp.concatenate([cosine * real - sine * imag, -(cosine * imag + sine * real)], axis=1)
    mixing[...] = coupled.astype(BF16)
    constant = dot(spread, mode_ref[0, 0:channels, :], across)
    bias = bias_ref[...] + middle(stiffness) * lift_ref[2:3, :] + middle(density) * lift_ref[3:4, :]
    offset[...] = jnp.sum(constant * bias, axis=1, keepdims=True)
    height = spread.shape[0]
    widest = wide_ref[0:channels, :]
    repeated = dot(dot(spread, local_ref[...].astype(F32), across), widest)
    pointwise[...] = (repeated * wide_ref[channels : channels + height, :]).astype(BF16)
    padded = wide_ref[channels + height :, 0:channels]
    lift_table[:, 0:FIELDS] = dot(padded, lift_ref[...], across)
    lift_table[:, FIELDS : FIELDS + 1] = dot(padded, bias_ref[...], across)
    lift_table[:, FIELDS + 1 :] = jnp.zeros_like(lift_table[:, FIELDS + 1 :])


def pointwise_body(stiffness, density, p_ref, q_ref, stiff, dense, lift_ref, left, offset, out, right):
    rows, group, depth = p_ref.shape
    padded_channels = lift_ref.shape[0]
    height = rows * padded_channels

    @pl.when(pl.program_id(0) == 0)
    def _():
        right[...] = jnp.zeros_like(right)

    weights = [lift_ref[:, index : index + 1] for index in range(FIELDS + 1)]
    stiff_middle, dense_middle = middle(stiffness), middle(density)
    for y in range(group):
        lifted = []
        for row in range(rows):
            total = jnp.broadcast_to(weights[FIELDS], (padded_channels, depth))
            line = slice(y, y + 1)
            values = (p_ref[row, line], q_ref[row, line], stiff[row, line] + stiff_middle, dense[row, line] + dense_middle)
            for value, weight in zip(values, weights):
                total = total + value * weight
            lifted.append(total)
        right[y, 0:height, :] = jnp.concatenate(lifted, axis=0).astype(BF16)
        out[:, y, :] = jnp.dot(left[...], right[y], preferred_element_type=F32) + offset[...]


def output_body(
    mine, other, mine_early, other_early, local, left, table_y, table_z, wave_ref, wave_other,
    features, wave_out, modes, right, sums,
):
    step = pl.program_id(0)
    core, column = lax.axis_index("gz"), lax.axis_index("gy")
    half_x, modes_y, width = mine.shape[1:]
    modes_x = 2 * half_x
    half = width // 2
    rows, channels, group, depth = features.shape
    coupled = FIELDS * modes_x

    @pl.when(step == 0)
    def _():
        chunk = 4
        left_y = table_y[column]
        for field in range(FIELDS):
            own, far = ((mine, other), (mine_early, other_early))[field // 2]
            for start in range(0, modes_x, chunk):
                parts = [[], []]
                for mode in range(start, start + chunk):
                    at = (field % 2, mode % half_x)
                    value = jnp.where(core == mode // half_x, own[at], far[at].astype(F32))
                    parts[0].append(value.astype(BF16))
                    parts[1].append(turned(value, half, -1.0).astype(BF16))
                stacked = jnp.concatenate([jnp.concatenate(part, axis=1) for part in parts], axis=0)
                result = jnp.dot(left_y, stacked, preferred_element_type=F32)
                for mode in range(start, start + chunk):
                    lanes = slice((mode - start) * width, (mode - start + 1) * width)
                    modes[:, mode * FIELDS + field, :] = result[:, lanes]
        z_half = depth // 2
        for row in range(rows):
            own = jnp.where(core == 0, wave_ref[row, :, :z_half], wave_ref[row, :, z_half:])
            wave_out[core * rows + row] = own
            wave_out[(1 - core) * rows + row] = wave_other[row]

    base = pl.multiple_of(step * group, group)
    lines = modes[pl.ds(base, group)].reshape(group * coupled, width).astype(BF16)
    waves = jnp.dot(lines, table_z[...], preferred_element_type=F32).astype(BF16)
    for y in range(group):
        lines = slice(y * coupled, (y + 1) * coupled)
        right[y, 0:coupled, :] = waves[lines, :depth]
        right[y, coupled:, :] = waves[lines, depth:]
        sums[:, y, :] = jnp.dot(left[...], right[y], preferred_element_type=F32)
    for row in range(rows):
        for channel in range(channels):
            at = row * channels + channel
            total = sums[at] + local[at]
            inner = math.sqrt(2.0 / math.pi) * (total + 0.044715 * (total * total * total))
            total = (0.5 * total) * (1.0 + jnp.tanh(inner))
            features[row, channel] = total.astype(BF16)


def xor_pairs(count, distance):
    return [(index, index ^ distance) for index in range(count)]


def odd_pairs(count):
    pairs = [(index, index + 1) for index in range(1, count - 1, 2)]
    return pairs + [(target, source) for source, target in pairs]


def per_device(
    pressure,
    previous,
    material,
    stiffness,
    density,
    nonlinear,
    lift_weight,
    lift_bias,
    mode_weight,
    local_weight,
):
    brick_x, brick_y, brick_z = pressure.shape
    cycle_count = lax.axis_size("gx")
    column_count = lax.axis_size("gy")
    core_count = lax.axis_size("gz")
    total_x = brick_x * cycle_count
    total_y = brick_y * column_count
    total_z = brick_z * core_count
    modes_x = total_x // 4
    modes_y = total_y // 4
    modes_z = total_z // 4
    width = 2 * modes_z
    channels = lift_bias.shape[0]
    rows = brick_x // core_count
    assert core_count == 2 and rows >= REACH
    blocks = cycle_count * core_count
    padded_channels = -(-channels // 8) * 8
    height = rows * channels
    coupled = FIELDS * modes_x
    right_depth = -(-rows * padded_channels // 128) * 128
    two_sided = column_count > 2

    kept_first = kept_modes(total_x, modes_x)
    kept_second = kept_modes(total_y, modes_y)
    kept_third = np.arange(modes_z)
    cz, sz = cos_sin(np.arange(total_z), kept_third, total_z)
    forward_z = np.concatenate([cz, -sz], 1)
    weight = np.where(kept_third == 0, 1.0, 2.0) / (total_x * total_y * total_z)
    wc, ws = [rounded((t.astype(np.float32) * weight).T.astype(np.float32)) for t in (cz, sz)]
    inverse_z = np.concatenate(
        [np.concatenate([wc, ws], 1), np.concatenate([-ws.astype(np.float32), wc.astype(np.float32)], 1)], 0
    )
    inverse_z = rounded(inverse_z)
    cy, sy = cos_sin(kept_second, np.arange(total_y), total_y)
    cy3, sy3 = [t.reshape(modes_y, column_count, brick_y).transpose(1, 0, 2) for t in (cy, sy)]
    forward_y = np.concatenate([cy3, sy3, cy3, sy3], 2)
    cy3, sy3 = [t.transpose(0, 2, 1) for t in (cy3, sy3)]
    inverse_y = np.concatenate([cy3, sy3], 2)
    cx, sx = [t.astype(np.float32) for t in cos_sin(np.arange(total_x), kept_first, total_x)]
    twiddle_x = np.stack([cx, sx], -1).reshape(-1)
    owner = np.tile(np.eye(channels, dtype=np.float32), (rows, 1))
    turn = np.zeros((blocks, 2, height, coupled), np.float32)
    for source, table in enumerate((cx, sx)):
        turn[:, source] = np.repeat(
            np.repeat(table.reshape(blocks, rows, modes_x), channels, 1), FIELDS, 2
        )
    padded_eye = np.eye(channels, padded_channels, dtype=np.float32)
    wide = np.zeros((channels + height + padded_channels, right_depth), np.float32)
    wide[:channels, : rows * padded_channels] = np.tile(padded_eye, (1, rows))
    wide[channels : channels + height, : rows * padded_channels] = np.kron(
        np.eye(rows), np.ones((channels, padded_channels))
    )
    wide[channels + height :, :channels] = padded_eye.T
    spread = np.tile(np.eye(channels, dtype=np.float32), (modes_x, 1))
    same = np.repeat(
        np.repeat(np.eye(modes_x, dtype=np.float32), channels, 0), FIELDS, 1
    )
    spread = np.concatenate([spread, same], 1)
    place = np.tile(np.eye(FIELDS, dtype=np.float32), (1, modes_x))

    def shape(*dims, dtype=F32):
        return jax.ShapeDtypeStruct(dims, dtype)

    cells = rows * brick_y * total_z
    field = shape(rows, brick_y, total_z)
    edge = [shape(rows, EDGE, total_z)] * (2 if two_sided else 1)
    half = shape(rows, brick_y, brick_z)

    swap_core = xor_pairs(core_count, 1)
    got = [lax.ppermute(array, "gz", swap_core) for array in (pressure, previous, material)]
    sending = shape(rows, brick_y, total_z, dtype=BF16)
    current, before, ratio, bend, stiff, dense, sent, *edge_values = call(
        lambda *refs: assemble_body(len(edge), *refs), [field] * 6 + [sending] + edge, [HBM] * 6 + [VMEM] * 3,
        [pltpu.SMEM(stiffness.shape, F32)] * 3 + [pltpu.VMEM((rows, brick_y, brick_z), F32)] * 2
        + [pltpu.VMEM((rows, brick_y, brick_z), jnp.int32), pltpu.SemaphoreType.DMA((6,))], moved=cells * 36
    )(stiffness, density, nonlinear, pressure, previous, material, *got)

    mixing, pointwise, lift_table, offset = call(
        prepare_body,
        [shape(height, 2 * coupled, dtype=BF16), shape(height, right_depth, dtype=BF16),
         shape(padded_channels, 8), shape(height, 1)],
        [SMEM] * 2 + [VMEM] * 9, flops=2_000_000_000, moved=4_000_000,
    )(
        stiffness, density, mode_weight.reshape(2, modes_x * channels, channels), lift_weight,
        lift_bias.reshape(1, channels), local_weight, spread, place, owner, turn, wide,
    )

    part = [shape(2, modes_x // 2, modes_y, width, dtype=dtype) for dtype in (F32, BF16)]
    spectrum = call(
        spectrum_body, part, [SMEM] + [VMEM] * 4,
        [pltpu.VMEM((4 * brick_y, 2 * rows * width), BF16), pltpu.VMEM((modes_y, 2 * rows * width), F32)],
        flops=cells * 1024, moved=cells * 16,
    )
    stages = [(axis, count, 2**bit) for axis, count in (("gy", column_count), ("gx", cycle_count))
              for bit in range((count - 1).bit_length())]
    swap = lambda value: lax.ppermute(value, "gz", swap_core)

    early, early_sent = spectrum(twiddle_x, stiff, dense, forward_z, forward_y)
    moves = [lambda value: swap(early_sent)] + [
        lambda value, stage=stage: lax.ppermute(value.astype(BF16), stage[0], xor_pairs(*stage[1:])) for stage in stages
    ]
    pending = None

    for repeat in range(STEPS):
        last = repeat == STEPS - 1
        far = lax.ppermute(sent, ("gx", "gz"), odd_pairs(blocks))
        mate = swap(sent)
        halos = [lax.ppermute(edge_values[0], "gy", xor_pairs(column_count, 1))]
        if two_sided:
            halos.append(lax.ppermute(edge_values[1], "gy", odd_pairs(column_count)))
        if pending is not None:
            early = early + pending.astype(F32)
            pending = None
        if moves:
            halos[0], early, early_sent = lax.optimization_barrier((halos[0], early, early_sent))
            pending = moves.pop(0)(early)
        outs = [field] + ([half] if last else [sending] + edge)
        body = lambda *refs, last=last: step_body(two_sided, last, *refs)
        new, sent, *edge_values = call(
            body, outs, [VMEM] * (6 + len(halos)),
            [pltpu.VMEM((brick_y + 2 * EDGE, total_z), F32)], flops=cells * 60, moved=cells * 28,
        )(current, before, ratio, bend, mate, far, *halos)
        current, before = new, current

    wave_other = swap(sent)
    total, sent = spectrum(twiddle_x, current, before, forward_z, forward_y)
    total = total + swap(sent).astype(F32)
    while moves:
        early = early + pending.astype(F32)
        pending = moves.pop(0)(early)
    early = early + pending.astype(F32)
    early_other = swap(early.astype(BF16))
    group = 8
    whole = lambda array: pl.BlockSpec(array.shape, lambda i: (0,) * len(array.shape))
    slab = pl.BlockSpec((rows, group, total_z), lambda i: (0, i, 0))
    strip = pl.BlockSpec((height, group, total_z), lambda i: (0, i, 0))
    for index, (axis, count, distance) in enumerate(stages):
        arrived = lax.ppermute(total.astype(BF16), axis, xor_pairs(count, distance))
        if index == 0:
            arrived, mixing, pointwise, lift_table, offset = lax.optimization_barrier(
                (arrived, mixing, pointwise, lift_table, offset)
            )
        if index == len(stages) - 1:
            local = pl.pallas_call(
                pointwise_body,
                grid=(brick_y // group,),
                out_shape=shape(height, brick_y, total_z),
                in_specs=[SMEM] * 2 + [slab] * 4 + [whole(lift_table), whole(pointwise), whole(offset)],
                out_specs=strip,
                scratch_shapes=[pltpu.VMEM((group, right_depth, total_z), BF16)],
                compiler_params=pltpu.CompilerParams(vmem_limit_bytes=24 * 1024 * 1024),
                cost_estimate=pl.CostEstimate(flops=cells * 40000, bytes_accessed=cells * 100, transcendentals=0),
            )(stiffness, density, current, before, stiff, dense, lift_table, pointwise, offset)
            arrived, local = lax.optimization_barrier((arrived, local))
        total = total + arrived.astype(F32)
    other = swap(total.astype(BF16))

    scoped = 12 * 2**20 + 4 * (6 * 2 * modes_x * modes_y * width + brick_y * coupled * width + 6 * group * coupled * total_z)
    features, wave = pl.pallas_call(
        output_body,
        grid=(brick_y // group,),
        out_shape=[shape(rows, channels, brick_y, total_z, dtype=BF16), shape(*pressure.shape)],
        in_specs=[whole(part[0]), whole(part[1])] * 2 + [strip, whole(mixing), whole(inverse_y), whole(inverse_z),
                  whole(field), whole(half)],
        out_specs=[pl.BlockSpec((rows, channels, group, total_z), lambda i: (0, 0, i, 0)), whole(pressure)],
        scratch_shapes=[
            pltpu.VMEM((brick_y, coupled, width), F32),
            pltpu.VMEM((group, 2 * coupled, total_z), BF16),
            pltpu.VMEM((height, group, total_z), F32),
        ],
        compiler_params=pltpu.CompilerParams(vmem_limit_bytes=scoped),
        cost_estimate=pl.CostEstimate(flops=cells * 2000, bytes_accessed=cells * 60, transcendentals=cells * 20),
    )(total, other, early, early_other, local, mixing, inverse_y, inverse_z, current, wave_other)
    features = features.transpose(0, 2, 1, 3)
    return (wave, features)


def solution(mesh):
    placed = (
        P(("grp", "gx"), "gy", "gz"),
        P(("grp", "gx"), "gy", "gz"),
        P(("grp", "gx"), "gy", "gz"),
        P(),
        P(),
        P(),
        P(),
        P(),
        P(),
        P(),
    )
    return jax.shard_map(
        per_device,
        mesh=mesh,
        in_specs=placed,
        out_specs=(P(("grp", "gx"), "gy", "gz"), P(("grp", "gx", "gz"), "gy", None, None)),
        check_vma=False,
    )
```

```python
import math

import numpy as np
import jax
import jax.numpy as jnp
from jax import lax
from jax.experimental import pallas as pl
from jax.experimental.pallas import tpu as pltpu
from jax.sharding import PartitionSpec as P
import ml_dtypes

STEPS = 4
FIELDS = 4
REACH = 4
EDGE = 8
stencil_taps = (-205.0 / 72.0, 8.0 / 5.0, -1.0 / 5.0, 8.0 / 315.0, -1.0 / 560.0)
F32 = jnp.float32
BF16 = jnp.bfloat16
HIGHEST = lax.Precision.HIGHEST

VMEM = pl.BlockSpec(memory_space=pltpu.VMEM)
SMEM = pl.BlockSpec(memory_space=pltpu.SMEM)
HBM = pl.BlockSpec(memory_space=pltpu.HBM)


def rounded(table):
    return table.astype(ml_dtypes.bfloat16)


def kept_modes(length, mode_count):
    position = np.arange(mode_count)
    return np.where(position < mode_count // 2, position, length - mode_count + position)


def cos_sin(source, target, length):
    product = (source[:, None] * target[None, :]) % length
    phases = np.float32(2.0 * math.pi / length) * product.astype(np.float32)
    return rounded(np.cos(phases)), rounded(np.sin(phases))


def call(body, outs, in_specs, scratch=(), flops=0, moved=0):
    return pl.pallas_call(
        body,
        out_shape=outs,
        in_specs=in_specs,
        out_specs=jax.tree.map(lambda _: VMEM, outs),
        scratch_shapes=list(scratch),
        compiler_params=pltpu.CompilerParams(vmem_limit_bytes=16 * 1024 * 1024),
        cost_estimate=pl.CostEstimate(flops=flops, bytes_accessed=moved, transcendentals=0),
    )


def high_low(value):
    high = value.astype(BF16)
    return high, (value - high.astype(F32)).astype(BF16)


def turned(value, half, sign):
    lane = lax.broadcasted_iota(jnp.int32, value.shape, value.ndim - 1)
    swapped = pltpu.roll(value, half, value.ndim - 1)
    return jnp.where(lane < half, sign * swapped, -sign * swapped)


def looked_up(material, table, entries):
    result = jnp.full(material.shape, table(0), F32)
    for entry in range(1, entries):
        result = jnp.where(material == entry, table(entry), result)
    return result


def middle(table):
    total = table[0]
    for entry in range(1, table.shape[0]):
        total = total + table[entry]
    return total * (1.0 / table.shape[0])


def edges(value_of, outs, row_parity, brick_y):
    for position, out in enumerate(outs):
        upper = row_parity == position
        out[...] = jnp.where(upper, value_of(brick_y - EDGE, brick_y), value_of(0, EDGE))


def slot():
    return (lax.axis_index("gz") + lax.axis_index("gx")) % 2


def assemble_body(count, *refs):
    tables_in, own_in, got = refs[:3], refs[3:6], refs[6:9]
    p_out, q_out, ratio, bend, sent, cells = refs[9:15]
    edge_outs = refs[15 : 15 + count]
    tables, own, semaphores = refs[15 + count : 18 + count], refs[18 + count : 21 + count], refs[21 + count]
    core, column = lax.axis_index("gz"), lax.axis_index("gy")
    rows, brick_y = p_out.shape[:2]
    start = slot() * rows
    sources = [source.at[pl.ds(start, rows)] for source in own_in[:2]] + [own_in[2]]
    copies = [
        pltpu.make_async_copy(source, target, semaphores.at[index])
        for index, (source, target) in enumerate(zip(list(tables_in) + sources, list(tables) + list(own)))
    ]
    for copy in copies:
        copy.start()
    for copy in copies:
        copy.wait()
    stiffness, density, nonlinear = tables
    entries = stiffness.shape[0]

    def whole(mine, other):
        return jnp.concatenate(
            [jnp.where(core == 0, mine, other), jnp.where(core == 0, other, mine)], axis=-1
        )

    for row in range(cells.shape[0]):
        cells[row] = whole(own[2][row], got[2][row])
    for row in range(rows):
        value = whole(own[0][row], got[0][start + row])
        p_out[row] = value
        sent[row] = value.astype(BF16)
        q_out[row] = whole(own[1][row], got[1][start + row])
        cell = cells[start + row]
        ratio[row] = looked_up(cell, lambda e: stiffness[e] / density[e], entries)
        bend[row] = looked_up(cell, lambda e: nonlinear[e], entries)
    edges(lambda a, b: p_out[:, a:b, :], edge_outs, column % 2, brick_y)


def step_body(two_sided, last, p_ref, q_ref, ratio, bend, mate, far, *rest):
    count = 2 if two_sided else 1
    halos = rest[:count]
    new_ref = rest[count]
    sent = None if last else rest[count + 1]
    edge_outs = rest[count + 2 : -1]
    padded = rest[-1]
    place = slot()
    parity = lax.axis_index("gy") % 2
    rows, brick_y, depth = p_ref.shape
    lane = lax.broadcasted_iota(jnp.int32, (brick_y, depth), 1)
    zero_edge = jnp.zeros((EDGE, depth), F32)

    def line(index):
        if 0 <= index < rows:
            return p_ref[index]
        if index < 0:
            return jnp.where(place == 0, far[index + rows].astype(F32), mate[index + rows])
        return jnp.where(place == 0, mate[index - rows], far[index - rows].astype(F32))

    for row in range(rows):
        first = halos[0][row]
        second = halos[1][row] if two_sided else zero_edge
        center = p_ref[row]
        padded[0:EDGE, :] = jnp.where(parity == 0, second, first)
        padded[EDGE : EDGE + brick_y, :] = center
        padded[EDGE + brick_y :, :] = jnp.where(parity == 0, first, second)
        total = (3.0 * stencil_taps[0]) * center
        for offset in range(1, REACH + 1):
            low, high = EDGE - offset, EDGE + offset
            pair = padded[low : low + brick_y, :] + padded[high : high + brick_y, :]
            pair = pair + (line(row - offset) + line(row + offset))
            pair = pair + jnp.where(lane >= offset, pltpu.roll(center, offset, 1), 0.0)
            pair = pair + jnp.where(
                lane < depth - offset, pltpu.roll(center, depth - offset, 1), 0.0
            )
            total = total + stencil_taps[offset] * pair
        change = center - q_ref[row]
        value = (center + change) + ratio[row] * total + bend[row] * change * change
        new_ref[row] = value
        if not last:
            sent[row] = value.astype(BF16)
    if not last:
        edges(lambda a, b: new_ref[:, a:b, :], edge_outs, parity, brick_y)


def transformed(sources, first, twiddle_x, table_z, table_y, lines, grid):
    column = lax.axis_index("gy")
    brick_y = lines.shape[0] // 4
    modes_y = grid.shape[0]
    width = table_z.shape[1]
    half = width // 2
    for field, rows in enumerate(sources):
        for row, load in enumerate(rows):
            high, low = high_low(load())
            modes = jnp.dot(high, table_z[...], preferred_element_type=F32)
            modes = modes + jnp.dot(low, table_z[...], preferred_element_type=F32)
            back = turned(modes, half, 1.0)
            high, low = high_low(modes)
            back_high, back_low = high_low(back)
            lanes = slice((field * len(rows) + row) * width, (field * len(rows) + row + 1) * width)
            for index, part in enumerate((high, back_high, low, back_low)):
                lines[index * brick_y : (index + 1) * brick_y, lanes] = part
    grid[...] = jnp.dot(table_y[column], lines[...], preferred_element_type=F32)

    def at_mode(field, modes_x):
        count = len(sources[field])
        values = [
            grid[:, (field * count + row) * width : (field * count + row + 1) * width] for row in range(count)
        ]
        backs = [turned(value, half, 1.0) for value in values]

        def summed(mode):
            total = jnp.zeros((modes_y, width), F32)
            for row in range(count):
                at = ((first + row) * modes_x + mode) * 2
                total = total + twiddle_x[at] * values[row] + twiddle_x[at + 1] * backs[row]
            return total

        return summed

    return at_mode


def materials_body(twiddle_x, stiffness, density, cells, table_z, table_y, keep, lines, grid):
    half_x = keep.shape[1]
    entries = stiffness.shape[0]
    rows = cells.shape[0]
    sources = []
    for table in (stiffness, density):
        center = middle(table)
        sources.append([
            lambda row=row, table=table, center=center: looked_up(cells[row], lambda e: table[e] - center, entries)
            for row in range(rows)
        ])
    at_mode = transformed(sources, lax.axis_index("gx") * rows, twiddle_x, table_z, table_y, lines, grid)
    core = lax.axis_index("gz")
    for field in range(2):
        summed = at_mode(field, 2 * half_x)

        @pl.loop(0, half_x)
        def _(mode):
            keep[field, mode] = summed(core * half_x + mode)


def prior_body(twiddle_x, own, mate, table_z, table_y, keep, lines, grid):
    half_x = keep.shape[0]
    rows = own.shape[0]
    place = slot()
    sources = [
        (lambda row=row: jnp.where(place == 0, own[row], mate[row])) for row in range(rows)
    ] + [(lambda row=row: jnp.where(place == 0, mate[row], own[row])) for row in range(rows)]
    at_mode = transformed([sources], lax.axis_index("gx") * (2 * rows), twiddle_x, table_z, table_y, lines, grid)
    core = lax.axis_index("gz")
    summed = at_mode(0, 2 * half_x)

    @pl.loop(0, half_x)
    def _(mode):
        keep[mode] = summed(core * half_x + mode)


def wave_body(twiddle_x, own, prior, table_z, table_y, keep, send, lines, grid):
    half_x = keep.shape[1]
    rows = own.shape[0]
    first = (lax.axis_index("gx") * 2 + slot()) * rows
    sources = [(lambda row=row: own[row]) for row in range(rows)]
    at_mode = transformed([sources], first, twiddle_x, table_z, table_y, lines, grid)
    core = lax.axis_index("gz")
    summed = at_mode(0, 2 * half_x)
    keep[1] = prior[...]
    send[1] = jnp.zeros_like(send[1])

    @pl.loop(0, half_x)
    def _(mode):
        keep[0, mode] = summed(core * half_x + mode)
        send[0, mode] = summed((1 - core) * half_x + mode).astype(BF16)


def prepare_body(
    stiffness, density, mode_ref, lift_ref, bias_ref, local_ref, spread_ref, place_ref, owner_ref, turn_ref,
    wide_ref, mixing, pointwise, lift_table, offset,
):
    block = lax.axis_index("gx") * 2 + lax.axis_index("gz")
    half = place_ref.shape[1]
    channels = lift_ref.shape[1]
    spread = owner_ref[...]

    def dot(a, b, dims=((1,), (0,))):
        return lax.dot_general(a, b, (dims, ((), ())), precision=HIGHEST, preferred_element_type=F32)

    across = ((1,), (1,))
    lifted = dot(dot(spread_ref[:, :channels], lift_ref[...], across), place_ref[...])
    lifted = lifted * spread_ref[:, channels : channels + half]
    real = dot(dot(spread, mode_ref[0], across), lifted)
    imag = dot(dot(spread, mode_ref[1], across), lifted)
    cosine = turn_ref[block, 0]
    sine = turn_ref[block, 1]
    coupled = jnp.concatenate([cosine * real - sine * imag, -(cosine * imag + sine * real)], axis=1)
    mixing[...] = coupled.astype(BF16)
    constant = dot(spread, mode_ref[0, 0:channels, :], across)
    bias = bias_ref[...] + middle(stiffness) * lift_ref[2:3, :] + middle(density) * lift_ref[3:4, :]
    offset[...] = jnp.sum(constant * bias, axis=1, keepdims=True)
    height = spread.shape[0]
    widest = wide_ref[0:channels, :]
    repeated = dot(dot(spread, local_ref[...].astype(F32), across), widest)
    pointwise[...] = (repeated * wide_ref[channels : channels + height, :]).astype(BF16)
    padded = wide_ref[channels + height :, 0:channels]
    lift_table[:, 0:FIELDS] = dot(padded, lift_ref[...], across)
    lift_table[:, FIELDS : FIELDS + 1] = dot(padded, bias_ref[...], across)
    lift_table[:, FIELDS + 1 :] = jnp.zeros_like(lift_table[:, FIELDS + 1 :])


def pointwise_body(stiffness, density, p_ref, q_ref, p_mate, q_mate, cells, lift_ref, left, offset, out, right):
    rows, group, depth = p_ref.shape
    padded_channels = lift_ref.shape[0]
    height = rows * padded_channels
    entries = stiffness.shape[0]
    core = lax.axis_index("gz")
    own = slot() == core

    @pl.when(pl.program_id(0) == 0)
    def _():
        right[...] = jnp.zeros_like(right)

    weights = [lift_ref[:, index : index + 1] for index in range(FIELDS + 1)]
    values = []
    for row in range(rows):
        cell = cells[core * rows + row]
        values.append((
            jnp.where(own, p_ref[row], p_mate[row]),
            jnp.where(own, q_ref[row], q_mate[row]),
            looked_up(cell, lambda e: stiffness[e], entries),
            looked_up(cell, lambda e: density[e], entries),
        ))
    for y in range(group):
        lifted = []
        for row in range(rows):
            total = jnp.broadcast_to(weights[FIELDS], (padded_channels, depth))
            for value, weight in zip(values[row], weights):
                total = total + value[y : y + 1, :] * weight
            lifted.append(total)
        right[y, 0:height, :] = jnp.concatenate(lifted, axis=0).astype(BF16)
        out[:, y, :] = jnp.dot(left[...], right[y], preferred_element_type=F32) + offset[...]


def output_body(
    mine, other, mine_early, other_early, local_low, local_high, left, table_y, table_z, wave_ref, wave_other,
    features, wave_out, modes, right, sums,
):
    step = pl.program_id(0)
    core, column = lax.axis_index("gz"), lax.axis_index("gy")
    half_x, modes_y, width = mine.shape[1:]
    modes_x = 2 * half_x
    half = width // 2
    rows, channels, group, depth = features.shape
    coupled = FIELDS * modes_x

    @pl.when(step == 0)
    def _():
        chunk = 4
        left_y = table_y[column]
        for field in range(FIELDS):
            own, far = ((mine, other), (mine_early, other_early))[field // 2]
            for start in range(0, modes_x, chunk):
                parts = [[], []]
                for mode in range(start, start + chunk):
                    at = (field % 2, mode % half_x)
                    value = jnp.where(core == mode // half_x, own[at], far[at].astype(F32))
                    parts[0].append(value.astype(BF16))
                    parts[1].append(turned(value, half, -1.0).astype(BF16))
                stacked = jnp.concatenate([jnp.concatenate(part, axis=1) for part in parts], axis=0)
                result = jnp.dot(left_y, stacked, preferred_element_type=F32)
                for mode in range(start, start + chunk):
                    lanes = slice((mode - start) * width, (mode - start + 1) * width)
                    modes[:, mode * FIELDS + field, :] = result[:, lanes]
        z_half = depth // 2
        place = slot()
        for row in range(rows):
            for ref, start in ((wave_ref, place * rows), (wave_other, (1 - place) * rows)):
                wave_out[start + row] = jnp.where(core == 0, ref[row, :, :z_half], ref[row, :, z_half:])

    base = pl.multiple_of(step * group, group)
    lines = modes[pl.ds(base, group)].reshape(group * coupled, width).astype(BF16)
    waves = jnp.dot(lines, table_z[...], preferred_element_type=F32).astype(BF16)
    for y in range(group):
        lines = slice(y * coupled, (y + 1) * coupled)
        right[y, 0:coupled, :] = waves[lines, :depth]
        right[y, coupled:, :] = waves[lines, depth:]
        sums[:, y, :] = jnp.dot(left[...], right[y], preferred_element_type=F32)
    for row in range(rows):
        for channel in range(channels):
            at = row * channels + channel
            total = sums[at] + jnp.where(step < pl.num_programs(0) // 2, local_low[at], local_high[at])
            inner = math.sqrt(2.0 / math.pi) * (total + 0.044715 * (total * total * total))
            total = (0.5 * total) * (1.0 + jnp.tanh(inner))
            features[row, channel] = total.astype(BF16)


def xor_pairs(count, distance):
    return [(index, index ^ distance) for index in range(count)]


def odd_pairs(count):
    pairs = [(index, index + 1) for index in range(1, count - 1, 2)]
    return pairs + [(target, source) for source, target in pairs]


def like_core_pairs(count):
    pairs = [(2 * chip + 1 - chip % 2, 2 * chip + 3 - chip % 2) for chip in range(count - 1)]
    return pairs + [(target, source) for source, target in pairs]


def per_device(
    pressure,
    previous,
    material,
    stiffness,
    density,
    nonlinear,
    lift_weight,
    lift_bias,
    mode_weight,
    local_weight,
):
    brick_x, brick_y, brick_z = pressure.shape
    cycle_count = lax.axis_size("gx")
    column_count = lax.axis_size("gy")
    core_count = lax.axis_size("gz")
    total_x = brick_x * cycle_count
    total_y = brick_y * column_count
    total_z = brick_z * core_count
    modes_x = total_x // 4
    modes_y = total_y // 4
    modes_z = total_z // 4
    width = 2 * modes_z
    channels = lift_bias.shape[0]
    rows = brick_x // core_count
    assert core_count == 2 and rows >= REACH
    blocks = cycle_count * core_count
    padded_channels = -(-channels // 8) * 8
    height = rows * channels
    coupled = FIELDS * modes_x
    right_depth = -(-rows * padded_channels // 128) * 128
    two_sided = column_count > 2

    kept_first = kept_modes(total_x, modes_x)
    kept_second = kept_modes(total_y, modes_y)
    kept_third = np.arange(modes_z)
    cz, sz = cos_sin(np.arange(total_z), kept_third, total_z)
    forward_z = np.concatenate([cz, -sz], 1)
    weight = np.where(kept_third == 0, 1.0, 2.0) / (total_x * total_y * total_z)
    wc, ws = [rounded((t.astype(np.float32) * weight).T.astype(np.float32)) for t in (cz, sz)]
    inverse_z = np.concatenate(
        [np.concatenate([wc, ws], 1), np.concatenate([-ws.astype(np.float32), wc.astype(np.float32)], 1)], 0
    )
    inverse_z = rounded(inverse_z)
    cy, sy = cos_sin(kept_second, np.arange(total_y), total_y)
    cy3, sy3 = [t.reshape(modes_y, column_count, brick_y).transpose(1, 0, 2) for t in (cy, sy)]
    forward_y = np.concatenate([cy3, sy3, cy3, sy3], 2)
    cy3, sy3 = [t.transpose(0, 2, 1) for t in (cy3, sy3)]
    inverse_y = np.concatenate([cy3, sy3], 2)
    cx, sx = [t.astype(np.float32) for t in cos_sin(np.arange(total_x), kept_first, total_x)]
    twiddle_x = np.stack([cx, sx], -1).reshape(-1)
    owner = np.tile(np.eye(channels, dtype=np.float32), (rows, 1))
    turn = np.zeros((blocks, 2, height, coupled), np.float32)
    for source, table in enumerate((cx, sx)):
        turn[:, source] = np.repeat(
            np.repeat(table.reshape(blocks, rows, modes_x), channels, 1), FIELDS, 2
        )
    padded_eye = np.eye(channels, padded_channels, dtype=np.float32)
    wide = np.zeros((channels + height + padded_channels, right_depth), np.float32)
    wide[:channels, : rows * padded_channels] = np.tile(padded_eye, (1, rows))
    wide[channels : channels + height, : rows * padded_channels] = np.kron(
        np.eye(rows), np.ones((channels, padded_channels))
    )
    wide[channels + height :, :channels] = padded_eye.T
    spread = np.tile(np.eye(channels, dtype=np.float32), (modes_x, 1))
    same = np.repeat(
        np.repeat(np.eye(modes_x, dtype=np.float32), channels, 0), FIELDS, 1
    )
    spread = np.concatenate([spread, same], 1)
    place = np.tile(np.eye(FIELDS, dtype=np.float32), (1, modes_x))

    def shape(*dims, dtype=F32):
        return jax.ShapeDtypeStruct(dims, dtype)

    cells_count = rows * brick_y * total_z
    field = shape(rows, brick_y, total_z)
    edge = [shape(rows, EDGE, total_z)] * (2 if two_sided else 1)

    swap_core = xor_pairs(core_count, 1)
    got = [lax.ppermute(array, "gz", swap_core) for array in (pressure, previous, material)]
    sending = shape(rows, brick_y, total_z, dtype=BF16)
    here = lambda *arrays: [pltpu.with_memory_space_constraint(array, pltpu.HBM) for array in arrays]
    current, before, ratio, bend, sent, cells, *edge_values = call(
        lambda *refs: assemble_body(len(edge), *refs),
        [field] * 4 + [sending, shape(brick_x, brick_y, total_z, dtype=jnp.int32)] + edge, [HBM] * 6 + [VMEM] * 3,
        [pltpu.SMEM(stiffness.shape, F32)] * 3 + [pltpu.VMEM((rows, brick_y, brick_z), F32)] * 2
        + [pltpu.VMEM((brick_x, brick_y, brick_z), jnp.int32), pltpu.SemaphoreType.DMA((6,))], moved=cells_count * 36
    )(*here(stiffness, density, nonlinear, pressure, previous, material), *got)

    mixing, pointwise, lift_table, offset = call(
        prepare_body,
        [shape(height, 2 * coupled, dtype=BF16), shape(height, right_depth, dtype=BF16),
         shape(padded_channels, 8), shape(height, 1)],
        [SMEM] * 2 + [VMEM] * 9, flops=2_000_000_000, moved=4_000_000,
    )(
        stiffness, density, mode_weight.reshape(2, modes_x * channels, channels), lift_weight,
        lift_bias.reshape(1, channels), local_weight, spread, place, owner, turn, wide,
    )

    part = [shape(2, modes_x // 2, modes_y, width, dtype=dtype) for dtype in (F32, BF16)]

    def spectrum(body, outs, inputs, lines, extra=0):
        return call(
            body, outs, [SMEM] * (1 + extra) + [VMEM] * (inputs + 2),
            [pltpu.VMEM((4 * brick_y, lines * width), BF16), pltpu.VMEM((modes_y, lines * width), F32)],
            flops=cells_count * 256 * lines, moved=cells_count * 2 * lines,
        )

    stages = [(axis, count, 2**bit) for axis, count in (("gy", column_count), ("gx", cycle_count))
              for bit in range((count - 1).bit_length())]
    swap = lambda value: lax.ppermute(value, "gz", swap_core)

    def exchange(value, axis, count, distance):
        return lax.ppermute(value.astype(BF16), axis, xor_pairs(count, distance))

    early = spectrum(materials_body, part[0], 1, 2 * brick_x, 2)(
        twiddle_x, stiffness, density, cells, forward_z, forward_y
    )
    moves = list(stages)
    pending = early_other = None

    def settle(value):
        return value if pending is None else value + pending.astype(F32)

    for repeat in range(STEPS):
        last = repeat == STEPS - 1
        far = lax.ppermute(sent, ("gx", "gz"), like_core_pairs(cycle_count))
        mate = swap(current)
        halos = [lax.ppermute(edge_values[0], "gy", xor_pairs(column_count, 1))]
        if two_sided:
            halos.append(lax.ppermute(edge_values[1], "gy", odd_pairs(column_count)))
        early, pending = settle(early), None
        halos[0], early = lax.optimization_barrier((halos[0], early))
        if moves:
            pending = exchange(early, *moves.pop(0))
        elif early_other is None:
            early_other = swap(early.astype(BF16))
        if last:
            prior = spectrum(prior_body, shape(modes_x // 2, modes_y, width), 2, brick_x)(
                twiddle_x, current, mate, forward_z, forward_y
            )
            far, prior = lax.optimization_barrier((far, prior))
            prior_mate = mate
        outs = [field] + ([] if last else [sending] + edge)
        body = lambda *refs, last=last: step_body(two_sided, last, *refs)
        new, *others = call(
            body, outs, [VMEM] * (6 + len(halos)),
            [pltpu.VMEM((brick_y + 2 * EDGE, total_z), F32)], flops=cells_count * 60, moved=cells_count * 28,
        )(current, before, ratio, bend, mate, far, *halos)
        if not last:
            sent, *edge_values = others
        current, before = new, current

    total, sent = spectrum(wave_body, part, 2, rows)(twiddle_x, current, prior, forward_z, forward_y)
    total = total + swap(sent).astype(F32)
    wave_other = swap(current)
    while moves or pending is not None:
        early, pending = settle(early), None
        if moves:
            pending = exchange(early, *moves.pop(0))
    if early_other is None:
        early_other = swap(early.astype(BF16))
    group = 8
    steps = brick_y // group
    whole = lambda array: pl.BlockSpec(array.shape, lambda i: (0,) * len(array.shape))

    def pointwise_part(start):
        slab = lambda count: pl.BlockSpec((count, group, total_z), lambda i: (0, i + start, 0))
        return pl.pallas_call(
            pointwise_body,
            grid=(steps // 2,),
            out_shape=shape(height, brick_y // 2, total_z),
            in_specs=[SMEM] * 2 + [slab(rows)] * 4 + [slab(brick_x), whole(lift_table), whole(pointwise), whole(offset)],
            out_specs=pl.BlockSpec((height, group, total_z), lambda i: (0, i, 0)),
            scratch_shapes=[pltpu.VMEM((group, right_depth, total_z), BF16)],
            compiler_params=pltpu.CompilerParams(vmem_limit_bytes=16 * 1024 * 1024),
            cost_estimate=pl.CostEstimate(flops=cells_count * 20000, bytes_accessed=cells_count * 50, transcendentals=0),
        )(stiffness, density, current, before, wave_other, prior_mate, cells, lift_table, pointwise, offset)

    for index, stage in enumerate(stages):
        arrived = exchange(total, *stage)
        if index == 0:
            arrived, mixing, pointwise, lift_table, offset = lax.optimization_barrier(
                (arrived, mixing, pointwise, lift_table, offset)
            )
        if index == len(stages) - 2:
            local_low = pointwise_part(0)
            arrived, local_low = lax.optimization_barrier((arrived, local_low))
        if index == len(stages) - 1:
            local_high = pointwise_part(steps // 2)
            arrived, local_high = lax.optimization_barrier((arrived, local_high))
        total = total + arrived.astype(F32)
    other = swap(total.astype(BF16))
    scoped = 12 * 2**20 + 4 * (6 * 2 * modes_x * modes_y * width + brick_y * coupled * width + 6 * group * coupled * total_z)
    features, wave = pl.pallas_call(
        output_body,
        grid=(steps,),
        out_shape=[shape(rows, channels, brick_y, total_z, dtype=BF16), shape(*pressure.shape)],
        in_specs=[whole(part[0]), whole(part[1])] * 2
        + [pl.BlockSpec((height, group, total_z), lambda i: (0, jnp.minimum(i, steps // 2 - 1), 0)),
           pl.BlockSpec((height, group, total_z), lambda i: (0, jnp.maximum(i - steps // 2, 0), 0)),
           whole(mixing), whole(inverse_y), whole(inverse_z),
                  whole(field), whole(field)],
        out_specs=[pl.BlockSpec((rows, channels, group, total_z), lambda i: (0, 0, i, 0)), whole(pressure)],
        scratch_shapes=[
            pltpu.VMEM((brick_y, coupled, width), F32),
            pltpu.VMEM((group, 2 * coupled, total_z), BF16),
            pltpu.VMEM((height, group, total_z), F32),
        ],
        compiler_params=pltpu.CompilerParams(vmem_limit_bytes=scoped),
        cost_estimate=pl.CostEstimate(flops=cells_count * 2000, bytes_accessed=cells_count * 60, transcendentals=cells_count * 20),
    )(total, other, early, early_other, local_low, local_high, mixing, inverse_y, inverse_z, current, wave_other)
    features = features.transpose(0, 2, 1, 3)
    return (wave, features)


def solution(mesh):
    placed = (
        P(("grp", "gx"), "gy", "gz"),
        P(("grp", "gx"), "gy", "gz"),
        P(("grp", "gx"), "gy", "gz"),
        P(),
        P(),
        P(),
        P(),
        P(),
        P(),
        P(),
    )
    return jax.shard_map(
        per_device,
        mesh=mesh,
        in_specs=placed,
        out_specs=(P(("grp", "gx"), "gy", "gz"), P(("grp", "gx", "gz"), "gy", None, None)),
        check_vma=False,
    )
```

```python
import math

import numpy as np
import jax
import jax.numpy as jnp
from jax import lax
from jax.experimental import pallas as pl
from jax.experimental.pallas import tpu as pltpu
from jax.sharding import PartitionSpec as P
import ml_dtypes

STEPS = 4
FIELDS = 4
REACH = 4
EDGE = 8
stencil_taps = (-205.0 / 72.0, 8.0 / 5.0, -1.0 / 5.0, 8.0 / 315.0, -1.0 / 560.0)
F32 = jnp.float32
BF16 = jnp.bfloat16
HIGHEST = lax.Precision.HIGHEST

VMEM = pl.BlockSpec(memory_space=pltpu.VMEM)
SMEM = pl.BlockSpec(memory_space=pltpu.SMEM)
HBM = pl.BlockSpec(memory_space=pltpu.HBM)


def rounded(table):
    return table.astype(ml_dtypes.bfloat16)


def kept_modes(length, mode_count):
    position = np.arange(mode_count)
    return np.where(position < mode_count // 2, position, length - mode_count + position)


def cos_sin(source, target, length):
    product = (source[:, None] * target[None, :]) % length
    phases = np.float32(2.0 * math.pi / length) * product.astype(np.float32)
    return rounded(np.cos(phases)), rounded(np.sin(phases))


def call(body, outs, in_specs, scratch=(), flops=0, moved=0):
    return pl.pallas_call(
        body,
        out_shape=outs,
        in_specs=in_specs,
        out_specs=jax.tree.map(lambda _: VMEM, outs),
        scratch_shapes=list(scratch),
        compiler_params=pltpu.CompilerParams(vmem_limit_bytes=16 * 1024 * 1024),
        cost_estimate=pl.CostEstimate(flops=flops, bytes_accessed=moved, transcendentals=0),
    )


def high_low(value):
    high = value.astype(BF16)
    return high, (value - high.astype(F32)).astype(BF16)


def turned(value, half, sign):
    lane = lax.broadcasted_iota(jnp.int32, value.shape, value.ndim - 1)
    swapped = pltpu.roll(value, half, value.ndim - 1)
    return jnp.where(lane < half, sign * swapped, -sign * swapped)


def looked_up(material, table, entries):
    result = jnp.full(material.shape, table(0), F32)
    for entry in range(1, entries):
        result = jnp.where(material == entry, table(entry), result)
    return result


def middle(table):
    total = table[0]
    for entry in range(1, table.shape[0]):
        total = total + table[entry]
    return total * (1.0 / table.shape[0])


def edges(value_of, outs, row_parity, brick_y):
    for position, out in enumerate(outs):
        upper = row_parity == position
        out[...] = jnp.where(upper, value_of(brick_y - EDGE, brick_y), value_of(0, EDGE))


def slot():
    return (lax.axis_index("gz") + lax.axis_index("gx")) % 2


def assemble_body(count, *refs):
    tables_in, own_in, got = refs[:3], refs[3:6], refs[6:9]
    p_out, q_out, ratio, bend, sent, cells = refs[9:15]
    edge_outs = refs[15 : 15 + count]
    tables, own, semaphores = refs[15 + count : 18 + count], refs[18 + count : 21 + count], refs[21 + count]
    core, column = lax.axis_index("gz"), lax.axis_index("gy")
    rows, brick_y = p_out.shape[:2]
    start = slot() * rows
    sources = [source.at[pl.ds(start, rows)] for source in own_in[:2]] + [own_in[2]]
    copies = [
        pltpu.make_async_copy(source, target, semaphores.at[index])
        for index, (source, target) in enumerate(zip(list(tables_in) + sources, list(tables) + list(own)))
    ]
    for copy in copies:
        copy.start()
    for copy in copies:
        copy.wait()
    stiffness, density, nonlinear = tables
    entries = stiffness.shape[0]

    def whole(mine, other):
        return jnp.concatenate(
            [jnp.where(core == 0, mine, other), jnp.where(core == 0, other, mine)], axis=-1
        )

    for row in range(cells.shape[0]):
        cells[row] = whole(own[2][row], got[2][row])
    for row in range(rows):
        value = whole(own[0][row], got[0][start + row])
        p_out[row] = value
        sent[row] = value.astype(BF16)
        q_out[row] = whole(own[1][row], got[1][start + row])
        cell = cells[start + row]
        ratio[row] = looked_up(cell, lambda e: stiffness[e] / density[e], entries)
        bend[row] = looked_up(cell, lambda e: nonlinear[e], entries)
    edges(lambda a, b: p_out[:, a:b, :], edge_outs, column % 2, brick_y)


def step_body(two_sided, last, p_ref, q_ref, ratio, bend, mate, far, *rest):
    count = 2 if two_sided else 1
    halos = rest[:count]
    new_ref = rest[count]
    sent = None if last else rest[count + 1]
    edge_outs = rest[count + 2 : -1]
    padded = rest[-1]
    place = slot()
    parity = lax.axis_index("gy") % 2
    rows, brick_y, depth = p_ref.shape
    lane = lax.broadcasted_iota(jnp.int32, (brick_y, depth), 1)
    zero_edge = jnp.zeros((EDGE, depth), F32)

    def line(index):
        if 0 <= index < rows:
            return p_ref[index]
        if index < 0:
            return jnp.where(place == 0, far[index + rows].astype(F32), mate[index + rows])
        return jnp.where(place == 0, mate[index - rows], far[index - rows].astype(F32))

    for row in range(rows):
        first = halos[0][row]
        second = halos[1][row] if two_sided else zero_edge
        center = p_ref[row]
        padded[0:EDGE, :] = jnp.where(parity == 0, second, first)
        padded[EDGE : EDGE + brick_y, :] = center
        padded[EDGE + brick_y :, :] = jnp.where(parity == 0, first, second)
        total = (3.0 * stencil_taps[0]) * center
        for offset in range(1, REACH + 1):
            low, high = EDGE - offset, EDGE + offset
            pair = padded[low : low + brick_y, :] + padded[high : high + brick_y, :]
            pair = pair + (line(row - offset) + line(row + offset))
            pair = pair + jnp.where(lane >= offset, pltpu.roll(center, offset, 1), 0.0)
            pair = pair + jnp.where(
                lane < depth - offset, pltpu.roll(center, depth - offset, 1), 0.0
            )
            total = total + stencil_taps[offset] * pair
        change = center - q_ref[row]
        value = (center + change) + ratio[row] * total + bend[row] * change * change
        new_ref[row] = value
        if not last:
            sent[row] = value.astype(BF16)
    if not last:
        edges(lambda a, b: new_ref[:, a:b, :], edge_outs, parity, brick_y)


def transformed(sources, first, twiddle_x, table_z, table_y, lines, grid):
    column = lax.axis_index("gy")
    brick_y = lines.shape[0] // 4
    modes_y = grid.shape[0]
    width = table_z.shape[1]
    half = width // 2
    for field, rows in enumerate(sources):
        for row, load in enumerate(rows):
            high, low = high_low(load())
            modes = jnp.dot(high, table_z[...], preferred_element_type=F32)
            modes = modes + jnp.dot(low, table_z[...], preferred_element_type=F32)
            back = turned(modes, half, 1.0)
            high, low = high_low(modes)
            back_high, back_low = high_low(back)
            lanes = slice((field * len(rows) + row) * width, (field * len(rows) + row + 1) * width)
            for index, part in enumerate((high, back_high, low, back_low)):
                lines[index * brick_y : (index + 1) * brick_y, lanes] = part
    grid[...] = jnp.dot(table_y[column], lines[...], preferred_element_type=F32)

    def at_mode(field, modes_x):
        count = len(sources[field])
        values = [
            grid[:, (field * count + row) * width : (field * count + row + 1) * width] for row in range(count)
        ]
        backs = [turned(value, half, 1.0) for value in values]

        def summed(mode):
            total = jnp.zeros((modes_y, width), F32)
            for row in range(count):
                at = ((first + row) * modes_x + mode) * 2
                total = total + twiddle_x[at] * values[row] + twiddle_x[at + 1] * backs[row]
            return total

        return summed

    return at_mode


def materials_body(*refs):
    sources, cells, keep, lines, grid = refs[:5], refs[5], refs[6], refs[7], refs[8]
    targets, semaphores = refs[9:14], refs[14]
    copies = [
        pltpu.make_async_copy(source, target, semaphores.at[index])
        for index, (source, target) in enumerate(zip(sources, targets))
    ]
    for copy in copies:
        copy.start()
    for copy in copies:
        copy.wait()
    twiddle_x, stiffness, density, table_z, table_y = targets
    half_x = keep.shape[1]
    entries = stiffness.shape[0]
    rows = cells.shape[0]
    sources = []
    for table in (stiffness, density):
        center = middle(table)
        sources.append([
            lambda row=row, table=table, center=center: looked_up(cells[row], lambda e: table[e] - center, entries)
            for row in range(rows)
        ])
    at_mode = transformed(sources, lax.axis_index("gx") * rows, twiddle_x, table_z, table_y, lines, grid)
    core = lax.axis_index("gz")
    for field in range(2):
        summed = at_mode(field, 2 * half_x)

        @pl.loop(0, half_x)
        def _(mode):
            keep[field, mode] = summed(core * half_x + mode)


def prior_body(twiddle_x, own, mate, table_z, table_y, keep, lines, grid):
    half_x = keep.shape[0]
    rows = own.shape[0]
    place = slot()
    sources = [
        (lambda row=row: jnp.where(place == 0, own[row], mate[row])) for row in range(rows)
    ] + [(lambda row=row: jnp.where(place == 0, mate[row], own[row])) for row in range(rows)]
    at_mode = transformed([sources], lax.axis_index("gx") * (2 * rows), twiddle_x, table_z, table_y, lines, grid)
    core = lax.axis_index("gz")
    summed = at_mode(0, 2 * half_x)

    @pl.loop(0, half_x)
    def _(mode):
        keep[mode] = summed(core * half_x + mode)


def wave_body(twiddle_x, own, prior, early, table_z, table_y, keep, send, lines, grid):
    half_x = keep.shape[1]
    rows = own.shape[0]
    first = (lax.axis_index("gx") * 2 + slot()) * rows
    sources = [(lambda row=row: own[row]) for row in range(rows)]
    at_mode = transformed([sources], first, twiddle_x, table_z, table_y, lines, grid)
    core = lax.axis_index("gz")
    summed = at_mode(0, 2 * half_x)
    keep[1] = prior[...]
    keep[2:4] = early[...]

    @pl.loop(0, half_x)
    def _(mode):
        keep[0, mode] = summed(core * half_x + mode)
        send[0, mode] = summed((1 - core) * half_x + mode).astype(BF16)


def prepare_body(
    stiffness, density, mode_ref, lift_ref, bias_ref, local_ref, spread_ref, place_ref, owner_ref, turn_ref,
    wide_ref, mixing, pointwise, lift_table, offset,
):
    block = lax.axis_index("gx") * 2 + lax.axis_index("gz")
    half = place_ref.shape[1]
    channels = lift_ref.shape[1]
    spread = owner_ref[...]

    def dot(a, b, dims=((1,), (0,))):
        return lax.dot_general(a, b, (dims, ((), ())), precision=HIGHEST, preferred_element_type=F32)

    across = ((1,), (1,))
    lifted = dot(dot(spread_ref[:, :channels], lift_ref[...], across), place_ref[...])
    lifted = lifted * spread_ref[:, channels : channels + half]
    real = dot(dot(spread, mode_ref[0], across), lifted)
    imag = dot(dot(spread, mode_ref[1], across), lifted)
    cosine = turn_ref[block, 0]
    sine = turn_ref[block, 1]
    coupled = jnp.concatenate([cosine * real - sine * imag, -(cosine * imag + sine * real)], axis=1)
    mixing[...] = coupled.astype(BF16)
    constant = dot(spread, mode_ref[0, 0:channels, :], across)
    bias = bias_ref[...] + middle(stiffness) * lift_ref[2:3, :] + middle(density) * lift_ref[3:4, :]
    offset[...] = jnp.sum(constant * bias, axis=1, keepdims=True)
    height = spread.shape[0]
    widest = wide_ref[0:channels, :]
    repeated = dot(dot(spread, local_ref[...].astype(F32), across), widest)
    pointwise[...] = (repeated * wide_ref[channels : channels + height, :]).astype(BF16)
    padded = wide_ref[channels + height :, 0:channels]
    lift_table[:, 0:FIELDS] = dot(padded, lift_ref[...], across)
    lift_table[:, FIELDS : FIELDS + 1] = dot(padded, bias_ref[...], across)
    lift_table[:, FIELDS + 1 :] = jnp.zeros_like(lift_table[:, FIELDS + 1 :])


def pointwise_body(stiffness, density, p_ref, q_ref, p_mate, q_mate, cells, lift_ref, left, offset, out, right):
    rows, group, depth = p_ref.shape
    padded_channels = lift_ref.shape[0]
    height = rows * padded_channels
    entries = stiffness.shape[0]
    core = lax.axis_index("gz")
    own = slot() == core

    @pl.when(pl.program_id(0) == 0)
    def _():
        right[...] = jnp.zeros_like(right)

    weights = [lift_ref[:, index : index + 1] for index in range(FIELDS + 1)]
    values = []
    for row in range(rows):
        cell = cells[core * rows + row]
        values.append((
            jnp.where(own, p_ref[row], p_mate[row]),
            jnp.where(own, q_ref[row], q_mate[row]),
            looked_up(cell, lambda e: stiffness[e], entries),
            looked_up(cell, lambda e: density[e], entries),
        ))
    for y in range(group):
        lifted = []
        for row in range(rows):
            total = jnp.broadcast_to(weights[FIELDS], (padded_channels, depth))
            for value, weight in zip(values[row], weights):
                total = total + value[y : y + 1, :] * weight
            lifted.append(total)
        right[y, 0:height, :] = jnp.concatenate(lifted, axis=0).astype(BF16)
        out[:, y, :] = jnp.dot(left[...], right[y], preferred_element_type=F32) + offset[...]


def output_body(
    mine, other, local_low, local_high, left, table_y, table_z, wave_ref, wave_other,
    features, wave_out, modes, right, sums,
):
    step = pl.program_id(0)
    core, column = lax.axis_index("gz"), lax.axis_index("gy")
    half_x, modes_y, width = mine.shape[1:]
    modes_x = 2 * half_x
    half = width // 2
    rows, channels, group, depth = features.shape
    coupled = FIELDS * modes_x

    @pl.when(step == 0)
    def _():
        chunk = 4
        left_y = table_y[column]
        for field in range(FIELDS):
            for start in range(0, modes_x, chunk):
                parts = [[], []]
                for mode in range(start, start + chunk):
                    at = (field, mode % half_x)
                    value = jnp.where(core == mode // half_x, mine[at], other[at].astype(F32))
                    parts[0].append(value.astype(BF16))
                    parts[1].append(turned(value, half, -1.0).astype(BF16))
                stacked = jnp.concatenate([jnp.concatenate(part, axis=1) for part in parts], axis=0)
                result = jnp.dot(left_y, stacked, preferred_element_type=F32)
                for mode in range(start, start + chunk):
                    lanes = slice((mode - start) * width, (mode - start + 1) * width)
                    modes[:, mode * FIELDS + field, :] = result[:, lanes]
        z_half = depth // 2
        place = slot()
        for row in range(rows):
            for ref, start in ((wave_ref, place * rows), (wave_other, (1 - place) * rows)):
                wave_out[start + row] = jnp.where(core == 0, ref[row, :, :z_half], ref[row, :, z_half:])

    base = pl.multiple_of(step * group, group)
    lines = modes[pl.ds(base, group)].reshape(group * coupled, width).astype(BF16)
    waves = jnp.dot(lines, table_z[...], preferred_element_type=F32).astype(BF16)
    for y in range(group):
        lines = slice(y * coupled, (y + 1) * coupled)
        right[y, 0:coupled, :] = waves[lines, :depth]
        right[y, coupled:, :] = waves[lines, depth:]
        sums[:, y, :] = jnp.dot(left[...], right[y], preferred_element_type=F32)
    for row in range(rows):
        for channel in range(channels):
            at = row * channels + channel
            total = sums[at] + jnp.where(step < pl.num_programs(0) // 2, local_low[at], local_high[at])
            inner = math.sqrt(2.0 / math.pi) * (total + 0.044715 * (total * total * total))
            total = (0.5 * total) * (1.0 + jnp.tanh(inner))
            features[row, channel] = total.astype(BF16)


def xor_pairs(count, distance):
    return [(index, index ^ distance) for index in range(count)]


def odd_pairs(count):
    pairs = [(index, index + 1) for index in range(1, count - 1, 2)]
    return pairs + [(target, source) for source, target in pairs]


def like_core_pairs(count):
    pairs = [(2 * chip + 1 - chip % 2, 2 * chip + 3 - chip % 2) for chip in range(count - 1)]
    return pairs + [(target, source) for source, target in pairs]


def per_device(
    pressure,
    previous,
    material,
    stiffness,
    density,
    nonlinear,
    lift_weight,
    lift_bias,
    mode_weight,
    local_weight,
):
    brick_x, brick_y, brick_z = pressure.shape
    cycle_count = lax.axis_size("gx")
    column_count = lax.axis_size("gy")
    core_count = lax.axis_size("gz")
    total_x = brick_x * cycle_count
    total_y = brick_y * column_count
    total_z = brick_z * core_count
    modes_x = total_x // 4
    modes_y = total_y // 4
    modes_z = total_z // 4
    width = 2 * modes_z
    channels = lift_bias.shape[0]
    rows = brick_x // core_count
    assert core_count == 2 and rows >= REACH
    blocks = cycle_count * core_count
    padded_channels = -(-channels // 8) * 8
    height = rows * channels
    coupled = FIELDS * modes_x
    right_depth = -(-rows * padded_channels // 128) * 128
    two_sided = column_count > 2

    kept_first = kept_modes(total_x, modes_x)
    kept_second = kept_modes(total_y, modes_y)
    kept_third = np.arange(modes_z)
    cz, sz = cos_sin(np.arange(total_z), kept_third, total_z)
    forward_z = np.concatenate([cz, -sz], 1)
    weight = np.where(kept_third == 0, 1.0, 2.0) / (total_x * total_y * total_z)
    wc, ws = [rounded((t.astype(np.float32) * weight).T.astype(np.float32)) for t in (cz, sz)]
    inverse_z = np.concatenate(
        [np.concatenate([wc, ws], 1), np.concatenate([-ws.astype(np.float32), wc.astype(np.float32)], 1)], 0
    )
    inverse_z = rounded(inverse_z)
    cy, sy = cos_sin(kept_second, np.arange(total_y), total_y)
    cy3, sy3 = [t.reshape(modes_y, column_count, brick_y).transpose(1, 0, 2) for t in (cy, sy)]
    forward_y = np.concatenate([cy3, sy3, cy3, sy3], 2)
    cy3, sy3 = [t.transpose(0, 2, 1) for t in (cy3, sy3)]
    inverse_y = np.concatenate([cy3, sy3], 2)
    cx, sx = [t.astype(np.float32) for t in cos_sin(np.arange(total_x), kept_first, total_x)]
    twiddle_x = np.stack([cx, sx], -1).reshape(-1)
    owner = np.tile(np.eye(channels, dtype=np.float32), (rows, 1))
    turn = np.zeros((blocks, 2, height, coupled), np.float32)
    for source, table in enumerate((cx, sx)):
        turn[:, source] = np.repeat(
            np.repeat(table.reshape(blocks, rows, modes_x), channels, 1), FIELDS, 2
        )
    padded_eye = np.eye(channels, padded_channels, dtype=np.float32)
    wide = np.zeros((channels + height + padded_channels, right_depth), np.float32)
    wide[:channels, : rows * padded_channels] = np.tile(padded_eye, (1, rows))
    wide[channels : channels + height, : rows * padded_channels] = np.kron(
        np.eye(rows), np.ones((channels, padded_channels))
    )
    wide[channels + height :, :channels] = padded_eye.T
    spread = np.tile(np.eye(channels, dtype=np.float32), (modes_x, 1))
    same = np.repeat(
        np.repeat(np.eye(modes_x, dtype=np.float32), channels, 0), FIELDS, 1
    )
    spread = np.concatenate([spread, same], 1)
    place = np.tile(np.eye(FIELDS, dtype=np.float32), (1, modes_x))

    def shape(*dims, dtype=F32):
        return jax.ShapeDtypeStruct(dims, dtype)

    cells_count = rows * brick_y * total_z
    field = shape(rows, brick_y, total_z)
    edge = [shape(rows, EDGE, total_z)] * (2 if two_sided else 1)

    swap_core = xor_pairs(core_count, 1)
    got = [lax.ppermute(array, "gz", swap_core) for array in (pressure, previous, material)]
    sending = shape(rows, brick_y, total_z, dtype=BF16)
    here = lambda *arrays: [pltpu.with_memory_space_constraint(array, pltpu.HBM) for array in arrays]
    current, before, ratio, bend, sent, cells, *edge_values = call(
        lambda *refs: assemble_body(len(edge), *refs),
        [field] * 4 + [sending, shape(brick_x, brick_y, total_z, dtype=jnp.int32)] + edge, [HBM] * 6 + [VMEM] * 3,
        [pltpu.SMEM(stiffness.shape, F32)] * 3 + [pltpu.VMEM((rows, brick_y, brick_z), F32)] * 2
        + [pltpu.VMEM((brick_x, brick_y, brick_z), jnp.int32), pltpu.SemaphoreType.DMA((6,))], moved=cells_count * 36
    )(*here(stiffness, density, nonlinear, pressure, previous, material), *got)

    mixing, pointwise, lift_table, offset = call(
        prepare_body,
        [shape(height, 2 * coupled, dtype=BF16), shape(height, right_depth, dtype=BF16),
         shape(padded_channels, 8), shape(height, 1)],
        [SMEM] * 2 + [VMEM] * 9, flops=2_000_000_000, moved=4_000_000,
    )(
        stiffness, density, mode_weight.reshape(2, modes_x * channels, channels), lift_weight,
        lift_bias.reshape(1, channels), local_weight, spread, place, owner, turn, wide,
    )

    part = lambda fields, dtype: shape(fields, modes_x // 2, modes_y, width, dtype=dtype)

    def spectrum(body, outs, inputs, lines, specs=None, scratch=()):
        return call(
            body, outs, specs or [SMEM] + [VMEM] * (inputs + 2),
            [pltpu.VMEM((4 * brick_y, lines * width), BF16), pltpu.VMEM((modes_y, lines * width), F32), *scratch],
            flops=cells_count * 256 * lines, moved=cells_count * 2 * lines,
        )

    stages = [(axis, count, 2**bit) for axis, count in (("gy", column_count), ("gx", cycle_count))
              for bit in range((count - 1).bit_length())]
    swap = lambda value: lax.ppermute(value, "gz", swap_core)

    def exchange(value, axis, count, distance):
        return lax.ppermute(value.astype(BF16), axis, xor_pairs(count, distance))

    tables = (twiddle_x, stiffness, density, forward_z, forward_y)
    early = spectrum(
        materials_body, part(2, F32), 1, 2 * brick_x, [HBM] * 5 + [VMEM],
        [(pltpu.SMEM if table.ndim == 1 else pltpu.VMEM)(table.shape, table.dtype) for table in tables]
        + [pltpu.SemaphoreType.DMA((5,))],
    )(*here(*[jnp.asarray(table) for table in tables]), cells)

    for repeat in range(STEPS):
        last = repeat == STEPS - 1
        far = lax.ppermute(sent, ("gx", "gz"), like_core_pairs(cycle_count))
        mate = swap(current)
        halos = [lax.ppermute(edge_values[0], "gy", xor_pairs(column_count, 1))]
        if two_sided:
            halos.append(lax.ppermute(edge_values[1], "gy", odd_pairs(column_count)))
        if repeat == 0:
            far, early = lax.optimization_barrier((far, early))
        if repeat == 1:
            far, mixing, pointwise, lift_table, offset = lax.optimization_barrier(
                (far, mixing, pointwise, lift_table, offset)
            )
        if last:
            prior = spectrum(prior_body, shape(modes_x // 2, modes_y, width), 2, brick_x)(
                twiddle_x, current, mate, forward_z, forward_y
            )
            far, prior = lax.optimization_barrier((far, prior))
            prior_mate = mate
        outs = [field] + ([] if last else [sending] + edge)
        body = lambda *refs, last=last: step_body(two_sided, last, *refs)
        new, *others = call(
            body, outs, [VMEM] * (6 + len(halos)),
            [pltpu.VMEM((brick_y + 2 * EDGE, total_z), F32)], flops=cells_count * 60, moved=cells_count * 28,
        )(current, before, ratio, bend, mate, far, *halos)
        if not last:
            sent, *edge_values = others
        current, before = new, current

    total, sent = spectrum(wave_body, [part(FIELDS, F32), part(1, BF16)], 3, rows)(
        twiddle_x, current, prior, early, forward_z, forward_y
    )
    total = total + jnp.pad(swap(sent).astype(F32), ((0, FIELDS - 1), (0, 0), (0, 0), (0, 0)))
    wave_other = swap(current)
    group = 8
    steps = brick_y // group
    whole = lambda array: pl.BlockSpec(array.shape, lambda i: (0,) * len(array.shape))

    def pointwise_part(start):
        slab = lambda count: pl.BlockSpec((count, group, total_z), lambda i: (0, i + start, 0))
        return pl.pallas_call(
            pointwise_body,
            grid=(steps // 2,),
            out_shape=shape(height, brick_y // 2, total_z),
            in_specs=[SMEM] * 2 + [slab(rows)] * 4 + [slab(brick_x), whole(lift_table), whole(pointwise), whole(offset)],
            out_specs=pl.BlockSpec((height, group, total_z), lambda i: (0, i, 0)),
            scratch_shapes=[pltpu.VMEM((group, right_depth, total_z), BF16)],
            compiler_params=pltpu.CompilerParams(vmem_limit_bytes=16 * 1024 * 1024),
            cost_estimate=pl.CostEstimate(flops=cells_count * 20000, bytes_accessed=cells_count * 50, transcendentals=0),
        )(stiffness, density, current, before, wave_other, prior_mate, cells, lift_table, pointwise, offset)

    for index, stage in enumerate(stages):
        arrived = exchange(total, *stage)
        if index == len(stages) - 2:
            local_low = pointwise_part(0)
            arrived, local_low = lax.optimization_barrier((arrived, local_low))
        if index == len(stages) - 1:
            local_high = pointwise_part(steps // 2)
            arrived, local_high = lax.optimization_barrier((arrived, local_high))
        total = total + arrived.astype(F32)
    other = swap(total.astype(BF16))
    scoped = 12 * 2**20 + 4 * (6 * 2 * modes_x * modes_y * width + brick_y * coupled * width + 6 * group * coupled * total_z)
    features, wave = pl.pallas_call(
        output_body,
        grid=(steps,),
        out_shape=[shape(rows, channels, brick_y, total_z, dtype=BF16), shape(*pressure.shape)],
        in_specs=[whole(part(FIELDS, F32)), whole(part(FIELDS, BF16)),
           pl.BlockSpec((height, group, total_z), lambda i: (0, jnp.minimum(i, steps // 2 - 1), 0)),
           pl.BlockSpec((height, group, total_z), lambda i: (0, jnp.maximum(i - steps // 2, 0), 0)),
           whole(mixing), whole(inverse_y), whole(inverse_z),
                  whole(field), whole(field)],
        out_specs=[pl.BlockSpec((rows, channels, group, total_z), lambda i: (0, 0, i, 0)), whole(pressure)],
        scratch_shapes=[
            pltpu.VMEM((brick_y, coupled, width), F32),
            pltpu.VMEM((group, 2 * coupled, total_z), BF16),
            pltpu.VMEM((height, group, total_z), F32),
        ],
        compiler_params=pltpu.CompilerParams(vmem_limit_bytes=scoped),
        cost_estimate=pl.CostEstimate(flops=cells_count * 2000, bytes_accessed=cells_count * 60, transcendentals=cells_count * 20),
    )(total, other, local_low, local_high, mixing, inverse_y, inverse_z, current, wave_other)
    features = features.transpose(0, 2, 1, 3)
    return (wave, features)


def solution(mesh):
    placed = (
        P(("grp", "gx"), "gy", "gz"),
        P(("grp", "gx"), "gy", "gz"),
        P(("grp", "gx"), "gy", "gz"),
        P(),
        P(),
        P(),
        P(),
        P(),
        P(),
        P(),
    )
    return jax.shard_map(
        per_device,
        mesh=mesh,
        in_specs=placed,
        out_specs=(P(("grp", "gx"), "gy", "gz"), P(("grp", "gx", "gz"), "gy", None, None)),
        check_vma=False,
    )
```

```python
import math

import numpy as np
import jax
import jax.numpy as jnp
from jax import lax
from jax.experimental import pallas as pl
from jax.experimental.pallas import tpu as pltpu
from jax.sharding import PartitionSpec as P
import ml_dtypes

STEPS = 4
FIELDS = 4
REACH = 4
PAD = 8
EDGE = STEPS * REACH
stencil_taps = (-205.0 / 72.0, 8.0 / 5.0, -1.0 / 5.0, 8.0 / 315.0, -1.0 / 560.0)
F32 = jnp.float32
BF16 = jnp.bfloat16
HIGHEST = lax.Precision.HIGHEST

VMEM = pl.BlockSpec(memory_space=pltpu.VMEM)
SMEM = pl.BlockSpec(memory_space=pltpu.SMEM)
HBM = pl.BlockSpec(memory_space=pltpu.HBM)


def rounded(table):
    return table.astype(ml_dtypes.bfloat16)


def kept_modes(length, mode_count):
    position = np.arange(mode_count)
    return np.where(position < mode_count // 2, position, length - mode_count + position)


def cos_sin(source, target, length):
    product = (source[:, None] * target[None, :]) % length
    phases = np.float32(2.0 * math.pi / length) * product.astype(np.float32)
    return rounded(np.cos(phases)), rounded(np.sin(phases))


def call(body, outs, in_specs, scratch=(), flops=0, moved=0):
    return pl.pallas_call(
        body,
        out_shape=outs,
        in_specs=in_specs,
        out_specs=jax.tree.map(lambda _: VMEM, outs),
        scratch_shapes=list(scratch),
        compiler_params=pltpu.CompilerParams(vmem_limit_bytes=16 * 1024 * 1024),
        cost_estimate=pl.CostEstimate(flops=flops, bytes_accessed=moved, transcendentals=0),
    )


def high_low(value):
    high = value.astype(BF16)
    return high, (value - high.astype(F32)).astype(BF16)


def turned(value, half, sign):
    lane = lax.broadcasted_iota(jnp.int32, value.shape, value.ndim - 1)
    swapped = pltpu.roll(value, half, value.ndim - 1)
    return jnp.where(lane < half, sign * swapped, -sign * swapped)


def looked_up(material, table, entries):
    result = jnp.full(material.shape, table(0), F32)
    for entry in range(1, entries):
        result = jnp.where(material == entry, table(entry), result)
    return result


def middle(table):
    total = table[0]
    for entry in range(1, table.shape[0]):
        total = total + table[entry]
    return total * (1.0 / table.shape[0])


def slot():
    return (lax.axis_index("gz") + lax.axis_index("gx")) % 2


def own_start(sides):
    return EDGE if sides == 2 else pl.multiple_of(EDGE * (lax.axis_index("gy") % 2), EDGE)


def pack_body(sides, *refs):
    own_in, sends, buffer, kinds, semaphores = refs[:3], refs[3 : 3 + 2 * sides], refs[-3], refs[-2], refs[-1]
    rows, brick_y = sends[0].shape[1], own_in[0].shape[1]
    parity = lax.axis_index("gy") % 2
    copies = []
    for position in range(sides):
        edge = pl.multiple_of(jnp.where(parity == position, brick_y - EDGE, 0), EDGE)
        for index in range(2):
            block = slot() if index == 0 else 1 - slot()
            for array, source in enumerate(own_in):
                at = (position * 2 + index) * 3 + array
                target = kinds.at[position * 2 + index] if array == 2 else buffer.at[(position * 2 + index) * 2 + array]
                copies.append(pltpu.make_async_copy(
                    source.at[pl.ds(block * rows, rows), pl.ds(edge, EDGE)], target, semaphores.at[at]
                ))
    for copy in copies:
        copy.start()
    for copy in copies:
        copy.wait()
    for index, send in enumerate(sends):
        send[0:2] = buffer[2 * index : 2 * index + 2].astype(BF16)
        send[2] = kinds[index].astype(F32).astype(BF16)


def assemble_body(sides, last_column, *refs):
    tables_in, own_in, got, borders = refs[:3], refs[3:6], refs[6:9], refs[9 : 9 + 2 * sides]
    refs = refs[9 + 2 * sides :]
    p_out, q_out, ratio, bend, sent, cells = refs[:6]
    tables, own, semaphores = refs[6:9], refs[9:12], refs[12]
    core, column = lax.axis_index("gz"), lax.axis_index("gy")
    rows = p_out.shape[0]
    brick_y = cells.shape[1]
    start = slot() * rows
    sources = [source.at[pl.ds(start, rows)] for source in own_in[:2]] + [own_in[2]]
    copies = [
        pltpu.make_async_copy(source, target, semaphores.at[index])
        for index, (source, target) in enumerate(zip(list(tables_in) + sources, list(tables) + list(own)))
    ]
    for copy in copies:
        copy.start()
    for copy in copies:
        copy.wait()
    stiffness, density, nonlinear = tables
    entries = stiffness.shape[0]

    def whole(mine, other):
        return jnp.concatenate(
            [jnp.where(core == 0, mine, other), jnp.where(core == 0, other, mine)], axis=-1
        )

    def place(row, at, length, current, before, cell, inside):
        lines = pl.ds(at, length)
        p_out[row, lines, :] = current
        sent[row, lines, :] = current.astype(BF16)
        q_out[row, lines, :] = before
        ratio[row, lines, :] = inside * looked_up(cell, lambda e: stiffness[e] / density[e], entries)
        bend[row, lines, :] = inside * looked_up(cell, lambda e: nonlinear[e], entries)

    for row in range(cells.shape[0]):
        cells[row] = whole(own[2][row], got[2][row])
    first = own_start(sides)
    for row in range(rows):
        current = whole(own[0][row], got[0][start + row])
        before = whole(own[1][row], got[1][start + row])
        place(row, first, brick_y, current, before, cells[start + row], 1.0)
        for position in range(sides):
            same, cross = borders[2 * position : 2 * position + 2]
            above = column % 2 == position
            at = pl.multiple_of(jnp.where(above, first + brick_y, 0), EDGE)
            inside = jnp.where(column == jnp.where(above, last_column, 0), 0.0, 1.0) if sides == 2 else 1.0
            current, before, cell = [whole(same[array, row].astype(F32), cross[array, row].astype(F32)) for array in range(3)]
            place(row, at, EDGE, current, before, cell.astype(jnp.int32), inside)


def step_body(sides, last, p_ref, q_ref, ratio, bend, mate, far, *outs):
    padded = outs[-1]
    place = slot()
    rows, length, depth = p_ref.shape
    lane = lax.broadcasted_iota(jnp.int32, (length, depth), 1)
    padded[0:PAD, :] = jnp.zeros((PAD, depth), F32)
    padded[PAD + length :, :] = jnp.zeros((PAD, depth), F32)

    def line(index):
        if 0 <= index < rows:
            return p_ref[index]
        if index < 0:
            return jnp.where(place == 0, far[index + rows].astype(F32), mate[index + rows])
        return jnp.where(place == 0, mate[index - rows], far[index - rows].astype(F32))

    for row in range(rows):
        center = p_ref[row]
        padded[PAD : PAD + length, :] = center
        total = (3.0 * stencil_taps[0]) * center
        for offset in range(1, REACH + 1):
            low, high = PAD - offset, PAD + offset
            pair = padded[low : low + length, :] + padded[high : high + length, :]
            pair = pair + (line(row - offset) + line(row + offset))
            pair = pair + jnp.where(lane >= offset, pltpu.roll(center, offset, 1), 0.0)
            pair = pair + jnp.where(
                lane < depth - offset, pltpu.roll(center, depth - offset, 1), 0.0
            )
            total = total + stencil_taps[offset] * pair
        change = center - q_ref[row]
        value = (center + change) + ratio[row] * total + bend[row] * change * change
        if last:
            new_ref, prior, prior_mate = outs[:3]
            brick_y = new_ref.shape[1]
            first = own_start(sides)
            padded[PAD : PAD + length, :] = value
            new_ref[row] = padded[pl.ds(first + PAD, brick_y), :]
            prior[row] = p_ref[row, pl.ds(first, brick_y), :]
            prior_mate[row] = mate[row, pl.ds(first, brick_y), :]
        else:
            outs[0][row] = value
            outs[1][row] = value.astype(BF16)


def transformed(sources, first, twiddle_x, table_z, table_y, lines, grid):
    column = lax.axis_index("gy")
    brick_y = lines.shape[0] // 4
    modes_y = grid.shape[0]
    width = table_z.shape[1]
    half = width // 2
    for field, rows in enumerate(sources):
        for row, load in enumerate(rows):
            high, low = high_low(load())
            modes = jnp.dot(high, table_z[...], preferred_element_type=F32)
            modes = modes + jnp.dot(low, table_z[...], preferred_element_type=F32)
            back = turned(modes, half, 1.0)
            high, low = high_low(modes)
            back_high, back_low = high_low(back)
            lanes = slice((field * len(rows) + row) * width, (field * len(rows) + row + 1) * width)
            for index, part in enumerate((high, back_high, low, back_low)):
                lines[index * brick_y : (index + 1) * brick_y, lanes] = part
    grid[...] = jnp.dot(table_y[column], lines[...], preferred_element_type=F32)

    def at_mode(field, modes_x):
        count = len(sources[field])
        values = [
            grid[:, (field * count + row) * width : (field * count + row + 1) * width] for row in range(count)
        ]
        backs = [turned(value, half, 1.0) for value in values]

        def summed(mode):
            total = jnp.zeros((modes_y, width), F32)
            for row in range(count):
                at = ((first + row) * modes_x + mode) * 2
                total = total + twiddle_x[at] * values[row] + twiddle_x[at + 1] * backs[row]
            return total

        return summed

    return at_mode


def materials_body(*refs):
    sources, cells, keep, lines, grid = refs[:5], refs[5], refs[6], refs[7], refs[8]
    targets, semaphores = refs[9:14], refs[14]
    copies = [
        pltpu.make_async_copy(source, target, semaphores.at[index])
        for index, (source, target) in enumerate(zip(sources, targets))
    ]
    for copy in copies:
        copy.start()
    for copy in copies:
        copy.wait()
    twiddle_x, stiffness, density, table_z, table_y = targets
    half_x = keep.shape[1]
    entries = stiffness.shape[0]
    rows = cells.shape[0]
    sources = []
    for table in (stiffness, density):
        center = middle(table)
        sources.append([
            lambda row=row, table=table, center=center: looked_up(cells[row], lambda e: table[e] - center, entries)
            for row in range(rows)
        ])
    at_mode = transformed(sources, lax.axis_index("gx") * rows, twiddle_x, table_z, table_y, lines, grid)
    core = lax.axis_index("gz")
    for field in range(2):
        summed = at_mode(field, 2 * half_x)

        @pl.loop(0, half_x)
        def _(mode):
            keep[field, mode] = summed(core * half_x + mode)


def prior_body(sides, twiddle_x, own, mate, table_z, table_y, keep, lines, grid):
    half_x = keep.shape[0]
    rows = own.shape[0]
    place = slot()
    inner = pl.ds(own_start(sides), lines.shape[0] // 4)
    sources = [
        (lambda row=row: jnp.where(place == 0, own[row, inner, :], mate[row, inner, :])) for row in range(rows)
    ] + [(lambda row=row: jnp.where(place == 0, mate[row, inner, :], own[row, inner, :])) for row in range(rows)]
    at_mode = transformed([sources], lax.axis_index("gx") * (2 * rows), twiddle_x, table_z, table_y, lines, grid)
    core = lax.axis_index("gz")
    summed = at_mode(0, 2 * half_x)

    @pl.loop(0, half_x)
    def _(mode):
        keep[mode] = summed(core * half_x + mode)


def wave_body(twiddle_x, own, prior, early, table_z, table_y, keep, send, lines, grid):
    half_x = keep.shape[1]
    rows = own.shape[0]
    first = (lax.axis_index("gx") * 2 + slot()) * rows
    sources = [(lambda row=row: own[row]) for row in range(rows)]
    at_mode = transformed([sources], first, twiddle_x, table_z, table_y, lines, grid)
    core = lax.axis_index("gz")
    summed = at_mode(0, 2 * half_x)
    keep[1] = prior[...]
    keep[2:4] = early[...]

    @pl.loop(0, half_x)
    def _(mode):
        keep[0, mode] = summed(core * half_x + mode)
        send[0, mode] = summed((1 - core) * half_x + mode).astype(BF16)


def prepare_body(
    stiffness, density, mode_ref, lift_ref, bias_ref, local_ref, spread_ref, place_ref, owner_ref, turn_ref,
    wide_ref, mixing, pointwise, lift_table, offset,
):
    block = lax.axis_index("gx") * 2 + lax.axis_index("gz")
    half = place_ref.shape[1]
    channels = lift_ref.shape[1]
    spread = owner_ref[...]

    def dot(a, b, dims=((1,), (0,))):
        return lax.dot_general(a, b, (dims, ((), ())), precision=HIGHEST, preferred_element_type=F32)

    across = ((1,), (1,))
    lifted = dot(dot(spread_ref[:, :channels], lift_ref[...], across), place_ref[...])
    lifted = lifted * spread_ref[:, channels : channels + half]
    real = dot(dot(spread, mode_ref[0], across), lifted)
    imag = dot(dot(spread, mode_ref[1], across), lifted)
    cosine = turn_ref[block, 0]
    sine = turn_ref[block, 1]
    coupled = jnp.concatenate([cosine * real - sine * imag, -(cosine * imag + sine * real)], axis=1)
    mixing[...] = coupled.astype(BF16)
    constant = dot(spread, mode_ref[0, 0:channels, :], across)
    bias = bias_ref[...] + middle(stiffness) * lift_ref[2:3, :] + middle(density) * lift_ref[3:4, :]
    offset[...] = jnp.sum(constant * bias, axis=1, keepdims=True)
    height = spread.shape[0]
    widest = wide_ref[0:channels, :]
    repeated = dot(dot(spread, local_ref[...].astype(F32), across), widest)
    pointwise[...] = (repeated * wide_ref[channels : channels + height, :]).astype(BF16)
    padded = wide_ref[channels + height :, 0:channels]
    lift_table[:, 0:FIELDS] = dot(padded, lift_ref[...], across)
    lift_table[:, FIELDS : FIELDS + 1] = dot(padded, bias_ref[...], across)
    lift_table[:, FIELDS + 1 :] = jnp.zeros_like(lift_table[:, FIELDS + 1 :])


def pointwise_body(stiffness, density, p_ref, q_ref, p_mate, q_mate, cells, lift_ref, left, offset, out, right):
    rows, group, depth = p_ref.shape
    padded_channels = lift_ref.shape[0]
    height = rows * padded_channels
    entries = stiffness.shape[0]
    core = lax.axis_index("gz")
    own = slot() == core

    @pl.when(pl.program_id(0) == 0)
    def _():
        right[...] = jnp.zeros_like(right)

    weights = [lift_ref[:, index : index + 1] for index in range(FIELDS + 1)]
    values = []
    for row in range(rows):
        cell = cells[core * rows + row]
        values.append((
            jnp.where(own, p_ref[row], p_mate[row]),
            jnp.where(own, q_ref[row], q_mate[row]),
            looked_up(cell, lambda e: stiffness[e], entries),
            looked_up(cell, lambda e: density[e], entries),
        ))
    for y in range(group):
        lifted = []
        for row in range(rows):
            total = jnp.broadcast_to(weights[FIELDS], (padded_channels, depth))
            for value, weight in zip(values[row], weights):
                total = total + value[y : y + 1, :] * weight
            lifted.append(total)
        right[y, 0:height, :] = jnp.concatenate(lifted, axis=0).astype(BF16)
        out[:, y, :] = jnp.dot(left[...], right[y], preferred_element_type=F32) + offset[...]


def output_body(
    mine, other, local_low, local_high, left, table_y, table_z, wave_ref, wave_other,
    features, wave_out, modes, right, sums,
):
    step = pl.program_id(0)
    core, column = lax.axis_index("gz"), lax.axis_index("gy")
    half_x, modes_y, width = mine.shape[1:]
    modes_x = 2 * half_x
    half = width // 2
    rows, channels, group, depth = features.shape
    coupled = FIELDS * modes_x

    @pl.when(step == 0)
    def _():
        chunk = 4
        left_y = table_y[column]
        for field in range(FIELDS):
            for start in range(0, modes_x, chunk):
                parts = [[], []]
                for mode in range(start, start + chunk):
                    at = (field, mode % half_x)
                    value = jnp.where(core == mode // half_x, mine[at], other[at].astype(F32))
                    parts[0].append(value.astype(BF16))
                    parts[1].append(turned(value, half, -1.0).astype(BF16))
                stacked = jnp.concatenate([jnp.concatenate(part, axis=1) for part in parts], axis=0)
                result = jnp.dot(left_y, stacked, preferred_element_type=F32)
                for mode in range(start, start + chunk):
                    lanes = slice((mode - start) * width, (mode - start + 1) * width)
                    modes[:, mode * FIELDS + field, :] = result[:, lanes]
        z_half = depth // 2
        place = slot()
        for row in range(rows):
            for ref, start in ((wave_ref, place * rows), (wave_other, (1 - place) * rows)):
                wave_out[start + row] = jnp.where(core == 0, ref[row, :, :z_half], ref[row, :, z_half:])

    base = pl.multiple_of(step * group, group)
    lines = modes[pl.ds(base, group)].reshape(group * coupled, width).astype(BF16)
    waves = jnp.dot(lines, table_z[...], preferred_element_type=F32).astype(BF16)
    for y in range(group):
        lines = slice(y * coupled, (y + 1) * coupled)
        right[y, 0:coupled, :] = waves[lines, :depth]
        right[y, coupled:, :] = waves[lines, depth:]
        sums[:, y, :] = jnp.dot(left[...], right[y], preferred_element_type=F32)
    for row in range(rows):
        for channel in range(channels):
            at = row * channels + channel
            total = sums[at] + jnp.where(step < pl.num_programs(0) // 2, local_low[at], local_high[at])
            inner = math.sqrt(2.0 / math.pi) * (total + 0.044715 * (total * total * total))
            total = (0.5 * total) * (1.0 + jnp.tanh(inner))
            features[row, channel] = total.astype(BF16)


def xor_pairs(count, distance):
    return [(index, index ^ distance) for index in range(count)]


def odd_pairs(count):
    pairs = [(index, index + 1) for index in range(1, count - 1, 2)]
    return pairs + [(target, source) for source, target in pairs]


def like_core_pairs(count):
    pairs = [(2 * chip + 1 - chip % 2, 2 * chip + 3 - chip % 2) for chip in range(count - 1)]
    return pairs + [(target, source) for source, target in pairs]


def per_device(
    pressure,
    previous,
    material,
    stiffness,
    density,
    nonlinear,
    lift_weight,
    lift_bias,
    mode_weight,
    local_weight,
):
    brick_x, brick_y, brick_z = pressure.shape
    cycle_count = lax.axis_size("gx")
    column_count = lax.axis_size("gy")
    core_count = lax.axis_size("gz")
    total_x = brick_x * cycle_count
    total_y = brick_y * column_count
    total_z = brick_z * core_count
    modes_x = total_x // 4
    modes_y = total_y // 4
    modes_z = total_z // 4
    width = 2 * modes_z
    channels = lift_bias.shape[0]
    rows = brick_x // core_count
    assert core_count == 2 and rows >= REACH
    blocks = cycle_count * core_count
    padded_channels = -(-channels // 8) * 8
    height = rows * channels
    coupled = FIELDS * modes_x
    right_depth = -(-rows * padded_channels // 128) * 128
    sides = 2 if column_count > 2 else 1
    assert brick_y >= EDGE

    kept_first = kept_modes(total_x, modes_x)
    kept_second = kept_modes(total_y, modes_y)
    kept_third = np.arange(modes_z)
    cz, sz = cos_sin(np.arange(total_z), kept_third, total_z)
    forward_z = np.concatenate([cz, -sz], 1)
    weight = np.where(kept_third == 0, 1.0, 2.0) / (total_x * total_y * total_z)
    wc, ws = [rounded((t.astype(np.float32) * weight).T.astype(np.float32)) for t in (cz, sz)]
    inverse_z = np.concatenate(
        [np.concatenate([wc, ws], 1), np.concatenate([-ws.astype(np.float32), wc.astype(np.float32)], 1)], 0
    )
    inverse_z = rounded(inverse_z)
    cy, sy = cos_sin(kept_second, np.arange(total_y), total_y)
    cy3, sy3 = [t.reshape(modes_y, column_count, brick_y).transpose(1, 0, 2) for t in (cy, sy)]
    forward_y = np.concatenate([cy3, sy3, cy3, sy3], 2)
    cy3, sy3 = [t.transpose(0, 2, 1) for t in (cy3, sy3)]
    inverse_y = np.concatenate([cy3, sy3], 2)
    cx, sx = [t.astype(np.float32) for t in cos_sin(np.arange(total_x), kept_first, total_x)]
    twiddle_x = np.stack([cx, sx], -1).reshape(-1)
    owner = np.tile(np.eye(channels, dtype=np.float32), (rows, 1))
    turn = np.zeros((blocks, 2, height, coupled), np.float32)
    for source, table in enumerate((cx, sx)):
        turn[:, source] = np.repeat(
            np.repeat(table.reshape(blocks, rows, modes_x), channels, 1), FIELDS, 2
        )
    padded_eye = np.eye(channels, padded_channels, dtype=np.float32)
    wide = np.zeros((channels + height + padded_channels, right_depth), np.float32)
    wide[:channels, : rows * padded_channels] = np.tile(padded_eye, (1, rows))
    wide[channels : channels + height, : rows * padded_channels] = np.kron(
        np.eye(rows), np.ones((channels, padded_channels))
    )
    wide[channels + height :, :channels] = padded_eye.T
    spread = np.tile(np.eye(channels, dtype=np.float32), (modes_x, 1))
    same = np.repeat(
        np.repeat(np.eye(modes_x, dtype=np.float32), channels, 0), FIELDS, 1
    )
    spread = np.concatenate([spread, same], 1)
    place = np.tile(np.eye(FIELDS, dtype=np.float32), (1, modes_x))

    def shape(*dims, dtype=F32):
        return jax.ShapeDtypeStruct(dims, dtype)

    cells_count = rows * brick_y * total_z
    field = shape(rows, brick_y, total_z)
    longer = brick_y + sides * EDGE
    wider = shape(rows, longer, total_z)
    border = shape(3, rows, EDGE, brick_z, dtype=BF16)

    swap_core = xor_pairs(core_count, 1)
    got = [lax.ppermute(array, "gz", swap_core) for array in (pressure, previous, material)]
    here = lambda *arrays: [pltpu.with_memory_space_constraint(array, pltpu.HBM) for array in arrays]
    sends = call(
        lambda *refs: pack_body(sides, *refs), [border] * (2 * sides), [HBM] * 3,
        [pltpu.VMEM((4 * sides, rows, EDGE, brick_z), F32), pltpu.VMEM((2 * sides, rows, EDGE, brick_z), jnp.int32),
         pltpu.SemaphoreType.DMA((6 * sides,))],
        moved=cells_count * 8,
    )(*here(pressure, previous, material))
    borders = []
    for position in range(sides):
        pairs = (xor_pairs if position == 0 else lambda count, _: odd_pairs(count))(column_count, 1)
        crossed = [(source * 2 + core, target * 2 + 1 - core) for source, target in pairs for core in range(2)]
        borders.append(lax.ppermute(sends[2 * position], "gy", pairs))
        borders.append(lax.ppermute(sends[2 * position + 1], ("gy", "gz"), crossed))
    sending = shape(rows, longer, total_z, dtype=BF16)
    current, before, ratio, bend, sent, cells = call(
        lambda *refs: assemble_body(sides, column_count - 1, *refs),
        [wider] * 4 + [sending, shape(brick_x, brick_y, total_z, dtype=jnp.int32)],
        [HBM] * 6 + [VMEM] * (3 + 2 * sides),
        [pltpu.SMEM(stiffness.shape, F32)] * 3 + [pltpu.VMEM((rows, brick_y, brick_z), F32)] * 2
        + [pltpu.VMEM((brick_x, brick_y, brick_z), jnp.int32), pltpu.SemaphoreType.DMA((6,))], moved=cells_count * 36
    )(*here(stiffness, density, nonlinear, pressure, previous, material), *got, *borders)

    mixing, pointwise, lift_table, offset = call(
        prepare_body,
        [shape(height, 2 * coupled, dtype=BF16), shape(height, right_depth, dtype=BF16),
         shape(padded_channels, 8), shape(height, 1)],
        [SMEM] * 2 + [VMEM] * 9, flops=2_000_000_000, moved=4_000_000,
    )(
        stiffness, density, mode_weight.reshape(2, modes_x * channels, channels), lift_weight,
        lift_bias.reshape(1, channels), local_weight, spread, place, owner, turn, wide,
    )

    part = lambda fields, dtype: shape(fields, modes_x // 2, modes_y, width, dtype=dtype)

    def spectrum(body, outs, inputs, lines, specs=None, scratch=()):
        return call(
            body, outs, specs or [SMEM] + [VMEM] * (inputs + 2),
            [pltpu.VMEM((4 * brick_y, lines * width), BF16), pltpu.VMEM((modes_y, lines * width), F32), *scratch],
            flops=cells_count * 256 * lines, moved=cells_count * 2 * lines,
        )

    stages = [(axis, count, 2**bit) for axis, count in (("gy", column_count), ("gx", cycle_count))
              for bit in range((count - 1).bit_length())]
    swap = lambda value: lax.ppermute(value, "gz", swap_core)

    def exchange(value, axis, count, distance):
        return lax.ppermute(value.astype(BF16), axis, xor_pairs(count, distance))

    tables = (twiddle_x, stiffness, density, forward_z, forward_y)
    early = spectrum(
        materials_body, part(2, F32), 1, 2 * brick_x, [HBM] * 5 + [VMEM],
        [(pltpu.SMEM if table.ndim == 1 else pltpu.VMEM)(table.shape, table.dtype) for table in tables]
        + [pltpu.SemaphoreType.DMA((5,))],
    )(*here(*[jnp.asarray(table) for table in tables]), cells)

    for repeat in range(STEPS):
        last = repeat == STEPS - 1
        far = lax.ppermute(sent, ("gx", "gz"), like_core_pairs(cycle_count))
        mate = swap(current)
        if repeat == 0:
            far, early = lax.optimization_barrier((far, early))
        if repeat == 1:
            far, mixing, pointwise, lift_table, offset = lax.optimization_barrier(
                (far, mixing, pointwise, lift_table, offset)
            )
        if last:
            prior = spectrum(lambda *refs: prior_body(sides, *refs), shape(modes_x // 2, modes_y, width), 2, brick_x)(
                twiddle_x, current, mate, forward_z, forward_y
            )
            far, prior = lax.optimization_barrier((far, prior))
        body = lambda *refs, last=last: step_body(sides, last, *refs)
        new, *others = call(
            body, [field] * 3 if last else [wider, sending], [VMEM] * 6,
            [pltpu.VMEM((longer + 2 * PAD, total_z), F32)], flops=cells_count * 60, moved=cells_count * 28,
        )(current, before, ratio, bend, mate, far)
        if last:
            before, prior_mate = others
        else:
            before, sent = current, others[0]
        current = new

    total, sent = spectrum(wave_body, [part(FIELDS, F32), part(1, BF16)], 3, rows)(
        twiddle_x, current, prior, early, forward_z, forward_y
    )
    total = total + jnp.pad(swap(sent).astype(F32), ((0, FIELDS - 1), (0, 0), (0, 0), (0, 0)))
    wave_other = swap(current)
    group = 8
    steps = brick_y // group
    whole = lambda array: pl.BlockSpec(array.shape, lambda i: (0,) * len(array.shape))

    def pointwise_part(start):
        slab = lambda count: pl.BlockSpec((count, group, total_z), lambda i: (0, i + start, 0))
        return pl.pallas_call(
            pointwise_body,
            grid=(steps // 2,),
            out_shape=shape(height, brick_y // 2, total_z),
            in_specs=[SMEM] * 2 + [slab(rows)] * 4 + [slab(brick_x), whole(lift_table), whole(pointwise), whole(offset)],
            out_specs=pl.BlockSpec((height, group, total_z), lambda i: (0, i, 0)),
            scratch_shapes=[pltpu.VMEM((group, right_depth, total_z), BF16)],
            compiler_params=pltpu.CompilerParams(vmem_limit_bytes=16 * 1024 * 1024),
            cost_estimate=pl.CostEstimate(flops=cells_count * 20000, bytes_accessed=cells_count * 50, transcendentals=0),
        )(stiffness, density, current, before, wave_other, prior_mate, cells, lift_table, pointwise, offset)

    for index, stage in enumerate(stages):
        arrived = exchange(total, *stage)
        if index == len(stages) - 2:
            local_low = pointwise_part(0)
            arrived, local_low = lax.optimization_barrier((arrived, local_low))
        if index == len(stages) - 1:
            local_high = pointwise_part(steps // 2)
            arrived, local_high = lax.optimization_barrier((arrived, local_high))
        total = total + arrived.astype(F32)
    other = swap(total.astype(BF16))
    scoped = 12 * 2**20 + 4 * (6 * 2 * modes_x * modes_y * width + brick_y * coupled * width + 6 * group * coupled * total_z)
    features, wave = pl.pallas_call(
        output_body,
        grid=(steps,),
        out_shape=[shape(rows, channels, brick_y, total_z, dtype=BF16), shape(*pressure.shape)],
        in_specs=[whole(part(FIELDS, F32)), whole(part(FIELDS, BF16)),
           pl.BlockSpec((height, group, total_z), lambda i: (0, jnp.minimum(i, steps // 2 - 1), 0)),
           pl.BlockSpec((height, group, total_z), lambda i: (0, jnp.maximum(i - steps // 2, 0), 0)),
           whole(mixing), whole(inverse_y), whole(inverse_z),
                  whole(field), whole(field)],
        out_specs=[pl.BlockSpec((rows, channels, group, total_z), lambda i: (0, 0, i, 0)), whole(pressure)],
        scratch_shapes=[
            pltpu.VMEM((brick_y, coupled, width), F32),
            pltpu.VMEM((group, 2 * coupled, total_z), BF16),
            pltpu.VMEM((height, group, total_z), F32),
        ],
        compiler_params=pltpu.CompilerParams(vmem_limit_bytes=scoped),
        cost_estimate=pl.CostEstimate(flops=cells_count * 2000, bytes_accessed=cells_count * 60, transcendentals=cells_count * 20),
    )(total, other, local_low, local_high, mixing, inverse_y, inverse_z, current, wave_other)
    features = features.transpose(0, 2, 1, 3)
    return (wave, features)


def solution(mesh):
    placed = (
        P(("grp", "gx"), "gy", "gz"),
        P(("grp", "gx"), "gy", "gz"),
        P(("grp", "gx"), "gy", "gz"),
        P(),
        P(),
        P(),
        P(),
        P(),
        P(),
        P(),
    )
    return jax.shard_map(
        per_device,
        mesh=mesh,
        in_specs=placed,
        out_specs=(P(("grp", "gx"), "gy", "gz"), P(("grp", "gx", "gz"), "gy", None, None)),
        check_vma=False,
    )
```

```python
import math

import numpy as np
import jax
import jax.numpy as jnp
from jax import lax
from jax.experimental import pallas as pl
from jax.experimental.pallas import tpu as pltpu
from jax.sharding import PartitionSpec as P
import ml_dtypes

STEPS = 4
FIELDS = 4
REACH = 4
EDGE = 8
stencil_taps = (-205.0 / 72.0, 8.0 / 5.0, -1.0 / 5.0, 8.0 / 315.0, -1.0 / 560.0)
F32 = jnp.float32
BF16 = jnp.bfloat16
HIGHEST = lax.Precision.HIGHEST

VMEM = pl.BlockSpec(memory_space=pltpu.VMEM)
SMEM = pl.BlockSpec(memory_space=pltpu.SMEM)
HBM = pl.BlockSpec(memory_space=pltpu.HBM)


def rounded(table):
    return table.astype(ml_dtypes.bfloat16)


def kept_modes(length, mode_count):
    position = np.arange(mode_count)
    return np.where(position < mode_count // 2, position, length - mode_count + position)


def cos_sin(source, target, length):
    product = (source[:, None] * target[None, :]) % length
    phases = np.float32(2.0 * math.pi / length) * product.astype(np.float32)
    return rounded(np.cos(phases)), rounded(np.sin(phases))


def call(body, outs, in_specs, scratch=(), flops=0, moved=0):
    return pl.pallas_call(
        body,
        out_shape=outs,
        in_specs=in_specs,
        out_specs=jax.tree.map(lambda _: VMEM, outs),
        scratch_shapes=list(scratch),
        compiler_params=pltpu.CompilerParams(vmem_limit_bytes=16 * 1024 * 1024),
        cost_estimate=pl.CostEstimate(flops=flops, bytes_accessed=moved, transcendentals=0),
    )


def high_low(value):
    high = value.astype(BF16)
    return high, (value - high.astype(F32)).astype(BF16)


def turned(value, half, sign):
    lane = lax.broadcasted_iota(jnp.int32, value.shape, value.ndim - 1)
    swapped = pltpu.roll(value, half, value.ndim - 1)
    return jnp.where(lane < half, sign * swapped, -sign * swapped)


def looked_up(material, table, entries):
    result = jnp.full(material.shape, table(0), F32)
    for entry in range(1, entries):
        result = jnp.where(material == entry, table(entry), result)
    return result


def middle(table):
    total = table[0]
    for entry in range(1, table.shape[0]):
        total = total + table[entry]
    return total * (1.0 / table.shape[0])


def edges(value_of, outs, row_parity, brick_y):
    for position, out in enumerate(outs):
        upper = row_parity == position
        out[...] = jnp.where(upper, value_of(brick_y - EDGE, brick_y), value_of(0, EDGE))


def slot():
    return (lax.axis_index("gz") + lax.axis_index("gx")) % 2


def assemble_body(count, *refs):
    tables_in, own_in, got = refs[:3], refs[3:6], refs[6:9]
    p_out, q_out, ratio, bend, sent, cells = refs[9:15]
    edge_outs = refs[15 : 15 + count]
    tables, own, semaphores = refs[15 + count : 18 + count], refs[18 + count : 21 + count], refs[21 + count]
    core, column = lax.axis_index("gz"), lax.axis_index("gy")
    rows, brick_y = p_out.shape[:2]
    start = slot() * rows
    sources = [source.at[pl.ds(start, rows)] for source in own_in[:2]] + [own_in[2]]
    copies = [
        pltpu.make_async_copy(source, target, semaphores.at[index])
        for index, (source, target) in enumerate(zip(list(tables_in) + sources, list(tables) + list(own)))
    ]
    for copy in copies:
        copy.start()
    for copy in copies:
        copy.wait()
    stiffness, density, nonlinear = tables
    entries = stiffness.shape[0]

    def whole(mine, other):
        return jnp.concatenate(
            [jnp.where(core == 0, mine, other), jnp.where(core == 0, other, mine)], axis=-1
        )

    for row in range(cells.shape[0]):
        cells[row] = whole(own[2][row], got[2][row])
    for row in range(rows):
        value = whole(own[0][row], got[0][start + row])
        p_out[row] = value
        sent[row] = value.astype(BF16)
        q_out[row] = whole(own[1][row], got[1][start + row])
        cell = cells[start + row]
        ratio[row] = looked_up(cell, lambda e: stiffness[e] / density[e], entries)
        bend[row] = looked_up(cell, lambda e: nonlinear[e], entries)
    edges(lambda a, b: p_out[:, a:b, :], edge_outs, column % 2, brick_y)


def step_body(two_sided, last, p_ref, q_ref, ratio, bend, mate, far, *rest):
    count = 2 if two_sided else 1
    halos = rest[:count]
    new_ref = rest[count]
    sent = None if last else rest[count + 1]
    edge_outs = rest[count + 2 : -1]
    padded = rest[-1]
    place = slot()
    parity = lax.axis_index("gy") % 2
    rows, brick_y, depth = p_ref.shape
    lane = lax.broadcasted_iota(jnp.int32, (brick_y, depth), 1)
    zero_edge = jnp.zeros((EDGE, depth), F32)

    cycle = lax.axis_index("gx")
    outside = cycle == jnp.where(place == 0, 0, lax.axis_size("gx") - 1)

    def line(index):
        if 0 <= index < rows:
            return p_ref[index]
        at = index % rows
        beyond = jnp.where(outside, 0.0, far[at].astype(F32))
        return jnp.where(place == (0 if index < 0 else 1), beyond, mate[at])

    for row in range(rows):
        first = halos[0][row]
        second = halos[1][row] if two_sided else zero_edge
        center = p_ref[row]
        padded[0:EDGE, :] = jnp.where(parity == 0, second, first)
        padded[EDGE : EDGE + brick_y, :] = center
        padded[EDGE + brick_y :, :] = jnp.where(parity == 0, first, second)
        total = (3.0 * stencil_taps[0]) * center
        for offset in range(1, REACH + 1):
            low, high = EDGE - offset, EDGE + offset
            pair = padded[low : low + brick_y, :] + padded[high : high + brick_y, :]
            pair = pair + (line(row - offset) + line(row + offset))
            pair = pair + jnp.where(lane >= offset, pltpu.roll(center, offset, 1), 0.0)
            pair = pair + jnp.where(
                lane < depth - offset, pltpu.roll(center, depth - offset, 1), 0.0
            )
            total = total + stencil_taps[offset] * pair
        change = center - q_ref[row]
        value = (center + change) + ratio[row] * total + bend[row] * change * change
        new_ref[row] = value
        if not last:
            sent[row] = value.astype(BF16)
    if not last:
        edges(lambda a, b: new_ref[:, a:b, :], edge_outs, parity, brick_y)


def transformed(sources, first, twiddle_x, table_z, table_y, lines, grid):
    column = lax.axis_index("gy")
    brick_y = lines.shape[0] // 4
    modes_y = grid.shape[0]
    width = table_z.shape[1]
    half = width // 2
    for field, rows in enumerate(sources):
        for row, load in enumerate(rows):
            high, low = high_low(load())
            modes = jnp.dot(high, table_z[...], preferred_element_type=F32)
            modes = modes + jnp.dot(low, table_z[...], preferred_element_type=F32)
            back = turned(modes, half, 1.0)
            high, low = high_low(modes)
            back_high, back_low = high_low(back)
            lanes = slice((field * len(rows) + row) * width, (field * len(rows) + row + 1) * width)
            for index, part in enumerate((high, back_high, low, back_low)):
                lines[index * brick_y : (index + 1) * brick_y, lanes] = part
    grid[...] = jnp.dot(table_y[column], lines[...], preferred_element_type=F32)

    def at_mode(field, modes_x):
        count = len(sources[field])
        values = [
            grid[:, (field * count + row) * width : (field * count + row + 1) * width] for row in range(count)
        ]
        backs = [turned(value, half, 1.0) for value in values]

        def summed(mode):
            total = jnp.zeros((modes_y, width), F32)
            for row in range(count):
                at = ((first + row) * modes_x + mode) * 2
                total = total + twiddle_x[at] * values[row] + twiddle_x[at + 1] * backs[row]
            return total

        return summed

    return at_mode


def materials_body(*refs):
    sources, cells, keep, lines, grid = refs[:5], refs[5], refs[6], refs[7], refs[8]
    targets, semaphores = refs[9:14], refs[14]
    copies = [
        pltpu.make_async_copy(source, target, semaphores.at[index])
        for index, (source, target) in enumerate(zip(sources, targets))
    ]
    for copy in copies:
        copy.start()
    for copy in copies:
        copy.wait()
    twiddle_x, stiffness, density, table_z, table_y = targets
    half_x = keep.shape[1]
    entries = stiffness.shape[0]
    rows = cells.shape[0]
    sources = []
    for table in (stiffness, density):
        center = middle(table)
        sources.append([
            lambda row=row, table=table, center=center: looked_up(cells[row], lambda e: table[e] - center, entries)
            for row in range(rows)
        ])
    at_mode = transformed(sources, lax.axis_index("gx") * rows, twiddle_x, table_z, table_y, lines, grid)
    core = lax.axis_index("gz")
    for field in range(2):
        summed = at_mode(field, 2 * half_x)

        @pl.loop(0, half_x)
        def _(mode):
            keep[field, mode] = summed(core * half_x + mode)


def prior_body(twiddle_x, own, mate, table_z, table_y, keep, lines, grid):
    half_x = keep.shape[0]
    rows = own.shape[0]
    place = slot()
    sources = [
        (lambda row=row: jnp.where(place == 0, own[row], mate[row])) for row in range(rows)
    ] + [(lambda row=row: jnp.where(place == 0, mate[row], own[row])) for row in range(rows)]
    at_mode = transformed([sources], lax.axis_index("gx") * (2 * rows), twiddle_x, table_z, table_y, lines, grid)
    core = lax.axis_index("gz")
    summed = at_mode(0, 2 * half_x)

    @pl.loop(0, half_x)
    def _(mode):
        keep[mode] = summed(core * half_x + mode)


def wave_body(twiddle_x, own, prior, early, table_z, table_y, keep, send, lines, grid):
    half_x = keep.shape[1]
    rows = own.shape[0]
    first = (lax.axis_index("gx") * 2 + slot()) * rows
    sources = [(lambda row=row: own[row]) for row in range(rows)]
    at_mode = transformed([sources], first, twiddle_x, table_z, table_y, lines, grid)
    core = lax.axis_index("gz")
    summed = at_mode(0, 2 * half_x)
    keep[1] = prior[...]
    keep[2:4] = early[...]

    @pl.loop(0, half_x)
    def _(mode):
        keep[0, mode] = summed(core * half_x + mode)
        send[0, mode] = summed((1 - core) * half_x + mode).astype(BF16)


def prepare_body(
    stiffness, density, mode_ref, lift_ref, bias_ref, local_ref, spread_ref, place_ref, owner_ref, turn_ref,
    wide_ref, mixing, pointwise, lift_table, offset,
):
    block = lax.axis_index("gx") * 2 + lax.axis_index("gz")
    half = place_ref.shape[1]
    channels = lift_ref.shape[1]
    spread = owner_ref[...]

    def dot(a, b, dims=((1,), (0,))):
        return lax.dot_general(a, b, (dims, ((), ())), precision=HIGHEST, preferred_element_type=F32)

    across = ((1,), (1,))
    lifted = dot(dot(spread_ref[:, :channels], lift_ref[...], across), place_ref[...])
    lifted = lifted * spread_ref[:, channels : channels + half]
    real = dot(dot(spread, mode_ref[0], across), lifted)
    imag = dot(dot(spread, mode_ref[1], across), lifted)
    cosine = turn_ref[block, 0]
    sine = turn_ref[block, 1]
    coupled = jnp.concatenate([cosine * real - sine * imag, -(cosine * imag + sine * real)], axis=1)
    mixing[...] = coupled.astype(BF16)
    constant = dot(spread, mode_ref[0, 0:channels, :], across)
    bias = bias_ref[...] + middle(stiffness) * lift_ref[2:3, :] + middle(density) * lift_ref[3:4, :]
    offset[...] = jnp.sum(constant * bias, axis=1, keepdims=True)
    height = spread.shape[0]
    widest = wide_ref[0:channels, :]
    repeated = dot(dot(spread, local_ref[...].astype(F32), across), widest)
    pointwise[...] = (repeated * wide_ref[channels : channels + height, :]).astype(BF16)
    padded = wide_ref[channels + height :, 0:channels]
    lift_table[:, 0:FIELDS] = dot(padded, lift_ref[...], across)
    lift_table[:, FIELDS : FIELDS + 1] = dot(padded, bias_ref[...], across)
    lift_table[:, FIELDS + 1 :] = jnp.zeros_like(lift_table[:, FIELDS + 1 :])


def pointwise_body(stiffness, density, p_ref, q_ref, p_mate, q_mate, cells, lift_ref, left, offset, out, right):
    rows, group, depth = p_ref.shape
    padded_channels = lift_ref.shape[0]
    height = rows * padded_channels
    entries = stiffness.shape[0]
    core = lax.axis_index("gz")
    own = slot() == core

    @pl.when(pl.program_id(0) == 0)
    def _():
        right[...] = jnp.zeros_like(right)

    weights = [lift_ref[:, index : index + 1] for index in range(FIELDS + 1)]
    values = []
    for row in range(rows):
        cell = cells[core * rows + row]
        values.append((
            jnp.where(own, p_ref[row], p_mate[row]),
            jnp.where(own, q_ref[row], q_mate[row]),
            looked_up(cell, lambda e: stiffness[e], entries),
            looked_up(cell, lambda e: density[e], entries),
        ))
    for y in range(group):
        lifted = []
        for row in range(rows):
            total = jnp.broadcast_to(weights[FIELDS], (padded_channels, depth))
            for value, weight in zip(values[row], weights):
                total = total + value[y : y + 1, :] * weight
            lifted.append(total)
        right[y, 0:height, :] = jnp.concatenate(lifted, axis=0).astype(BF16)
        out[:, y, :] = jnp.dot(left[...], right[y], preferred_element_type=F32) + offset[...]


def output_body(
    mine, other, local_low, local_high, left, table_y, table_z, wave_ref, wave_other,
    features, wave_out, modes, right, sums,
):
    step = pl.program_id(0)
    core, column = lax.axis_index("gz"), lax.axis_index("gy")
    half_x, modes_y, width = mine.shape[1:]
    modes_x = 2 * half_x
    half = width // 2
    rows, channels, group, depth = features.shape
    coupled = FIELDS * modes_x

    @pl.when(step == 0)
    def _():
        chunk = 4
        left_y = table_y[column]
        for field in range(FIELDS):
            for start in range(0, modes_x, chunk):
                parts = [[], []]
                for mode in range(start, start + chunk):
                    at = (field, mode % half_x)
                    value = jnp.where(core == mode // half_x, mine[at], other[at].astype(F32))
                    parts[0].append(value.astype(BF16))
                    parts[1].append(turned(value, half, -1.0).astype(BF16))
                stacked = jnp.concatenate([jnp.concatenate(part, axis=1) for part in parts], axis=0)
                result = jnp.dot(left_y, stacked, preferred_element_type=F32)
                for mode in range(start, start + chunk):
                    lanes = slice((mode - start) * width, (mode - start + 1) * width)
                    modes[:, mode * FIELDS + field, :] = result[:, lanes]
        z_half = depth // 2
        place = slot()
        for row in range(rows):
            for ref, start in ((wave_ref, place * rows), (wave_other, (1 - place) * rows)):
                wave_out[start + row] = jnp.where(core == 0, ref[row, :, :z_half], ref[row, :, z_half:])

    base = pl.multiple_of(step * group, group)
    lines = modes[pl.ds(base, group)].reshape(group * coupled, width).astype(BF16)
    waves = jnp.dot(lines, table_z[...], preferred_element_type=F32).astype(BF16)
    for y in range(group):
        lines = slice(y * coupled, (y + 1) * coupled)
        right[y, 0:coupled, :] = waves[lines, :depth]
        right[y, coupled:, :] = waves[lines, depth:]
        sums[:, y, :] = jnp.dot(left[...], right[y], preferred_element_type=F32)
    for row in range(rows):
        for channel in range(channels):
            at = row * channels + channel
            total = sums[at] + jnp.where(step < pl.num_programs(0) // 2, local_low[at], local_high[at])
            inner = math.sqrt(2.0 / math.pi) * (total + 0.044715 * (total * total * total))
            total = (0.5 * total) * (1.0 + jnp.tanh(inner))
            features[row, channel] = total.astype(BF16)


def xor_pairs(count, distance):
    return [(index, index ^ distance) for index in range(count)]


def odd_pairs(count):
    pairs = [(index, index + 1) for index in range(1, count - 1, 2)]
    return pairs + [(target, source) for source, target in pairs]


def row_pairs(cycles, columns):
    place = lambda cycle, column, core: (cycle * columns + column) * 2 + core
    pairs = []
    for column in range(columns):
        for cycle in range(cycles - 1):
            one, two = place(cycle, column, 1 - cycle % 2), place(cycle + 1, column, 1 - cycle % 2)
            pairs += [(one, two), (two, one)]
        for cycle, core in ((0, 0), (cycles - 1, 1 - (cycles - 1) % 2)):
            pairs.append((place(cycle, column, core), place(cycle, column ^ 1, core)))
    return pairs


def per_device(
    pressure,
    previous,
    material,
    stiffness,
    density,
    nonlinear,
    lift_weight,
    lift_bias,
    mode_weight,
    local_weight,
):
    brick_x, brick_y, brick_z = pressure.shape
    cycle_count = lax.axis_size("gx")
    column_count = lax.axis_size("gy")
    core_count = lax.axis_size("gz")
    total_x = brick_x * cycle_count
    total_y = brick_y * column_count
    total_z = brick_z * core_count
    modes_x = total_x // 4
    modes_y = total_y // 4
    modes_z = total_z // 4
    width = 2 * modes_z
    channels = lift_bias.shape[0]
    rows = brick_x // core_count
    assert core_count == 2 and rows >= REACH
    blocks = cycle_count * core_count
    padded_channels = -(-channels // 8) * 8
    height = rows * channels
    coupled = FIELDS * modes_x
    right_depth = -(-rows * padded_channels // 128) * 128
    two_sided = column_count > 2

    kept_first = kept_modes(total_x, modes_x)
    kept_second = kept_modes(total_y, modes_y)
    kept_third = np.arange(modes_z)
    cz, sz = cos_sin(np.arange(total_z), kept_third, total_z)
    forward_z = np.concatenate([cz, -sz], 1)
    weight = np.where(kept_third == 0, 1.0, 2.0) / (total_x * total_y * total_z)
    wc, ws = [rounded((t.astype(np.float32) * weight).T.astype(np.float32)) for t in (cz, sz)]
    inverse_z = np.concatenate(
        [np.concatenate([wc, ws], 1), np.concatenate([-ws.astype(np.float32), wc.astype(np.float32)], 1)], 0
    )
    inverse_z = rounded(inverse_z)
    cy, sy = cos_sin(kept_second, np.arange(total_y), total_y)
    cy3, sy3 = [t.reshape(modes_y, column_count, brick_y).transpose(1, 0, 2) for t in (cy, sy)]
    forward_y = np.concatenate([cy3, sy3, cy3, sy3], 2)
    cy3, sy3 = [t.transpose(0, 2, 1) for t in (cy3, sy3)]
    inverse_y = np.concatenate([cy3, sy3], 2)
    cx, sx = [t.astype(np.float32) for t in cos_sin(np.arange(total_x), kept_first, total_x)]
    twiddle_x = np.stack([cx, sx], -1).reshape(-1)
    owner = np.tile(np.eye(channels, dtype=np.float32), (rows, 1))
    turn = np.zeros((blocks, 2, height, coupled), np.float32)
    for source, table in enumerate((cx, sx)):
        turn[:, source] = np.repeat(
            np.repeat(table.reshape(blocks, rows, modes_x), channels, 1), FIELDS, 2
        )
    padded_eye = np.eye(channels, padded_channels, dtype=np.float32)
    wide = np.zeros((channels + height + padded_channels, right_depth), np.float32)
    wide[:channels, : rows * padded_channels] = np.tile(padded_eye, (1, rows))
    wide[channels : channels + height, : rows * padded_channels] = np.kron(
        np.eye(rows), np.ones((channels, padded_channels))
    )
    wide[channels + height :, :channels] = padded_eye.T
    spread = np.tile(np.eye(channels, dtype=np.float32), (modes_x, 1))
    same = np.repeat(
        np.repeat(np.eye(modes_x, dtype=np.float32), channels, 0), FIELDS, 1
    )
    spread = np.concatenate([spread, same], 1)
    place = np.tile(np.eye(FIELDS, dtype=np.float32), (1, modes_x))

    def shape(*dims, dtype=F32):
        return jax.ShapeDtypeStruct(dims, dtype)

    cells_count = rows * brick_y * total_z
    field = shape(rows, brick_y, total_z)
    edge = [shape(rows, EDGE, total_z)] * (2 if two_sided else 1)

    swap_core = xor_pairs(core_count, 1)
    got = [lax.ppermute(array, "gz", swap_core) for array in (pressure, previous, material)]
    sending = shape(rows, brick_y, total_z, dtype=BF16)
    here = lambda *arrays: [pltpu.with_memory_space_constraint(array, pltpu.HBM) for array in arrays]
    current, before, ratio, bend, sent, cells, *edge_values = call(
        lambda *refs: assemble_body(len(edge), *refs),
        [field] * 4 + [sending, shape(brick_x, brick_y, total_z, dtype=jnp.int32)] + edge, [HBM] * 6 + [VMEM] * 3,
        [pltpu.SMEM(stiffness.shape, F32)] * 3 + [pltpu.VMEM((rows, brick_y, brick_z), F32)] * 2
        + [pltpu.VMEM((brick_x, brick_y, brick_z), jnp.int32), pltpu.SemaphoreType.DMA((6,))], moved=cells_count * 36
    )(*here(stiffness, density, nonlinear, pressure, previous, material), *got)

    mixing, pointwise, lift_table, offset = call(
        prepare_body,
        [shape(height, 2 * coupled, dtype=BF16), shape(height, right_depth, dtype=BF16),
         shape(padded_channels, 8), shape(height, 1)],
        [SMEM] * 2 + [VMEM] * 9, flops=2_000_000_000, moved=4_000_000,
    )(
        stiffness, density, mode_weight.reshape(2, modes_x * channels, channels), lift_weight,
        lift_bias.reshape(1, channels), local_weight, spread, place, owner, turn, wide,
    )

    part = lambda fields, dtype: shape(fields, modes_x // 2, modes_y, width, dtype=dtype)

    def spectrum(body, outs, inputs, lines, specs=None, scratch=()):
        return call(
            body, outs, specs or [SMEM] + [VMEM] * (inputs + 2),
            [pltpu.VMEM((4 * brick_y, lines * width), BF16), pltpu.VMEM((modes_y, lines * width), F32), *scratch],
            flops=cells_count * 256 * lines, moved=cells_count * 2 * lines,
        )

    stages = [(axis, count, 2 ** (bit + 1) - 1) for axis, count in (("gy", column_count), ("gx", cycle_count))
              for bit in range((count - 1).bit_length())]
    swap = lambda value: lax.ppermute(value, "gz", swap_core)

    def exchange(value, axis, count, distance):
        return lax.ppermute(value.astype(BF16), axis, xor_pairs(count, distance))

    tables = (twiddle_x, stiffness, density, forward_z, forward_y)
    early = spectrum(
        materials_body, part(2, F32), 1, 2 * brick_x, [HBM] * 5 + [VMEM],
        [(pltpu.SMEM if table.ndim == 1 else pltpu.VMEM)(table.shape, table.dtype) for table in tables]
        + [pltpu.SemaphoreType.DMA((5,))],
    )(*here(*[jnp.asarray(table) for table in tables]), cells)

    for repeat in range(STEPS):
        last = repeat == STEPS - 1
        far = lax.ppermute(sent, ("gx", "gy", "gz"), row_pairs(cycle_count, column_count))
        mate = swap(current)
        halos = [lax.ppermute(edge_values[0], "gy", xor_pairs(column_count, 1))]
        if two_sided:
            halos.append(lax.ppermute(edge_values[1], "gy", odd_pairs(column_count)))
        if repeat == 0:
            far, early = lax.optimization_barrier((far, early))
        if repeat == 1:
            far, mixing, pointwise, lift_table, offset = lax.optimization_barrier(
                (far, mixing, pointwise, lift_table, offset)
            )
        if last:
            prior = spectrum(prior_body, shape(modes_x // 2, modes_y, width), 2, brick_x)(
                twiddle_x, current, mate, forward_z, forward_y
            )
            far, prior = lax.optimization_barrier((far, prior))
            prior_mate = mate
        outs = [field] + ([] if last else [sending] + edge)
        body = lambda *refs, last=last: step_body(two_sided, last, *refs)
        new, *others = call(
            body, outs, [VMEM] * (6 + len(halos)),
            [pltpu.VMEM((brick_y + 2 * EDGE, total_z), F32)], flops=cells_count * 60, moved=cells_count * 28,
        )(current, before, ratio, bend, mate, far, *halos)
        if not last:
            sent, *edge_values = others
        current, before = new, current

    total, sent = spectrum(wave_body, [part(FIELDS, F32), part(1, BF16)], 3, rows)(
        twiddle_x, current, prior, early, forward_z, forward_y
    )
    total = total + jnp.pad(swap(sent).astype(F32), ((0, FIELDS - 1), (0, 0), (0, 0), (0, 0)))
    wave_other = swap(current)
    group = 8
    steps = brick_y // group
    whole = lambda array: pl.BlockSpec(array.shape, lambda i: (0,) * len(array.shape))

    def pointwise_part(start):
        slab = lambda count: pl.BlockSpec((count, group, total_z), lambda i: (0, i + start, 0))
        return pl.pallas_call(
            pointwise_body,
            grid=(steps // 2,),
            out_shape=shape(height, brick_y // 2, total_z),
            in_specs=[SMEM] * 2 + [slab(rows)] * 4 + [slab(brick_x), whole(lift_table), whole(pointwise), whole(offset)],
            out_specs=pl.BlockSpec((height, group, total_z), lambda i: (0, i, 0)),
            scratch_shapes=[pltpu.VMEM((group, right_depth, total_z), BF16)],
            compiler_params=pltpu.CompilerParams(vmem_limit_bytes=16 * 1024 * 1024),
            cost_estimate=pl.CostEstimate(flops=cells_count * 20000, bytes_accessed=cells_count * 50, transcendentals=0),
        )(stiffness, density, current, before, wave_other, prior_mate, cells, lift_table, pointwise, offset)

    for index, stage in enumerate(stages):
        arrived = exchange(total, *stage)
        if index == len(stages) - 2:
            local_low = pointwise_part(0)
            arrived, local_low = lax.optimization_barrier((arrived, local_low))
        if index == len(stages) - 1:
            local_high = pointwise_part(steps // 2)
            arrived, local_high = lax.optimization_barrier((arrived, local_high))
        total = total + arrived.astype(F32)
    other = swap(total.astype(BF16))
    scoped = 12 * 2**20 + 4 * (6 * 2 * modes_x * modes_y * width + brick_y * coupled * width + 6 * group * coupled * total_z)
    features, wave = pl.pallas_call(
        output_body,
        grid=(steps,),
        out_shape=[shape(rows, channels, brick_y, total_z, dtype=BF16), shape(*pressure.shape)],
        in_specs=[whole(part(FIELDS, F32)), whole(part(FIELDS, BF16)),
           pl.BlockSpec((height, group, total_z), lambda i: (0, jnp.minimum(i, steps // 2 - 1), 0)),
           pl.BlockSpec((height, group, total_z), lambda i: (0, jnp.maximum(i - steps // 2, 0), 0)),
           whole(mixing), whole(inverse_y), whole(inverse_z),
                  whole(field), whole(field)],
        out_specs=[pl.BlockSpec((rows, channels, group, total_z), lambda i: (0, 0, i, 0)), whole(pressure)],
        scratch_shapes=[
            pltpu.VMEM((brick_y, coupled, width), F32),
            pltpu.VMEM((group, 2 * coupled, total_z), BF16),
            pltpu.VMEM((height, group, total_z), F32),
        ],
        compiler_params=pltpu.CompilerParams(vmem_limit_bytes=scoped),
        cost_estimate=pl.CostEstimate(flops=cells_count * 2000, bytes_accessed=cells_count * 60, transcendentals=cells_count * 20),
    )(total, other, local_low, local_high, mixing, inverse_y, inverse_z, current, wave_other)
    features = features.transpose(0, 2, 1, 3)
    return (wave, features)


def solution(mesh):
    placed = (
        P(("grp", "gx"), "gy", "gz"),
        P(("grp", "gx"), "gy", "gz"),
        P(("grp", "gx"), "gy", "gz"),
        P(),
        P(),
        P(),
        P(),
        P(),
        P(),
        P(),
    )
    return jax.shard_map(
        per_device,
        mesh=mesh,
        in_specs=placed,
        out_specs=(P(("grp", "gx"), "gy", "gz"), P(("grp", "gx", "gz"), "gy", None, None)),
        check_vma=False,
    )
```

```python
import math

import numpy as np
import jax
import jax.numpy as jnp
from jax import lax
from jax.experimental import pallas as pl
from jax.experimental.pallas import tpu as pltpu
from jax.sharding import PartitionSpec as P
import ml_dtypes

STEPS = 4
FIELDS = 4
REACH = 4
EDGE = 8
stencil_taps = (-205.0 / 72.0, 8.0 / 5.0, -1.0 / 5.0, 8.0 / 315.0, -1.0 / 560.0)
F32 = jnp.float32
BF16 = jnp.bfloat16
HIGHEST = lax.Precision.HIGHEST

VMEM = pl.BlockSpec(memory_space=pltpu.VMEM)
SMEM = pl.BlockSpec(memory_space=pltpu.SMEM)
HBM = pl.BlockSpec(memory_space=pltpu.HBM)


def rounded(table):
    return table.astype(ml_dtypes.bfloat16)


def kept_modes(length, mode_count):
    position = np.arange(mode_count)
    return np.where(position < mode_count // 2, position, length - mode_count + position)


def cos_sin(source, target, length):
    product = (source[:, None] * target[None, :]) % length
    phases = np.float32(2.0 * math.pi / length) * product.astype(np.float32)
    return rounded(np.cos(phases)), rounded(np.sin(phases))


def call(body, outs, in_specs, scratch=(), flops=0, moved=0):
    return pl.pallas_call(
        body,
        out_shape=outs,
        in_specs=in_specs,
        out_specs=jax.tree.map(lambda _: VMEM, outs),
        scratch_shapes=list(scratch),
        compiler_params=pltpu.CompilerParams(vmem_limit_bytes=16 * 1024 * 1024),
        cost_estimate=pl.CostEstimate(flops=flops, bytes_accessed=moved, transcendentals=0),
    )


def begin(sources, targets, semaphores):
    copies = [
        pltpu.make_async_copy(source, target, semaphores.at[index])
        for index, (source, target) in enumerate(zip(sources, targets))
    ]
    for copy in copies:
        copy.start()
    return copies


def here(*arrays):
    return [pltpu.with_memory_space_constraint(jnp.asarray(array), pltpu.HBM) for array in arrays]


def room(*arrays):
    return [(pltpu.SMEM if array.ndim == 1 else pltpu.VMEM)(array.shape, array.dtype) for array in arrays] + [
        pltpu.SemaphoreType.DMA((len(arrays),))
    ]


def high_low(value):
    high = value.astype(BF16)
    return high, (value - high.astype(F32)).astype(BF16)


def turned(value, half, sign):
    lane = lax.broadcasted_iota(jnp.int32, value.shape, value.ndim - 1)
    swapped = pltpu.roll(value, half, value.ndim - 1)
    return jnp.where(lane < half, sign * swapped, -sign * swapped)


def looked_up(material, table, entries):
    result = jnp.full(material.shape, table(0), F32)
    for entry in range(1, entries):
        result = jnp.where(material == entry, table(entry), result)
    return result


def middle(table):
    total = table[0]
    for entry in range(1, table.shape[0]):
        total = total + table[entry]
    return total * (1.0 / table.shape[0])


def edges(value_of, outs, row_parity, brick_y):
    for position, out in enumerate(outs):
        upper = row_parity == position
        out[...] = jnp.where(upper, value_of(brick_y - EDGE, brick_y), value_of(0, EDGE))


def slot():
    return (lax.axis_index("gz") + lax.axis_index("gx")) % 2


def assemble_body(count, *refs):
    tables_in, own_in, got = refs[:3], refs[3:6], refs[6:9]
    p_out, q_out, ratio, bend, sent, cells = refs[9:15]
    edge_outs = refs[15 : 15 + count]
    tables, own, semaphores = refs[15 + count : 18 + count], refs[18 + count : 21 + count], refs[21 + count]
    core, column = lax.axis_index("gz"), lax.axis_index("gy")
    rows, brick_y = p_out.shape[:2]
    start = slot() * rows
    sources = [source.at[pl.ds(start, rows)] for source in own_in[:2]] + [own_in[2]]
    copies = [
        pltpu.make_async_copy(source, target, semaphores.at[index])
        for index, (source, target) in enumerate(zip(list(tables_in) + sources, list(tables) + list(own)))
    ]
    for copy in copies:
        copy.start()
    for copy in copies:
        copy.wait()
    stiffness, density, nonlinear = tables
    entries = stiffness.shape[0]

    def whole(mine, other):
        return jnp.concatenate(
            [jnp.where(core == 0, mine, other), jnp.where(core == 0, other, mine)], axis=-1
        )

    for row in range(cells.shape[0]):
        cells[row] = whole(own[2][row], got[2][row])
    for row in range(rows):
        value = whole(own[0][row], got[0][start + row])
        p_out[row] = value
        sent[row] = value.astype(BF16)
        q_out[row] = whole(own[1][row], got[1][start + row])
        cell = cells[start + row]
        ratio[row] = looked_up(cell, lambda e: stiffness[e] / density[e], entries)
        bend[row] = looked_up(cell, lambda e: nonlinear[e], entries)
    edges(lambda a, b: p_out[:, a:b, :], edge_outs, column % 2, brick_y)


def step_body(two_sided, last, p_ref, q_ref, ratio, bend, mate, far, *rest):
    count = 2 if two_sided else 1
    halos = rest[:count]
    new_ref = rest[count]
    sent = None if last else rest[count + 1]
    edge_outs = rest[count + 2 : -1]
    padded = rest[-1]
    place = slot()
    parity = lax.axis_index("gy") % 2
    rows, brick_y, depth = p_ref.shape
    lane = lax.broadcasted_iota(jnp.int32, (brick_y, depth), 1)
    zero_edge = jnp.zeros((EDGE, depth), F32)

    cycle = lax.axis_index("gx")
    outside = cycle == jnp.where(place == 0, 0, lax.axis_size("gx") - 1)

    def line(index):
        if 0 <= index < rows:
            return p_ref[index]
        at = index % rows
        beyond = jnp.where(outside, 0.0, far[at].astype(F32))
        return jnp.where(place == (0 if index < 0 else 1), beyond, mate[at])

    for row in range(rows):
        first = halos[0][row]
        second = halos[1][row] if two_sided else zero_edge
        center = p_ref[row]
        padded[0:EDGE, :] = jnp.where(parity == 0, second, first)
        padded[EDGE : EDGE + brick_y, :] = center
        padded[EDGE + brick_y :, :] = jnp.where(parity == 0, first, second)
        total = (3.0 * stencil_taps[0]) * center
        for offset in range(1, REACH + 1):
            low, high = EDGE - offset, EDGE + offset
            pair = padded[low : low + brick_y, :] + padded[high : high + brick_y, :]
            pair = pair + (line(row - offset) + line(row + offset))
            pair = pair + jnp.where(lane >= offset, pltpu.roll(center, offset, 1), 0.0)
            pair = pair + jnp.where(
                lane < depth - offset, pltpu.roll(center, depth - offset, 1), 0.0
            )
            total = total + stencil_taps[offset] * pair
        change = center - q_ref[row]
        value = (center + change) + ratio[row] * total + bend[row] * change * change
        new_ref[row] = value
        if not last:
            sent[row] = value.astype(BF16)
    if not last:
        edges(lambda a, b: new_ref[:, a:b, :], edge_outs, parity, brick_y)


def transformed(sources, first, twiddle_x, table_z, table_y, lines, grid, late=()):
    column = lax.axis_index("gy")
    brick_y = lines.shape[0] // 4
    modes_y = grid.shape[0]
    width = table_z.shape[1]
    half = width // 2
    for field, rows in enumerate(sources):
        for row, load in enumerate(rows):
            high, low = high_low(load())
            modes = jnp.dot(high, table_z[...], preferred_element_type=F32)
            modes = modes + jnp.dot(low, table_z[...], preferred_element_type=F32)
            back = turned(modes, half, 1.0)
            high, low = high_low(modes)
            back_high, back_low = high_low(back)
            lanes = slice((field * len(rows) + row) * width, (field * len(rows) + row + 1) * width)
            for index, part in enumerate((high, back_high, low, back_low)):
                lines[index * brick_y : (index + 1) * brick_y, lanes] = part
    grid[...] = jnp.dot(table_y[column], lines[...], preferred_element_type=F32)
    for copy in late:
        copy.wait()

    def at_mode(field, modes_x):
        count = len(sources[field])
        values = [
            grid[:, (field * count + row) * width : (field * count + row + 1) * width] for row in range(count)
        ]
        backs = [turned(value, half, 1.0) for value in values]

        def summed(mode):
            total = jnp.zeros((modes_y, width), F32)
            for row in range(count):
                at = ((first + row) * modes_x + mode) * 2
                total = total + twiddle_x[at] * values[row] + twiddle_x[at + 1] * backs[row]
            return total

        return summed

    return at_mode


def materials_body(*refs):
    sources, cells, keep, table_z, table_y, lines, grid = refs[:5], *refs[5:11]
    twiddle_x, stiffness, density, semaphores = refs[11:15]
    copies = begin(sources, (twiddle_x, stiffness, density, table_z, table_y), semaphores)
    for copy in copies:
        copy.wait()
    half_x = keep.shape[1]
    entries = stiffness.shape[0]
    rows = cells.shape[0]
    sources = []
    for table in (stiffness, density):
        center = middle(table)
        sources.append([
            lambda row=row, table=table, center=center: looked_up(cells[row], lambda e: table[e] - center, entries)
            for row in range(rows)
        ])
    at_mode = transformed(sources, lax.axis_index("gx") * rows, twiddle_x, table_z, table_y, lines, grid)
    core = lax.axis_index("gz")
    for field in range(2):
        summed = at_mode(field, 2 * half_x)

        @pl.loop(0, half_x)
        def _(mode):
            keep[field, mode] = summed(core * half_x + mode)


def prior_body(twiddles, own, mate, table_z, table_y, keep, lines, grid, twiddle_x, semaphores):
    copies = begin((twiddles,), (twiddle_x,), semaphores)
    half_x = keep.shape[0]
    rows = own.shape[0]
    place = slot()
    sources = [
        (lambda row=row: jnp.where(place == 0, own[row], mate[row])) for row in range(rows)
    ] + [(lambda row=row: jnp.where(place == 0, mate[row], own[row])) for row in range(rows)]
    at_mode = transformed([sources], lax.axis_index("gx") * (2 * rows), twiddle_x, table_z, table_y, lines, grid, copies)
    core = lax.axis_index("gz")
    summed = at_mode(0, 2 * half_x)

    @pl.loop(0, half_x)
    def _(mode):
        keep[mode] = summed(core * half_x + mode)


def wave_body(twiddles, own, prior, early, table_z, table_y, keep, send, lines, grid, twiddle_x, semaphores):
    copies = begin((twiddles,), (twiddle_x,), semaphores)
    half_x = keep.shape[1]
    rows = own.shape[0]
    first = (lax.axis_index("gx") * 2 + slot()) * rows
    sources = [(lambda row=row: own[row]) for row in range(rows)]
    at_mode = transformed([sources], first, twiddle_x, table_z, table_y, lines, grid, copies)
    core = lax.axis_index("gz")
    summed = at_mode(0, 2 * half_x)
    keep[1] = prior[...]
    keep[2:4] = early[...]

    @pl.loop(0, half_x)
    def _(mode):
        keep[0, mode] = summed(core * half_x + mode)
        send[0, mode] = summed((1 - core) * half_x + mode).astype(BF16)


def prepare_body(*refs):
    sources, outs, targets, semaphores = refs[:11], refs[11:15], refs[15:26], refs[26]
    mixing, pointwise, lift_table, offset = outs
    block = lax.axis_index("gx") * 2 + lax.axis_index("gz")
    copies = begin([*sources[:9], sources[9].at[block], sources[10]], targets, semaphores)
    for copy in copies:
        copy.wait()
    stiffness, density, mode_ref, lift_ref, bias_ref, local_ref, spread_ref, place_ref, owner_ref, turn_ref, wide_ref = targets
    half = place_ref.shape[1]
    channels = lift_ref.shape[1]
    spread = owner_ref[...]

    def dot(a, b, dims=((1,), (0,))):
        return lax.dot_general(a, b, (dims, ((), ())), precision=HIGHEST, preferred_element_type=F32)

    across = ((1,), (1,))
    lifted = dot(dot(spread_ref[:, :channels], lift_ref[...], across), place_ref[...])
    lifted = lifted * spread_ref[:, channels : channels + half]
    flat = [mode_ref[index].reshape(-1, channels) for index in range(2)]
    real, imag = [dot(dot(spread, values, across), lifted) for values in flat]
    cosine = turn_ref[0]
    sine = turn_ref[1]
    coupled = jnp.concatenate([cosine * real - sine * imag, -(cosine * imag + sine * real)], axis=1)
    width = 2 * half
    blocks = mixing.shape[0]
    for index in range(blocks):
        parts = [jnp.zeros((coupled.shape[0], width * index), F32)] * (index > 0) + [coupled]
        parts += [jnp.zeros((coupled.shape[0], width * (blocks - 1 - index)), F32)] * (index < blocks - 1)
        line = jnp.concatenate(parts, axis=1) if blocks > 1 else coupled
        mixing[index] = line.astype(BF16)
    constant = dot(spread, mode_ref[0, :, 0, :], across)
    bias = bias_ref[...] + middle(stiffness) * lift_ref[2:3, :] + middle(density) * lift_ref[3:4, :]
    offset[...] = jnp.sum(constant * bias, axis=1, keepdims=True)
    height = spread.shape[0]
    widest = wide_ref[0:channels, :]
    repeated = dot(dot(spread, local_ref[...].astype(F32), across), widest)
    pointwise[...] = (repeated * wide_ref[channels : channels + height, :]).astype(BF16)
    padded = wide_ref[channels + height :, 0:channels]
    lift_table[:, 0:FIELDS] = dot(padded, lift_ref[...], across)
    lift_table[:, FIELDS : FIELDS + 1] = dot(padded, bias_ref[...], across)
    lift_table[:, FIELDS + 1 :] = jnp.zeros_like(lift_table[:, FIELDS + 1 :])


def pointwise_body(stiffness_in, density_in, p_ref, q_ref, p_mate, q_mate, cells, lift_ref, left, offset, *rest):
    out, right, stiffness, density, semaphores = rest[-5:]
    rows, group, depth = p_ref.shape
    padded_channels = lift_ref.shape[0]
    height = rows * padded_channels
    entries = stiffness.shape[0]
    core = lax.axis_index("gz")
    own = slot() == core

    @pl.when(pl.program_id(0) == 0)
    def _():
        right[...] = jnp.zeros_like(right)
        for copy in begin((stiffness_in, density_in), (stiffness, density), semaphores):
            copy.wait()

    weights = [lift_ref[:, index : index + 1] for index in range(FIELDS + 1)]
    values = []
    for row in range(rows):
        cell = cells[core * rows + row]
        values.append((
            jnp.where(own, p_ref[row], p_mate[row]),
            jnp.where(own, q_ref[row], q_mate[row]),
            looked_up(cell, lambda e: stiffness[e], entries),
            looked_up(cell, lambda e: density[e], entries),
        ))
    for y in range(group):
        lifted = []
        for row in range(rows):
            total = jnp.broadcast_to(weights[FIELDS], (padded_channels, depth))
            for value, weight in zip(values[row], weights):
                total = total + value[y : y + 1, :] * weight
            lifted.append(total)
        right[y, 0:height, :] = jnp.concatenate(lifted, axis=0).astype(BF16)
        out[:, y, :] = jnp.dot(left[...], right[y], preferred_element_type=F32) + offset[...]


def join_body(own, other, wave_out):
    core = lax.axis_index("gz")
    rows, _, depth = own.shape
    half = depth // 2
    place = slot()
    for row in range(rows):
        for ref, start in ((own, place * rows), (other, (1 - place) * rows)):
            wave_out[start + row] = jnp.where(core == 0, ref[row, :, :half], ref[row, :, half:])


def output_body(
    mine, other, local, left, table_y, table_z, features, modes, right, sums,
):
    step = pl.program_id(0)
    core, column = lax.axis_index("gz"), lax.axis_index("gy")
    half_x, modes_y, width = mine.shape[1:]
    modes_x = 2 * half_x
    half = width // 2
    rows, channels, group, depth = features.shape
    coupled = FIELDS * modes_x

    @pl.when(step == 0)
    def _():
        chunk = min(8, modes_x)
        left_y = table_y[column]
        for field in range(FIELDS):
            for start in range(0, modes_x, chunk):
                parts = [[], []]
                for mode in range(start, start + chunk):
                    at = (field, mode % half_x)
                    value = jnp.where(core == mode // half_x, mine[at], other[at].astype(F32))
                    parts[0].append(value.astype(BF16))
                    parts[1].append(turned(value, half, -1.0).astype(BF16))
                stacked = jnp.concatenate([jnp.concatenate(part, axis=1) for part in parts], axis=0)
                result = jnp.dot(left_y, stacked, preferred_element_type=F32)
                for mode in range(start, start + chunk):
                    lanes = slice((mode - start) * width, (mode - start + 1) * width)
                    modes[:, mode * FIELDS + field, :] = result[:, lanes]

    base = pl.multiple_of(step * group, group)
    lines = modes[pl.ds(base, group)].reshape(group * coupled, width).astype(BF16)
    waves = jnp.dot(lines, table_z[...], preferred_element_type=F32).astype(BF16)
    joined, height = left.shape[:2]
    for y in range(group):
        lines = slice(y * coupled, (y + 1) * coupled)
        start = y * 2 * coupled
        right[start : start + coupled, :] = waves[lines, :depth]
        right[start + coupled : start + 2 * coupled, :] = waves[lines, depth:]
    span = joined * 2 * coupled
    every = left[...].reshape(joined * height, span)
    for first in range(0, group, joined):
        start = first * 2 * coupled
        result = jnp.dot(every, right[start : start + span, :], preferred_element_type=F32)
        for index in range(joined):
            sums[:, first + index, :] = result[index * height : (index + 1) * height]
    for row in range(rows):
        for channel in range(channels):
            at = row * channels + channel
            total = sums[at] + local[at, pl.ds(base, group), :]
            scale = math.sqrt(2.0 / math.pi)
            inner = total * (scale + (scale * 0.044715) * (total * total))
            part = 0.5 * total
            total = part + part * jnp.tanh(inner)
            features[row, channel] = total.astype(BF16)


def xor_pairs(count, distance):
    return [(index, index ^ distance) for index in range(count)]


def odd_pairs(count):
    pairs = [(index, index + 1) for index in range(1, count - 1, 2)]
    return pairs + [(target, source) for source, target in pairs]


def row_pairs(cycles, columns):
    place = lambda cycle, column, core: (cycle * columns + column) * 2 + core
    pairs = []
    for column in range(columns):
        for cycle in range(cycles - 1):
            one, two = place(cycle, column, 1 - cycle % 2), place(cycle + 1, column, 1 - cycle % 2)
            pairs += [(one, two), (two, one)]
        for cycle, core in ((0, 0), (cycles - 1, 1 - (cycles - 1) % 2)):
            pairs.append((place(cycle, column, core), place(cycle, column ^ 1, core)))
    return pairs


def per_device(
    pressure,
    previous,
    material,
    stiffness,
    density,
    nonlinear,
    lift_weight,
    lift_bias,
    mode_weight,
    local_weight,
):
    brick_x, brick_y, brick_z = pressure.shape
    cycle_count = lax.axis_size("gx")
    column_count = lax.axis_size("gy")
    core_count = lax.axis_size("gz")
    total_x = brick_x * cycle_count
    total_y = brick_y * column_count
    total_z = brick_z * core_count
    modes_x = total_x // 4
    modes_y = total_y // 4
    modes_z = total_z // 4
    width = 2 * modes_z
    channels = lift_bias.shape[0]
    rows = brick_x // core_count
    assert core_count == 2 and rows >= REACH
    blocks = cycle_count * core_count
    padded_channels = -(-channels // 8) * 8
    height = rows * channels
    coupled = FIELDS * modes_x
    joined = max(1, 256 // (2 * coupled))
    right_depth = -(-rows * padded_channels // 128) * 128
    two_sided = column_count > 2

    kept_first = kept_modes(total_x, modes_x)
    kept_second = kept_modes(total_y, modes_y)
    kept_third = np.arange(modes_z)
    cz, sz = cos_sin(np.arange(total_z), kept_third, total_z)
    forward_z = np.concatenate([cz, -sz], 1)
    weight = np.where(kept_third == 0, 1.0, 2.0) / (total_x * total_y * total_z)
    wc, ws = [rounded((t.astype(np.float32) * weight).T.astype(np.float32)) for t in (cz, sz)]
    inverse_z = np.concatenate(
        [np.concatenate([wc, ws], 1), np.concatenate([-ws.astype(np.float32), wc.astype(np.float32)], 1)], 0
    )
    inverse_z = rounded(inverse_z)
    cy, sy = cos_sin(kept_second, np.arange(total_y), total_y)
    cy3, sy3 = [t.reshape(modes_y, column_count, brick_y).transpose(1, 0, 2) for t in (cy, sy)]
    forward_y = np.concatenate([cy3, sy3, cy3, sy3], 2)
    cy3, sy3 = [t.transpose(0, 2, 1) for t in (cy3, sy3)]
    inverse_y = np.concatenate([cy3, sy3], 2)
    cx, sx = [t.astype(np.float32) for t in cos_sin(np.arange(total_x), kept_first, total_x)]
    twiddle_x = np.stack([cx, sx], -1).reshape(-1)
    owner = np.tile(np.eye(channels, dtype=np.float32), (rows, 1))
    turn = np.zeros((blocks, 2, height, coupled), np.float32)
    for source, table in enumerate((cx, sx)):
        turn[:, source] = np.repeat(
            np.repeat(table.reshape(blocks, rows, modes_x), channels, 1), FIELDS, 2
        )
    padded_eye = np.eye(channels, padded_channels, dtype=np.float32)
    wide = np.zeros((channels + height + padded_channels, right_depth), np.float32)
    wide[:channels, : rows * padded_channels] = np.tile(padded_eye, (1, rows))
    wide[channels : channels + height, : rows * padded_channels] = np.kron(
        np.eye(rows), np.ones((channels, padded_channels))
    )
    wide[channels + height :, :channels] = padded_eye.T
    spread = np.repeat(np.eye(channels, dtype=np.float32), modes_x, 0)
    same = np.tile(np.repeat(np.eye(modes_x, dtype=np.float32), FIELDS, 1), (channels, 1))
    spread = np.concatenate([spread, same], 1)
    place = np.tile(np.eye(FIELDS, dtype=np.float32), (1, modes_x))

    def shape(*dims, dtype=F32):
        return jax.ShapeDtypeStruct(dims, dtype)

    cells_count = rows * brick_y * total_z
    field = shape(rows, brick_y, total_z)
    edge = [shape(rows, EDGE, total_z)] * (2 if two_sided else 1)

    swap_core = xor_pairs(core_count, 1)
    got = [lax.ppermute(array, "gz", swap_core) for array in (pressure, previous, material)]
    sending = shape(rows, brick_y, total_z, dtype=BF16)
    current, before, ratio, bend, sent, cells, *edge_values = call(
        lambda *refs: assemble_body(len(edge), *refs),
        [field] * 4 + [sending, shape(brick_x, brick_y, total_z, dtype=jnp.int32)] + edge, [HBM] * 6 + [VMEM] * 3,
        [pltpu.SMEM(stiffness.shape, F32)] * 3 + [pltpu.VMEM((rows, brick_y, brick_z), F32)] * 2
        + [pltpu.VMEM((brick_x, brick_y, brick_z), jnp.int32), pltpu.SemaphoreType.DMA((6,))], moved=cells_count * 36
    )(*here(stiffness, density, nonlinear, pressure, previous, material), *got)

    weights = (
        stiffness, density, mode_weight.transpose(0, 2, 1, 3), lift_weight, lift_bias.reshape(1, channels),
        local_weight, spread, place, owner, turn, wide,
    )
    mixing, pointwise, lift_table, offset = call(
        prepare_body,
        [shape(joined, height, joined * 2 * coupled, dtype=BF16), shape(height, right_depth, dtype=BF16),
         shape(padded_channels, 8), shape(height, 1)],
        [HBM] * 11, room(*weights[:9], turn[0], wide), flops=2_000_000_000, moved=4_000_000,
    )(*here(*weights))

    part = lambda fields, dtype: shape(fields, modes_x // 2, modes_y, width, dtype=dtype)

    def spectrum(body, outs, inputs, lines, specs=None, scratch=()):
        return call(
            body, outs, specs or [HBM] + [VMEM] * (inputs + 2),
            [pltpu.VMEM((4 * brick_y, lines * width), BF16), pltpu.VMEM((modes_y, lines * width), F32), *scratch],
            flops=cells_count * 256 * lines, moved=cells_count * 2 * lines,
        )

    stages = [(axis, count, 2 ** (bit + 1) - 1) for axis, count in (("gy", column_count), ("gx", cycle_count))
              for bit in range((count - 1).bit_length())]
    swap = lambda value: lax.ppermute(value, "gz", swap_core)

    def exchange(value, axis, count, distance):
        return lax.ppermute(value.astype(BF16), axis, xor_pairs(count, distance))

    tables = (twiddle_x, stiffness, density, forward_z, forward_y)
    early, forward_z, forward_y = spectrum(
        materials_body,
        [part(2, F32)] + [jax.ShapeDtypeStruct(table.shape, table.dtype) for table in (forward_z, forward_y)],
        1, 2 * brick_x, [HBM] * 5 + [VMEM], room(*tables[:3])[:3] + [pltpu.SemaphoreType.DMA((5,))],
    )(*here(*tables), cells)
    twiddles = here(twiddle_x)
    twiddle_room = room(twiddle_x)

    for repeat in range(STEPS):
        last = repeat == STEPS - 1
        far = lax.ppermute(sent, ("gx", "gy", "gz"), row_pairs(cycle_count, column_count))
        mate = swap(current)
        halos = [lax.ppermute(edge_values[0], "gy", xor_pairs(column_count, 1))]
        if two_sided:
            halos.append(lax.ppermute(edge_values[1], "gy", odd_pairs(column_count)))
        if repeat == 0:
            far, early = lax.optimization_barrier((far, early))
        if repeat == 1:
            far, mixing, pointwise, lift_table, offset = lax.optimization_barrier(
                (far, mixing, pointwise, lift_table, offset)
            )
        if last:
            prior = spectrum(prior_body, shape(modes_x // 2, modes_y, width), 2, brick_x, None, twiddle_room)(
                *twiddles, current, mate, forward_z, forward_y
            )
            far, prior = lax.optimization_barrier((far, prior))
            prior_mate = mate
        outs = [field] + ([] if last else [sending] + edge)
        body = lambda *refs, last=last: step_body(two_sided, last, *refs)
        new, *others = call(
            body, outs, [VMEM] * (6 + len(halos)),
            [pltpu.VMEM((brick_y + 2 * EDGE, total_z), F32)], flops=cells_count * 60, moved=cells_count * 28,
        )(current, before, ratio, bend, mate, far, *halos)
        if not last:
            sent, *edge_values = others
        current, before = new, current

    total, sent = spectrum(wave_body, [part(FIELDS, F32), part(1, BF16)], 3, rows, None, twiddle_room)(
        *twiddles, current, prior, early, forward_z, forward_y
    )
    total = total + jnp.pad(swap(sent).astype(F32), ((0, FIELDS - 1), (0, 0), (0, 0), (0, 0)))
    wave_other = swap(current)
    group = 8
    steps = brick_y // group
    whole = lambda array: pl.BlockSpec(array.shape, lambda i: (0,) * len(array.shape))

    def pointwise_part(start, held=()):
        slab = lambda count: pl.BlockSpec((count, group, total_z), lambda i: (0, i + start, 0))
        return pl.pallas_call(
            pointwise_body,
            grid=(steps // 2,),
            out_shape=shape(height, brick_y, total_z),
            in_specs=[HBM] * 2 + [slab(rows)] * 4 + [slab(brick_x), whole(lift_table), whole(pointwise), whole(offset)]
            + [pl.BlockSpec(memory_space=pl.ANY)] * len(held),
            out_specs=pl.BlockSpec((height, group, total_z), lambda i: (0, i + start, 0)),
            input_output_aliases={10: 0} if held else {},
            scratch_shapes=[pltpu.VMEM((group, right_depth, total_z), BF16)] + room(stiffness, density),
            compiler_params=pltpu.CompilerParams(vmem_limit_bytes=16 * 1024 * 1024),
            cost_estimate=pl.CostEstimate(flops=cells_count * 20000, bytes_accessed=cells_count * 50, transcendentals=0),
        )(*here(stiffness, density), current, before, wave_other, prior_mate, cells, lift_table, pointwise, offset, *held)

    for index, stage in enumerate(stages):
        arrived = exchange(total, *stage)
        if index == len(stages) - 2:
            local = pointwise_part(0)
            wave = call(join_body, shape(*pressure.shape), [VMEM] * 2, moved=cells_count * 12)(current, wave_other)
            arrived, local, wave = lax.optimization_barrier((arrived, local, wave))
        if index == len(stages) - 1:
            local = pointwise_part(steps // 2, (local,))
            arrived, local = lax.optimization_barrier((arrived, local))
        total = total + arrived.astype(F32)
    other = swap(total.astype(BF16))
    batch = min(32, brick_y)
    scoped = 14 * 2**20 + 4 * (brick_y * coupled * width + 6 * batch * coupled * total_z)
    features = pl.pallas_call(
        output_body,
        grid=(brick_y // batch,),
        out_shape=shape(rows, channels, brick_y, total_z, dtype=BF16),
        in_specs=[VMEM, VMEM,
                  VMEM, VMEM, VMEM, VMEM],
        out_specs=pl.BlockSpec((rows, channels, batch, total_z), lambda i: (0, 0, i, 0)),
        scratch_shapes=[
            pltpu.VMEM((brick_y, coupled, width), F32),
            pltpu.VMEM((batch * 2 * coupled, total_z), BF16),
            pltpu.VMEM((height, batch, total_z), F32),
        ],
        compiler_params=pltpu.CompilerParams(vmem_limit_bytes=scoped),
        cost_estimate=pl.CostEstimate(flops=cells_count * 2000, bytes_accessed=cells_count * 60, transcendentals=cells_count * 20),
    )(total, other, local, mixing, inverse_y, inverse_z)
    features = features.transpose(0, 2, 1, 3)
    return (wave, features)


def solution(mesh):
    placed = (
        P(("grp", "gx"), "gy", "gz"),
        P(("grp", "gx"), "gy", "gz"),
        P(("grp", "gx"), "gy", "gz"),
        P(),
        P(),
        P(),
        P(),
        P(),
        P(),
        P(),
    )
    return jax.shard_map(
        per_device,
        mesh=mesh,
        in_specs=placed,
        out_specs=(P(("grp", "gx"), "gy", "gz"), P(("grp", "gx", "gz"), "gy", None, None)),
        check_vma=False,
    )
```

```python
import math

import numpy as np
import jax
import jax.numpy as jnp
from jax import lax
from jax.experimental import pallas as pl
from jax.experimental.pallas import tpu as pltpu
from jax.sharding import PartitionSpec as P
import ml_dtypes

STEPS = 4
FIELDS = 4
REACH = 4
EDGE = 8
stencil_taps = (-205.0 / 72.0, 8.0 / 5.0, -1.0 / 5.0, 8.0 / 315.0, -1.0 / 560.0)
F32 = jnp.float32
BF16 = jnp.bfloat16
HIGHEST = lax.Precision.HIGHEST

VMEM = pl.BlockSpec(memory_space=pltpu.VMEM)
SMEM = pl.BlockSpec(memory_space=pltpu.SMEM)
HBM = pl.BlockSpec(memory_space=pltpu.HBM)


def rounded(table):
    return table.astype(ml_dtypes.bfloat16)


def kept_modes(length, mode_count):
    position = np.arange(mode_count)
    return np.where(position < mode_count // 2, position, length - mode_count + position)


def cos_sin(source, target, length):
    product = (source[:, None] * target[None, :]) % length
    phases = np.float32(2.0 * math.pi / length) * product.astype(np.float32)
    return rounded(np.cos(phases)), rounded(np.sin(phases))


def call(body, outs, in_specs, scratch=(), flops=0, moved=0):
    return pl.pallas_call(
        body,
        out_shape=outs,
        in_specs=in_specs,
        out_specs=jax.tree.map(lambda _: VMEM, outs),
        scratch_shapes=list(scratch),
        compiler_params=pltpu.CompilerParams(vmem_limit_bytes=16 * 1024 * 1024),
        cost_estimate=pl.CostEstimate(flops=flops, bytes_accessed=moved, transcendentals=0),
    )


def begin(sources, targets, semaphores):
    copies = [
        pltpu.make_async_copy(source, target, semaphores.at[index])
        for index, (source, target) in enumerate(zip(sources, targets))
    ]
    for copy in copies:
        copy.start()
    return copies


def here(*arrays):
    return [pltpu.with_memory_space_constraint(jnp.asarray(array), pltpu.HBM) for array in arrays]


def room(*arrays):
    return [(pltpu.SMEM if array.ndim == 1 else pltpu.VMEM)(array.shape, array.dtype) for array in arrays] + [
        pltpu.SemaphoreType.DMA((len(arrays),))
    ]


def high_low(value):
    high = value.astype(BF16)
    return high, (value - high.astype(F32)).astype(BF16)


def turned(value, half, sign):
    lane = lax.broadcasted_iota(jnp.int32, value.shape, value.ndim - 1)
    swapped = pltpu.roll(value, half, value.ndim - 1)
    return jnp.where(lane < half, sign * swapped, -sign * swapped)


def looked_up(material, table, entries):
    result = jnp.full(material.shape, table(0), F32)
    for entry in range(1, entries):
        result = jnp.where(material == entry, table(entry), result)
    return result


def middle(table):
    total = table[0]
    for entry in range(1, table.shape[0]):
        total = total + table[entry]
    return total * (1.0 / table.shape[0])


def edges(value_of, outs, row_parity, brick_y):
    for position, out in enumerate(outs):
        upper = row_parity == position
        out[...] = jnp.where(upper, value_of(brick_y - EDGE, brick_y), value_of(0, EDGE))


def slot():
    return (lax.axis_index("gz") + lax.axis_index("gx")) % 2


def assemble_body(count, *refs):
    tables_in, own_in, got = refs[:3], refs[3:6], refs[6:9]
    p_out, q_out, ratio, bend, sent, cells = refs[9:15]
    edge_outs = refs[15 : 15 + count]
    tables, own, semaphores = refs[15 + count : 18 + count], refs[18 + count : 21 + count], refs[21 + count]
    core, column = lax.axis_index("gz"), lax.axis_index("gy")
    rows, brick_y = p_out.shape[:2]
    start = slot() * rows
    sources = [source.at[pl.ds(start, rows)] for source in own_in[:2]] + [own_in[2]]
    copies = [
        pltpu.make_async_copy(source, target, semaphores.at[index])
        for index, (source, target) in enumerate(zip(list(tables_in) + sources, list(tables) + list(own)))
    ]
    for copy in copies:
        copy.start()
    for copy in copies:
        copy.wait()
    stiffness, density, nonlinear = tables
    entries = stiffness.shape[0]

    def whole(mine, other):
        return jnp.concatenate(
            [jnp.where(core == 0, mine, other), jnp.where(core == 0, other, mine)], axis=-1
        )

    for row in range(cells.shape[0]):
        cells[row] = whole(own[2][row], got[2][row])
    for row in range(rows):
        value = whole(own[0][row], got[0][start + row])
        p_out[row] = value
        sent[row] = value.astype(BF16)
        q_out[row] = whole(own[1][row], got[1][start + row])
        cell = cells[start + row]
        ratio[row] = looked_up(cell, lambda e: stiffness[e] / density[e], entries)
        bend[row] = looked_up(cell, lambda e: nonlinear[e], entries)
    edges(lambda a, b: p_out[:, a:b, :], edge_outs, column % 2, brick_y)


def step_body(two_sided, last, p_ref, q_ref, ratio, bend, mate, far, *rest):
    count = 2 if two_sided else 1
    halos = rest[:count]
    new_ref = rest[count]
    sent = None if last else rest[count + 1]
    edge_outs = rest[count + 2 : -1]
    padded = rest[-1]
    place = slot()
    parity = lax.axis_index("gy") % 2
    rows, brick_y, depth = p_ref.shape
    lane = lax.broadcasted_iota(jnp.int32, (brick_y, depth), 1)
    zero_edge = jnp.zeros((EDGE, depth), F32)

    cycle = lax.axis_index("gx")
    outside = cycle == jnp.where(place == 0, 0, lax.axis_size("gx") - 1)

    def line(index):
        if 0 <= index < rows:
            return p_ref[index]
        at = index % rows
        beyond = jnp.where(outside, 0.0, far[at].astype(F32))
        return jnp.where(place == (0 if index < 0 else 1), beyond, mate[at])

    for row in range(rows):
        first = halos[0][row]
        second = halos[1][row] if two_sided else zero_edge
        center = p_ref[row]
        padded[0:EDGE, :] = jnp.where(parity == 0, second, first)
        padded[EDGE : EDGE + brick_y, :] = center
        padded[EDGE + brick_y :, :] = jnp.where(parity == 0, first, second)
        total = (3.0 * stencil_taps[0]) * center
        for offset in range(1, REACH + 1):
            low, high = EDGE - offset, EDGE + offset
            pair = padded[low : low + brick_y, :] + padded[high : high + brick_y, :]
            pair = pair + (line(row - offset) + line(row + offset))
            pair = pair + jnp.where(lane >= offset, pltpu.roll(center, offset, 1), 0.0)
            pair = pair + jnp.where(
                lane < depth - offset, pltpu.roll(center, depth - offset, 1), 0.0
            )
            total = total + stencil_taps[offset] * pair
        change = center - q_ref[row]
        value = (center + change) + ratio[row] * total + bend[row] * change * change
        new_ref[row] = value
        if not last:
            sent[row] = value.astype(BF16)
    if not last:
        edges(lambda a, b: new_ref[:, a:b, :], edge_outs, parity, brick_y)


def transformed(sources, first, twiddle_x, table_z, table_y, lines, grid, late=()):
    column = lax.axis_index("gy")
    brick_y = lines.shape[0] // 4
    modes_y = grid.shape[0]
    width = table_z.shape[1]
    half = width // 2
    for field, rows in enumerate(sources):
        for row, load in enumerate(rows):
            high, low = high_low(load())
            modes = jnp.dot(high, table_z[...], preferred_element_type=F32)
            modes = modes + jnp.dot(low, table_z[...], preferred_element_type=F32)
            back = turned(modes, half, 1.0)
            high, low = high_low(modes)
            back_high, back_low = high_low(back)
            lanes = slice((field * len(rows) + row) * width, (field * len(rows) + row + 1) * width)
            for index, part in enumerate((high, back_high, low, back_low)):
                lines[index * brick_y : (index + 1) * brick_y, lanes] = part
    grid[...] = jnp.dot(table_y[column], lines[...], preferred_element_type=F32)
    for copy in late:
        copy.wait()

    def at_mode(field, modes_x):
        count = len(sources[field])
        values = [
            grid[:, (field * count + row) * width : (field * count + row + 1) * width] for row in range(count)
        ]
        backs = [turned(value, half, 1.0) for value in values]

        def summed(mode):
            total = jnp.zeros((modes_y, width), F32)
            for row in range(count):
                at = ((first + row) * modes_x + mode) * 2
                total = total + twiddle_x[at] * values[row] + twiddle_x[at + 1] * backs[row]
            return total

        return summed

    return at_mode


def materials_body(*refs):
    sources, cells, keep, table_z, table_y, lines, grid = refs[:5], *refs[5:11]
    twiddle_x, stiffness, density, semaphores = refs[11:15]
    copies = begin(sources, (twiddle_x, stiffness, density, table_z, table_y), semaphores)
    for copy in copies:
        copy.wait()
    half_x = keep.shape[1]
    entries = stiffness.shape[0]
    rows = cells.shape[0]
    sources = []
    for table in (stiffness, density):
        center = middle(table)
        sources.append([
            lambda row=row, table=table, center=center: looked_up(cells[row], lambda e: table[e] - center, entries)
            for row in range(rows)
        ])
    at_mode = transformed(sources, lax.axis_index("gx") * rows, twiddle_x, table_z, table_y, lines, grid)
    core = lax.axis_index("gz")
    for field in range(2):
        summed = at_mode(field, 2 * half_x)

        @pl.loop(0, half_x)
        def _(mode):
            keep[field, mode] = summed(core * half_x + mode)


def prior_body(twiddles, own, mate, table_z, table_y, keep, lines, grid, twiddle_x, semaphores):
    copies = begin((twiddles,), (twiddle_x,), semaphores)
    half_x = keep.shape[0]
    rows = own.shape[0]
    place = slot()
    sources = [
        (lambda row=row: jnp.where(place == 0, own[row], mate[row])) for row in range(rows)
    ] + [(lambda row=row: jnp.where(place == 0, mate[row], own[row])) for row in range(rows)]
    at_mode = transformed([sources], lax.axis_index("gx") * (2 * rows), twiddle_x, table_z, table_y, lines, grid, copies)
    core = lax.axis_index("gz")
    summed = at_mode(0, 2 * half_x)

    @pl.loop(0, half_x)
    def _(mode):
        keep[mode] = summed(core * half_x + mode)


def wave_body(twiddles, own, prior, early, table_z, table_y, keep, send, lines, grid, twiddle_x, semaphores):
    copies = begin((twiddles,), (twiddle_x,), semaphores)
    half_x = keep.shape[1]
    rows = own.shape[0]
    first = (lax.axis_index("gx") * 2 + slot()) * rows
    sources = [(lambda row=row: own[row]) for row in range(rows)]
    at_mode = transformed([sources], first, twiddle_x, table_z, table_y, lines, grid, copies)
    core = lax.axis_index("gz")
    summed = at_mode(0, 2 * half_x)
    keep[1] = prior[...]
    keep[2:4] = early[...]

    @pl.loop(0, half_x)
    def _(mode):
        keep[0, mode] = summed(core * half_x + mode)
        send[0, mode] = summed((1 - core) * half_x + mode).astype(BF16)


def prepare_body(*refs):
    sources, outs, targets, semaphores = refs[:11], refs[11:15], refs[15:26], refs[26]
    mixing, pointwise, lift_table, offset = outs
    block = lax.axis_index("gx") * 2 + lax.axis_index("gz")
    copies = begin([*sources[:9], sources[9].at[block], sources[10]], targets, semaphores)
    for copy in copies:
        copy.wait()
    stiffness, density, mode_ref, lift_ref, bias_ref, local_ref, spread_ref, place_ref, owner_ref, turn_ref, wide_ref = targets
    half = place_ref.shape[1]
    channels = lift_ref.shape[1]
    spread = owner_ref[...]

    def dot(a, b, dims=((1,), (0,))):
        return lax.dot_general(a, b, (dims, ((), ())), precision=HIGHEST, preferred_element_type=F32)

    across = ((1,), (1,))
    lifted = dot(dot(spread_ref[:, :channels], lift_ref[...], across), place_ref[...])
    lifted = lifted * spread_ref[:, channels : channels + half]
    flat = [mode_ref[index].reshape(-1, channels) for index in range(2)]
    real, imag = [dot(dot(spread, values, across), lifted) for values in flat]
    cosine = turn_ref[0]
    sine = turn_ref[1]
    coupled = jnp.concatenate([cosine * real - sine * imag, -(cosine * imag + sine * real)], axis=1)
    mixing[...] = coupled.astype(BF16)
    constant = dot(spread, mode_ref[0, :, 0, :], across)
    bias = bias_ref[...] + middle(stiffness) * lift_ref[2:3, :] + middle(density) * lift_ref[3:4, :]
    offset[...] = jnp.sum(constant * bias, axis=1, keepdims=True)
    height = spread.shape[0]
    widest = wide_ref[0:channels, :]
    repeated = dot(dot(spread, local_ref[...].astype(F32), across), widest)
    pointwise[...] = (repeated * wide_ref[channels : channels + height, :]).astype(BF16)
    padded = wide_ref[channels + height :, 0:channels]
    lift_table[:, 0:FIELDS] = dot(padded, lift_ref[...], across)
    lift_table[:, FIELDS : FIELDS + 1] = dot(padded, bias_ref[...], across)
    lift_table[:, FIELDS + 1 :] = jnp.zeros_like(lift_table[:, FIELDS + 1 :])


def widen_body(mixing, repeat_ref, out):
    rows, span = repeat_ref.shape[0], mixing.shape[1]
    count = rows // mixing.shape[0]
    values = jnp.dot(repeat_ref[...], mixing[...], preferred_element_type=F32)
    column = lax.broadcasted_iota(jnp.int32, (rows, span), 0) % count
    parts = [jnp.where(column == index, values, 0.0) for index in range(count)]
    out[...] = jnp.concatenate(parts, axis=1).astype(BF16)


def pointwise_body(stiffness_in, density_in, p_ref, q_ref, p_mate, q_mate, cells, lift_ref, left, offset, *rest):
    out, right, stiffness, density, semaphores = rest[-5:]
    rows, group, depth = p_ref.shape
    padded_channels = lift_ref.shape[0]
    height = rows * padded_channels
    entries = stiffness.shape[0]
    core = lax.axis_index("gz")
    own = slot() == core

    @pl.when(pl.program_id(0) == 0)
    def _():
        right[...] = jnp.zeros_like(right)
        for copy in begin((stiffness_in, density_in), (stiffness, density), semaphores):
            copy.wait()

    weights = [lift_ref[:, index : index + 1] for index in range(FIELDS + 1)]
    values = []
    for row in range(rows):
        cell = cells[core * rows + row]
        values.append((
            jnp.where(own, p_ref[row], p_mate[row]),
            jnp.where(own, q_ref[row], q_mate[row]),
            looked_up(cell, lambda e: stiffness[e], entries),
            looked_up(cell, lambda e: density[e], entries),
        ))
    for y in range(group):
        lifted = []
        for row in range(rows):
            total = jnp.broadcast_to(weights[FIELDS], (padded_channels, depth))
            for value, weight in zip(values[row], weights):
                total = total + value[y : y + 1, :] * weight
            lifted.append(total)
        right[y, 0:height, :] = jnp.concatenate(lifted, axis=0).astype(BF16)
        out[:, y, :] = jnp.dot(left[...], right[y], preferred_element_type=F32) + offset[...]


def join_body(own, other, wave_out):
    core = lax.axis_index("gz")
    rows, _, depth = own.shape
    half = depth // 2
    place = slot()
    for row in range(rows):
        for ref, start in ((own, place * rows), (other, (1 - place) * rows)):
            wave_out[start + row] = jnp.where(core == 0, ref[row, :, :half], ref[row, :, half:])


def output_body(
    mine, other, local, left, table_y, table_z, features, modes, right,
):
    step = pl.program_id(0)
    core, column = lax.axis_index("gz"), lax.axis_index("gy")
    half_x, modes_y, width = mine.shape[1:]
    modes_x = 2 * half_x
    half = width // 2
    rows, channels, group, depth = features.shape
    coupled = FIELDS * modes_x

    @pl.when(step == 0)
    def _():
        chunk = min(8, modes_x)
        left_y = table_y[column]
        for field in range(FIELDS):
            for start in range(0, modes_x, chunk):
                parts = [[], []]
                for mode in range(start, start + chunk):
                    at = (field, mode % half_x)
                    value = jnp.where(core == mode // half_x, mine[at], other[at].astype(F32))
                    parts[0].append(value.astype(BF16))
                    parts[1].append(turned(value, half, -1.0).astype(BF16))
                stacked = jnp.concatenate([jnp.concatenate(part, axis=1) for part in parts], axis=0)
                result = jnp.dot(left_y, stacked, preferred_element_type=F32)
                for mode in range(start, start + chunk):
                    lanes = slice((mode - start) * width, (mode - start + 1) * width)
                    modes[:, mode * FIELDS + field, :] = result[:, lanes]

    base = pl.multiple_of(step * group, group)
    lines = modes[pl.ds(base, group)].reshape(group * coupled, width).astype(BF16)
    waves = jnp.dot(lines, table_z[...], preferred_element_type=F32).astype(BF16)
    count = left.shape[1] // (2 * coupled)
    for y in range(group):
        lines = slice(y * coupled, (y + 1) * coupled)
        start = y * 2 * coupled
        right[start : start + coupled, :] = waves[lines, :depth]
        right[start + coupled : start + 2 * coupled, :] = waves[lines, depth:]
    for first in range(0, group, 2 * count):
        results = []
        for start in (first * 2 * coupled, (first + count) * 2 * coupled):
            results.append(jnp.dot(
                left[...], right[start : start + count * 2 * coupled, :], preferred_element_type=F32
            ))
        for row in range(rows):
            for channel in range(channels):
                at = row * channels + channel
                total = jnp.concatenate([result[at * count : (at + 1) * count] for result in results], axis=0)
                total = total + local[at, pl.ds(base + first, 2 * count), :]
                scale = math.sqrt(2.0 / math.pi)
                inner = total * (scale + (scale * 0.044715) * (total * total))
                part = 0.5 * total
                total = part + part * jnp.tanh(inner)
                features[row, channel, first : first + 2 * count, :] = total.astype(BF16)


def xor_pairs(count, distance):
    return [(index, index ^ distance) for index in range(count)]


def odd_pairs(count):
    pairs = [(index, index + 1) for index in range(1, count - 1, 2)]
    return pairs + [(target, source) for source, target in pairs]


def row_pairs(cycles, columns):
    place = lambda cycle, column, core: (cycle * columns + column) * 2 + core
    pairs = []
    for column in range(columns):
        for cycle in range(cycles - 1):
            one, two = place(cycle, column, 1 - cycle % 2), place(cycle + 1, column, 1 - cycle % 2)
            pairs += [(one, two), (two, one)]
        for cycle, core in ((0, 0), (cycles - 1, 1 - (cycles - 1) % 2)):
            pairs.append((place(cycle, column, core), place(cycle, column ^ 1, core)))
    return pairs


def per_device(
    pressure,
    previous,
    material,
    stiffness,
    density,
    nonlinear,
    lift_weight,
    lift_bias,
    mode_weight,
    local_weight,
):
    brick_x, brick_y, brick_z = pressure.shape
    cycle_count = lax.axis_size("gx")
    column_count = lax.axis_size("gy")
    core_count = lax.axis_size("gz")
    total_x = brick_x * cycle_count
    total_y = brick_y * column_count
    total_z = brick_z * core_count
    modes_x = total_x // 4
    modes_y = total_y // 4
    modes_z = total_z // 4
    width = 2 * modes_z
    channels = lift_bias.shape[0]
    rows = brick_x // core_count
    assert core_count == 2 and rows >= REACH
    blocks = cycle_count * core_count
    padded_channels = -(-channels // 8) * 8
    height = rows * channels
    coupled = FIELDS * modes_x
    right_depth = -(-rows * padded_channels // 128) * 128
    two_sided = column_count > 2

    kept_first = kept_modes(total_x, modes_x)
    kept_second = kept_modes(total_y, modes_y)
    kept_third = np.arange(modes_z)
    cz, sz = cos_sin(np.arange(total_z), kept_third, total_z)
    forward_z = np.concatenate([cz, -sz], 1)
    weight = np.where(kept_third == 0, 1.0, 2.0) / (total_x * total_y * total_z)
    wc, ws = [rounded((t.astype(np.float32) * weight).T.astype(np.float32)) for t in (cz, sz)]
    inverse_z = np.concatenate(
        [np.concatenate([wc, ws], 1), np.concatenate([-ws.astype(np.float32), wc.astype(np.float32)], 1)], 0
    )
    inverse_z = rounded(inverse_z)
    cy, sy = cos_sin(kept_second, np.arange(total_y), total_y)
    cy3, sy3 = [t.reshape(modes_y, column_count, brick_y).transpose(1, 0, 2) for t in (cy, sy)]
    forward_y = np.concatenate([cy3, sy3, cy3, sy3], 2)
    cy3, sy3 = [t.transpose(0, 2, 1) for t in (cy3, sy3)]
    inverse_y = np.concatenate([cy3, sy3], 2)
    cx, sx = [t.astype(np.float32) for t in cos_sin(np.arange(total_x), kept_first, total_x)]
    twiddle_x = np.stack([cx, sx], -1).reshape(-1)
    owner = np.tile(np.eye(channels, dtype=np.float32), (rows, 1))
    turn = np.zeros((blocks, 2, height, coupled), np.float32)
    for source, table in enumerate((cx, sx)):
        turn[:, source] = np.repeat(
            np.repeat(table.reshape(blocks, rows, modes_x), channels, 1), FIELDS, 2
        )
    padded_eye = np.eye(channels, padded_channels, dtype=np.float32)
    wide = np.zeros((channels + height + padded_channels, right_depth), np.float32)
    wide[:channels, : rows * padded_channels] = np.tile(padded_eye, (1, rows))
    wide[channels : channels + height, : rows * padded_channels] = np.kron(
        np.eye(rows), np.ones((channels, padded_channels))
    )
    wide[channels + height :, :channels] = padded_eye.T
    spread = np.repeat(np.eye(channels, dtype=np.float32), modes_x, 0)
    same = np.tile(np.repeat(np.eye(modes_x, dtype=np.float32), FIELDS, 1), (channels, 1))
    spread = np.concatenate([spread, same], 1)
    place = np.tile(np.eye(FIELDS, dtype=np.float32), (1, modes_x))

    def shape(*dims, dtype=F32):
        return jax.ShapeDtypeStruct(dims, dtype)

    cells_count = rows * brick_y * total_z
    field = shape(rows, brick_y, total_z)
    edge = [shape(rows, EDGE, total_z)] * (2 if two_sided else 1)

    swap_core = xor_pairs(core_count, 1)
    got = [lax.ppermute(array, "gz", swap_core) for array in (pressure, previous, material)]
    sending = shape(rows, brick_y, total_z, dtype=BF16)
    current, before, ratio, bend, sent, cells, *edge_values = call(
        lambda *refs: assemble_body(len(edge), *refs),
        [field] * 4 + [sending, shape(brick_x, brick_y, total_z, dtype=jnp.int32)] + edge, [HBM] * 6 + [VMEM] * 3,
        [pltpu.SMEM(stiffness.shape, F32)] * 3 + [pltpu.VMEM((rows, brick_y, brick_z), F32)] * 2
        + [pltpu.VMEM((brick_x, brick_y, brick_z), jnp.int32), pltpu.SemaphoreType.DMA((6,))], moved=cells_count * 36
    )(*here(stiffness, density, nonlinear, pressure, previous, material), *got)

    weights = (
        stiffness, density, mode_weight.transpose(0, 2, 1, 3), lift_weight, lift_bias.reshape(1, channels),
        local_weight, spread, place, owner, turn, wide,
    )
    mixing, pointwise, lift_table, offset = call(
        prepare_body,
        [shape(height, 2 * coupled, dtype=BF16), shape(height, right_depth, dtype=BF16),
         shape(padded_channels, 8), shape(height, 1)],
        [HBM] * 11, room(*weights[:9], turn[0], wide), flops=2_000_000_000, moved=4_000_000,
    )(*here(*weights))

    part = lambda fields, dtype: shape(fields, modes_x // 2, modes_y, width, dtype=dtype)

    def spectrum(body, outs, inputs, lines, specs=None, scratch=()):
        return call(
            body, outs, specs or [HBM] + [VMEM] * (inputs + 2),
            [pltpu.VMEM((4 * brick_y, lines * width), BF16), pltpu.VMEM((modes_y, lines * width), F32), *scratch],
            flops=cells_count * 256 * lines, moved=cells_count * 2 * lines,
        )

    stages = [(axis, count, 2 ** (bit + 1) - 1) for axis, count in (("gy", column_count), ("gx", cycle_count))
              for bit in range((count - 1).bit_length())]
    swap = lambda value: lax.ppermute(value, "gz", swap_core)

    def exchange(value, axis, count, distance):
        return lax.ppermute(value.astype(BF16), axis, xor_pairs(count, distance))

    tables = (twiddle_x, stiffness, density, forward_z, forward_y)
    early, forward_z, forward_y = spectrum(
        materials_body,
        [part(2, F32)] + [jax.ShapeDtypeStruct(table.shape, table.dtype) for table in (forward_z, forward_y)],
        1, 2 * brick_x, [HBM] * 5 + [VMEM], room(*tables[:3])[:3] + [pltpu.SemaphoreType.DMA((5,))],
    )(*here(*tables), cells)
    twiddles = here(twiddle_x)
    twiddle_room = room(twiddle_x)

    for repeat in range(STEPS):
        last = repeat == STEPS - 1
        far = lax.ppermute(sent, ("gx", "gy", "gz"), row_pairs(cycle_count, column_count))
        mate = swap(current)
        halos = [lax.ppermute(edge_values[0], "gy", xor_pairs(column_count, 1))]
        if two_sided:
            halos.append(lax.ppermute(edge_values[1], "gy", odd_pairs(column_count)))
        if repeat == 0:
            far, early = lax.optimization_barrier((far, early))
        if repeat == 2:
            repeats = np.repeat(np.eye(height), 8, 0).astype(ml_dtypes.bfloat16)
            wide_mixing = call(
                widen_body, shape(height * 8, 16 * coupled, dtype=BF16), [VMEM] * 2, flops=1_000_000_000, moved=2_000_000
            )(mixing, repeats)
            far, wide_mixing = lax.optimization_barrier((far, wide_mixing))
        if repeat == 1:
            far, mixing, pointwise, lift_table, offset = lax.optimization_barrier(
                (far, mixing, pointwise, lift_table, offset)
            )
        if last:
            prior = spectrum(prior_body, shape(modes_x // 2, modes_y, width), 2, brick_x, None, twiddle_room)(
                *twiddles, current, mate, forward_z, forward_y
            )
            far, prior = lax.optimization_barrier((far, prior))
            prior_mate = mate
        outs = [field] + ([] if last else [sending] + edge)
        body = lambda *refs, last=last: step_body(two_sided, last, *refs)
        new, *others = call(
            body, outs, [VMEM] * (6 + len(halos)),
            [pltpu.VMEM((brick_y + 2 * EDGE, total_z), F32)], flops=cells_count * 60, moved=cells_count * 28,
        )(current, before, ratio, bend, mate, far, *halos)
        if not last:
            sent, *edge_values = others
        current, before = new, current

    total, sent = spectrum(wave_body, [part(FIELDS, F32), part(1, BF16)], 3, rows, None, twiddle_room)(
        *twiddles, current, prior, early, forward_z, forward_y
    )
    total = total + jnp.pad(swap(sent).astype(F32), ((0, FIELDS - 1), (0, 0), (0, 0), (0, 0)))
    wave_other = swap(current)
    group = 8
    steps = brick_y // group
    whole = lambda array: pl.BlockSpec(array.shape, lambda i: (0,) * len(array.shape))

    def pointwise_part(start, held=()):
        slab = lambda count: pl.BlockSpec((count, group, total_z), lambda i: (0, i + start, 0))
        return pl.pallas_call(
            pointwise_body,
            grid=(steps // 2,),
            out_shape=shape(height, brick_y, total_z),
            in_specs=[HBM] * 2 + [slab(rows)] * 4 + [slab(brick_x), whole(lift_table), whole(pointwise), whole(offset)]
            + [pl.BlockSpec(memory_space=pl.ANY)] * len(held),
            out_specs=pl.BlockSpec((height, group, total_z), lambda i: (0, i + start, 0)),
            input_output_aliases={10: 0} if held else {},
            scratch_shapes=[pltpu.VMEM((group, right_depth, total_z), BF16)] + room(stiffness, density),
            compiler_params=pltpu.CompilerParams(vmem_limit_bytes=16 * 1024 * 1024),
            cost_estimate=pl.CostEstimate(flops=cells_count * 20000, bytes_accessed=cells_count * 50, transcendentals=0),
        )(*here(stiffness, density), current, before, wave_other, prior_mate, cells, lift_table, pointwise, offset, *held)

    for index, stage in enumerate(stages):
        arrived = exchange(total, *stage)
        if index == len(stages) - 2:
            local = pointwise_part(0)
            wave = call(join_body, shape(*pressure.shape), [VMEM] * 2, moved=cells_count * 12)(current, wave_other)
            arrived, local, wave = lax.optimization_barrier((arrived, local, wave))
        if index == len(stages) - 1:
            local = pointwise_part(steps // 2, (local,))
            arrived, local = lax.optimization_barrier((arrived, local))
        total = total + arrived.astype(F32)
    other = swap(total.astype(BF16))
    batch = min(32, brick_y)
    scoped = 10 * 2**20 + 20 * height * 16 * coupled + 4 * (brick_y * coupled * width + 6 * batch * coupled * total_z)
    features = pl.pallas_call(
        output_body,
        grid=(brick_y // batch,),
        out_shape=shape(rows, channels, brick_y, total_z, dtype=BF16),
        in_specs=[VMEM, VMEM,
                  VMEM, VMEM, VMEM, VMEM],
        out_specs=pl.BlockSpec((rows, channels, batch, total_z), lambda i: (0, 0, i, 0)),
        scratch_shapes=[
            pltpu.VMEM((brick_y, coupled, width), F32),
            pltpu.VMEM((batch * 2 * coupled, total_z), BF16),
        ],
        compiler_params=pltpu.CompilerParams(vmem_limit_bytes=scoped),
        cost_estimate=pl.CostEstimate(flops=cells_count * 2000, bytes_accessed=cells_count * 60, transcendentals=cells_count * 20),
    )(total, other, local, wide_mixing, inverse_y, inverse_z)
    features = features.transpose(0, 2, 1, 3)
    return (wave, features)


def solution(mesh):
    placed = (
        P(("grp", "gx"), "gy", "gz"),
        P(("grp", "gx"), "gy", "gz"),
        P(("grp", "gx"), "gy", "gz"),
        P(),
        P(),
        P(),
        P(),
        P(),
        P(),
        P(),
    )
    return jax.shard_map(
        per_device,
        mesh=mesh,
        in_specs=placed,
        out_specs=(P(("grp", "gx"), "gy", "gz"), P(("grp", "gx", "gz"), "gy", None, None)),
        check_vma=False,
    )
```

```python
import math

import numpy as np
import jax
import jax.numpy as jnp
from jax import lax
from jax.experimental import pallas as pl
from jax.experimental.pallas import tpu as pltpu
from jax.sharding import PartitionSpec as P
import ml_dtypes

STEPS = 4
FIELDS = 4
REACH = 4
EDGE = 8
stencil_taps = (-205.0 / 72.0, 8.0 / 5.0, -1.0 / 5.0, 8.0 / 315.0, -1.0 / 560.0)
F32 = jnp.float32
BF16 = jnp.bfloat16
HIGHEST = lax.Precision.HIGHEST

VMEM = pl.BlockSpec(memory_space=pltpu.VMEM)
SMEM = pl.BlockSpec(memory_space=pltpu.SMEM)
HBM = pl.BlockSpec(memory_space=pltpu.HBM)


def rounded(table):
    return table.astype(ml_dtypes.bfloat16)


def kept_modes(length, mode_count):
    position = np.arange(mode_count)
    return np.where(position < mode_count // 2, position, length - mode_count + position)


def cos_sin(source, target, length):
    product = (source[:, None] * target[None, :]) % length
    phases = np.float32(2.0 * math.pi / length) * product.astype(np.float32)
    return rounded(np.cos(phases)), rounded(np.sin(phases))


def call(body, outs, in_specs, scratch=(), flops=0, moved=0):
    return pl.pallas_call(
        body,
        out_shape=outs,
        in_specs=in_specs,
        out_specs=jax.tree.map(lambda _: VMEM, outs),
        scratch_shapes=list(scratch),
        compiler_params=pltpu.CompilerParams(vmem_limit_bytes=16 * 1024 * 1024),
        cost_estimate=pl.CostEstimate(flops=flops, bytes_accessed=moved, transcendentals=0),
    )


def begin(sources, targets, semaphores):
    copies = [
        pltpu.make_async_copy(source, target, semaphores.at[index])
        for index, (source, target) in enumerate(zip(sources, targets))
    ]
    for copy in copies:
        copy.start()
    return copies


def here(*arrays):
    return [pltpu.with_memory_space_constraint(jnp.asarray(array), pltpu.HBM) for array in arrays]


def room(*arrays):
    return [(pltpu.SMEM if array.ndim == 1 else pltpu.VMEM)(array.shape, array.dtype) for array in arrays] + [
        pltpu.SemaphoreType.DMA((len(arrays),))
    ]


def high_low(value):
    high = value.astype(BF16)
    return high, (value - high.astype(F32)).astype(BF16)


def turned(value, half, sign):
    lane = lax.broadcasted_iota(jnp.int32, value.shape, value.ndim - 1)
    swapped = pltpu.roll(value, half, value.ndim - 1)
    return jnp.where(lane < half, sign * swapped, -sign * swapped)


def looked_up(material, table, entries):
    result = jnp.full(material.shape, table(0), F32)
    for entry in range(1, entries):
        result = jnp.where(material == entry, table(entry), result)
    return result


def middle(table):
    total = table[0]
    for entry in range(1, table.shape[0]):
        total = total + table[entry]
    return total * (1.0 / table.shape[0])


def edges(value_of, outs, row_parity, brick_y):
    for position, out in enumerate(outs):
        upper = row_parity == position
        out[...] = jnp.where(upper, value_of(brick_y - EDGE, brick_y), value_of(0, EDGE))


def slot():
    return (lax.axis_index("gz") + lax.axis_index("gx")) % 2


def fetch_body(*refs):
    tables_in, own_in = refs[:3], refs[3:6]
    p_out, q_out, m_out = refs[6:9]
    tables_out = refs[9]
    tables, semaphores = refs[10:13], refs[13]
    rows = p_out.shape[0]
    start = slot() * rows
    sources = [source.at[pl.ds(start, rows)] for source in own_in[:2]] + [own_in[2]]
    copies = begin(list(tables_in) + sources, list(tables) + [p_out, q_out, m_out], semaphores)
    for copy in copies:
        copy.wait()
    stiffness, density, nonlinear = tables
    for entry in range(stiffness.shape[0]):
        tables_out[2 * entry] = jnp.full(tables_out.shape[1:], stiffness[entry] / density[entry], F32)
        tables_out[2 * entry + 1] = jnp.full(tables_out.shape[1:], nonlinear[entry], F32)


def assemble_body(count, *refs):
    own, tables, got = refs[:3], refs[3], refs[4:7]
    p_out, q_out, ratio, bend, sent, cells = refs[7:13]
    edge_outs = refs[13 : 13 + count]
    core, column = lax.axis_index("gz"), lax.axis_index("gy")
    rows, brick_y, depth = p_out.shape
    start = slot() * rows
    entries = tables.shape[0] // 2

    def whole(mine, other):
        return jnp.concatenate(
            [jnp.where(core == 0, mine, other), jnp.where(core == 0, other, mine)], axis=-1
        )

    def chosen(cell, place):
        result = jnp.broadcast_to(tables[place, 0:1, 0:1], cell.shape)
        for entry in range(1, entries):
            result = jnp.where(cell == entry, jnp.broadcast_to(tables[2 * entry + place, 0:1, 0:1], cell.shape), result)
        return result

    for row in range(cells.shape[0]):
        cells[row] = whole(own[2][row], got[2][row])
    for row in range(rows):
        value = whole(own[0][row], got[0][start + row])
        p_out[row] = value
        sent[row] = value.astype(BF16)
        q_out[row] = whole(own[1][row], got[1][start + row])
        cell = cells[start + row]
        ratio[row] = chosen(cell, 0)
        bend[row] = chosen(cell, 1)
    edges(lambda a, b: p_out[:, a:b, :], edge_outs, column % 2, brick_y)


def step_body(two_sided, last, p_ref, q_ref, ratio, bend, mate, far, *rest):
    count = 2 if two_sided else 1
    halos = rest[:count]
    new_ref = rest[count]
    sent = None if last else rest[count + 1]
    edge_outs = rest[count + 2 : -1]
    padded = rest[-1]
    place = slot()
    parity = lax.axis_index("gy") % 2
    rows, brick_y, depth = p_ref.shape
    lane = lax.broadcasted_iota(jnp.int32, (brick_y, depth), 1)
    zero_edge = jnp.zeros((EDGE, depth), F32)

    cycle = lax.axis_index("gx")
    outside = cycle == jnp.where(place == 0, 0, lax.axis_size("gx") - 1)

    def line(index):
        if 0 <= index < rows:
            return p_ref[index]
        at = index % rows
        beyond = jnp.where(outside, 0.0, far[at].astype(F32))
        return jnp.where(place == (0 if index < 0 else 1), beyond, mate[at])

    for row in range(rows):
        first = halos[0][row]
        second = halos[1][row] if two_sided else zero_edge
        center = p_ref[row]
        padded[0:EDGE, :] = jnp.where(parity == 0, second, first)
        padded[EDGE : EDGE + brick_y, :] = center
        padded[EDGE + brick_y :, :] = jnp.where(parity == 0, first, second)
        total = (3.0 * stencil_taps[0]) * center
        for offset in range(1, REACH + 1):
            low, high = EDGE - offset, EDGE + offset
            pair = padded[low : low + brick_y, :] + padded[high : high + brick_y, :]
            pair = pair + (line(row - offset) + line(row + offset))
            pair = pair + jnp.where(lane >= offset, pltpu.roll(center, offset, 1), 0.0)
            pair = pair + jnp.where(
                lane < depth - offset, pltpu.roll(center, depth - offset, 1), 0.0
            )
            total = total + stencil_taps[offset] * pair
        change = center - q_ref[row]
        value = (center + change) + ratio[row] * total + bend[row] * change * change
        new_ref[row] = value
        if not last:
            sent[row] = value.astype(BF16)
    if not last:
        edges(lambda a, b: new_ref[:, a:b, :], edge_outs, parity, brick_y)


def transformed(sources, first, twiddle_x, table_z, table_y, lines, grid, late=()):
    column = lax.axis_index("gy")
    brick_y = lines.shape[0] // 4
    modes_y = grid.shape[0]
    width = table_z.shape[1]
    half = width // 2
    for field, rows in enumerate(sources):
        for row, load in enumerate(rows):
            high, low = high_low(load())
            modes = jnp.dot(high, table_z[...], preferred_element_type=F32)
            modes = modes + jnp.dot(low, table_z[...], preferred_element_type=F32)
            back = turned(modes, half, 1.0)
            high, low = high_low(modes)
            back_high, back_low = high_low(back)
            lanes = slice((field * len(rows) + row) * width, (field * len(rows) + row + 1) * width)
            for index, part in enumerate((high, back_high, low, back_low)):
                lines[index * brick_y : (index + 1) * brick_y, lanes] = part
    grid[...] = jnp.dot(table_y[column], lines[...], preferred_element_type=F32)
    for copy in late:
        copy.wait()

    def at_mode(field, modes_x):
        count = len(sources[field])
        values = [
            grid[:, (field * count + row) * width : (field * count + row + 1) * width] for row in range(count)
        ]
        backs = [turned(value, half, 1.0) for value in values]

        def summed(mode):
            total = jnp.zeros((modes_y, width), F32)
            for row in range(count):
                at = ((first + row) * modes_x + mode) * 2
                total = total + twiddle_x[at] * values[row] + twiddle_x[at + 1] * backs[row]
            return total

        return summed

    return at_mode


def materials_body(*refs):
    sources, cells, keep, table_z, table_y, lines, grid = refs[:5], *refs[5:11]
    twiddle_x, stiffness, density, semaphores = refs[11:15]
    copies = begin(sources, (twiddle_x, stiffness, density, table_z, table_y), semaphores)
    for copy in copies:
        copy.wait()
    half_x = keep.shape[1]
    entries = stiffness.shape[0]
    rows = cells.shape[0]
    sources = []
    for table in (stiffness, density):
        center = middle(table)
        sources.append([
            lambda row=row, table=table, center=center: looked_up(cells[row], lambda e: table[e] - center, entries)
            for row in range(rows)
        ])
    at_mode = transformed(sources, lax.axis_index("gx") * rows, twiddle_x, table_z, table_y, lines, grid)
    core = lax.axis_index("gz")
    for field in range(2):
        summed = at_mode(field, 2 * half_x)

        @pl.loop(0, half_x)
        def _(mode):
            keep[field, mode] = summed(core * half_x + mode)


def prior_body(twiddles, own, mate, table_z, table_y, keep, lines, grid, twiddle_x, semaphores):
    copies = begin((twiddles,), (twiddle_x,), semaphores)
    half_x = keep.shape[0]
    rows = own.shape[0]
    place = slot()
    sources = [
        (lambda row=row: jnp.where(place == 0, own[row], mate[row])) for row in range(rows)
    ] + [(lambda row=row: jnp.where(place == 0, mate[row], own[row])) for row in range(rows)]
    at_mode = transformed([sources], lax.axis_index("gx") * (2 * rows), twiddle_x, table_z, table_y, lines, grid, copies)
    core = lax.axis_index("gz")
    summed = at_mode(0, 2 * half_x)

    @pl.loop(0, half_x)
    def _(mode):
        keep[mode] = summed(core * half_x + mode)


def wave_body(twiddles, own, prior, early, table_z, table_y, keep, send, lines, grid, twiddle_x, semaphores):
    copies = begin((twiddles,), (twiddle_x,), semaphores)
    half_x = keep.shape[1]
    rows = own.shape[0]
    first = (lax.axis_index("gx") * 2 + slot()) * rows
    sources = [(lambda row=row: own[row]) for row in range(rows)]
    at_mode = transformed([sources], first, twiddle_x, table_z, table_y, lines, grid, copies)
    core = lax.axis_index("gz")
    summed = at_mode(0, 2 * half_x)
    keep[1] = prior[...]
    keep[2:4] = early[...]

    @pl.loop(0, half_x)
    def _(mode):
        keep[0, mode] = summed(core * half_x + mode)
        send[0, mode] = summed((1 - core) * half_x + mode).astype(BF16)


def prepare_body(*refs):
    sources, outs, targets, semaphores = refs[:11], refs[11:15], refs[15:26], refs[26]
    mixing, pointwise, lift_table, offset = outs
    block = lax.axis_index("gx") * 2 + lax.axis_index("gz")
    copies = begin([*sources[:9], sources[9].at[block], sources[10]], targets, semaphores)
    for copy in copies:
        copy.wait()
    stiffness, density, mode_ref, lift_ref, bias_ref, local_ref, spread_ref, place_ref, owner_ref, turn_ref, wide_ref = targets
    half = place_ref.shape[1]
    channels = lift_ref.shape[1]
    spread = owner_ref[...]

    def dot(a, b, dims=((1,), (0,))):
        return lax.dot_general(a, b, (dims, ((), ())), precision=HIGHEST, preferred_element_type=F32)

    across = ((1,), (1,))
    lifted = dot(dot(spread_ref[:, :channels], lift_ref[...], across), place_ref[...])
    lifted = lifted * spread_ref[:, channels : channels + half]
    flat = [mode_ref[index].reshape(-1, channels) for index in range(2)]
    real, imag = [dot(dot(spread, values, across), lifted) for values in flat]
    cosine = turn_ref[0]
    sine = turn_ref[1]
    coupled = jnp.concatenate([cosine * real - sine * imag, -(cosine * imag + sine * real)], axis=1)
    mixing[...] = coupled.astype(BF16)
    constant = dot(spread, mode_ref[0, :, 0, :], across)
    bias = bias_ref[...] + middle(stiffness) * lift_ref[2:3, :] + middle(density) * lift_ref[3:4, :]
    offset[...] = jnp.sum(constant * bias, axis=1, keepdims=True)
    height = spread.shape[0]
    widest = wide_ref[0:channels, :]
    repeated = dot(dot(spread, local_ref[...].astype(F32), across), widest)
    pointwise[...] = (repeated * wide_ref[channels : channels + height, :]).astype(BF16)
    padded = wide_ref[channels + height :, 0:channels]
    lift_table[:, 0:FIELDS] = dot(padded, lift_ref[...], across)
    lift_table[:, FIELDS : FIELDS + 1] = dot(padded, bias_ref[...], across)
    lift_table[:, FIELDS + 1 :] = jnp.zeros_like(lift_table[:, FIELDS + 1 :])


def widen_body(mixing, repeat_ref, out):
    rows, span = repeat_ref.shape[0], mixing.shape[1]
    count = rows // mixing.shape[0]
    values = jnp.dot(repeat_ref[...], mixing[...], preferred_element_type=F32)
    column = lax.broadcasted_iota(jnp.int32, (rows, span), 0) % count
    parts = [jnp.where(column == index, values, 0.0) for index in range(count)]
    out[...] = jnp.concatenate(parts, axis=1).astype(BF16)


def pointwise_body(stiffness_in, density_in, p_ref, q_ref, p_mate, q_mate, cells, lift_ref, left, offset, *rest):
    out, right, stiffness, density, semaphores = rest[-5:]
    rows, group, depth = p_ref.shape
    padded_channels = lift_ref.shape[0]
    height = rows * padded_channels
    entries = stiffness.shape[0]
    core = lax.axis_index("gz")
    own = slot() == core

    @pl.when(pl.program_id(0) == 0)
    def _():
        right[...] = jnp.zeros_like(right)
        for copy in begin((stiffness_in, density_in), (stiffness, density), semaphores):
            copy.wait()

    weights = [lift_ref[:, index : index + 1] for index in range(FIELDS + 1)]
    values = []
    for row in range(rows):
        cell = cells[core * rows + row]
        values.append((
            jnp.where(own, p_ref[row], p_mate[row]),
            jnp.where(own, q_ref[row], q_mate[row]),
            looked_up(cell, lambda e: stiffness[e], entries),
            looked_up(cell, lambda e: density[e], entries),
        ))
    for y in range(group):
        lifted = []
        for row in range(rows):
            total = jnp.broadcast_to(weights[FIELDS], (padded_channels, depth))
            for value, weight in zip(values[row], weights):
                total = total + value[y : y + 1, :] * weight
            lifted.append(total)
        right[y, 0:height, :] = jnp.concatenate(lifted, axis=0).astype(BF16)
        out[:, y, :] = jnp.dot(left[...], right[y], preferred_element_type=F32) + offset[...]


def join_body(own, other, wave_out):
    core = lax.axis_index("gz")
    rows, _, depth = own.shape
    half = depth // 2
    place = slot()
    for row in range(rows):
        for ref, start in ((own, place * rows), (other, (1 - place) * rows)):
            wave_out[start + row] = jnp.where(core == 0, ref[row, :, :half], ref[row, :, half:])


def output_body(
    mine, other, local, left, table_y, table_z, features, modes, right,
):
    step = pl.program_id(0)
    core, column = lax.axis_index("gz"), lax.axis_index("gy")
    half_x, modes_y, width = mine.shape[1:]
    modes_x = 2 * half_x
    half = width // 2
    rows, channels, group, depth = features.shape
    coupled = FIELDS * modes_x

    @pl.when(step == 0)
    def _():
        chunk = min(8, modes_x)
        left_y = table_y[column]
        for field in range(FIELDS):
            for start in range(0, modes_x, chunk):
                parts = [[], []]
                for mode in range(start, start + chunk):
                    at = (field, mode % half_x)
                    value = jnp.where(core == mode // half_x, mine[at], other[at].astype(F32))
                    parts[0].append(value.astype(BF16))
                    parts[1].append(turned(value, half, -1.0).astype(BF16))
                stacked = jnp.concatenate([jnp.concatenate(part, axis=1) for part in parts], axis=0)
                result = jnp.dot(left_y, stacked, preferred_element_type=F32)
                for mode in range(start, start + chunk):
                    lanes = slice((mode - start) * width, (mode - start + 1) * width)
                    modes[:, mode * FIELDS + field, :] = result[:, lanes]

    base = pl.multiple_of(step * group, group)
    lines = modes[pl.ds(base, group)].reshape(group * coupled, width).astype(BF16)
    waves = jnp.dot(lines, table_z[...], preferred_element_type=F32).astype(BF16)
    count = left.shape[1] // (2 * coupled)
    for y in range(group):
        lines = slice(y * coupled, (y + 1) * coupled)
        start = y * 2 * coupled
        right[start : start + coupled, :] = waves[lines, :depth]
        right[start + coupled : start + 2 * coupled, :] = waves[lines, depth:]
    for first in range(0, group, 2 * count):
        results = []
        for start in (first * 2 * coupled, (first + count) * 2 * coupled):
            results.append(jnp.dot(
                left[...], right[start : start + count * 2 * coupled, :], preferred_element_type=F32
            ))
        for row in range(rows):
            for channel in range(channels):
                at = row * channels + channel
                total = jnp.concatenate([result[at * count : (at + 1) * count] for result in results], axis=0)
                total = total + local[at, pl.ds(base + first, 2 * count), :]
                scale = math.sqrt(2.0 / math.pi)
                inner = total * (scale + (scale * 0.044715) * (total * total))
                part = 0.5 * total
                total = part + part * jnp.tanh(inner)
                features[row, channel, first : first + 2 * count, :] = total.astype(BF16)


def xor_pairs(count, distance):
    return [(index, index ^ distance) for index in range(count)]


def odd_pairs(count):
    pairs = [(index, index + 1) for index in range(1, count - 1, 2)]
    return pairs + [(target, source) for source, target in pairs]


def row_pairs(cycles, columns):
    place = lambda cycle, column, core: (cycle * columns + column) * 2 + core
    pairs = []
    for column in range(columns):
        for cycle in range(cycles - 1):
            one, two = place(cycle, column, 1 - cycle % 2), place(cycle + 1, column, 1 - cycle % 2)
            pairs += [(one, two), (two, one)]
        for cycle, core in ((0, 0), (cycles - 1, 1 - (cycles - 1) % 2)):
            pairs.append((place(cycle, column, core), place(cycle, column ^ 1, core)))
    return pairs


def per_device(
    pressure,
    previous,
    material,
    stiffness,
    density,
    nonlinear,
    lift_weight,
    lift_bias,
    mode_weight,
    local_weight,
):
    brick_x, brick_y, brick_z = pressure.shape
    cycle_count = lax.axis_size("gx")
    column_count = lax.axis_size("gy")
    core_count = lax.axis_size("gz")
    total_x = brick_x * cycle_count
    total_y = brick_y * column_count
    total_z = brick_z * core_count
    modes_x = total_x // 4
    modes_y = total_y // 4
    modes_z = total_z // 4
    width = 2 * modes_z
    channels = lift_bias.shape[0]
    rows = brick_x // core_count
    assert core_count == 2 and rows >= REACH
    blocks = cycle_count * core_count
    padded_channels = -(-channels // 8) * 8
    height = rows * channels
    coupled = FIELDS * modes_x
    right_depth = -(-rows * padded_channels // 128) * 128
    two_sided = column_count > 2

    kept_first = kept_modes(total_x, modes_x)
    kept_second = kept_modes(total_y, modes_y)
    kept_third = np.arange(modes_z)
    cz, sz = cos_sin(np.arange(total_z), kept_third, total_z)
    forward_z = np.concatenate([cz, -sz], 1)
    weight = np.where(kept_third == 0, 1.0, 2.0) / (total_x * total_y * total_z)
    wc, ws = [rounded((t.astype(np.float32) * weight).T.astype(np.float32)) for t in (cz, sz)]
    inverse_z = np.concatenate(
        [np.concatenate([wc, ws], 1), np.concatenate([-ws.astype(np.float32), wc.astype(np.float32)], 1)], 0
    )
    inverse_z = rounded(inverse_z)
    cy, sy = cos_sin(kept_second, np.arange(total_y), total_y)
    cy3, sy3 = [t.reshape(modes_y, column_count, brick_y).transpose(1, 0, 2) for t in (cy, sy)]
    forward_y = np.concatenate([cy3, sy3, cy3, sy3], 2)
    cy3, sy3 = [t.transpose(0, 2, 1) for t in (cy3, sy3)]
    inverse_y = np.concatenate([cy3, sy3], 2)
    cx, sx = [t.astype(np.float32) for t in cos_sin(np.arange(total_x), kept_first, total_x)]
    twiddle_x = np.stack([cx, sx], -1).reshape(-1)
    owner = np.tile(np.eye(channels, dtype=np.float32), (rows, 1))
    turn = np.zeros((blocks, 2, height, coupled), np.float32)
    for source, table in enumerate((cx, sx)):
        turn[:, source] = np.repeat(
            np.repeat(table.reshape(blocks, rows, modes_x), channels, 1), FIELDS, 2
        )
    padded_eye = np.eye(channels, padded_channels, dtype=np.float32)
    wide = np.zeros((channels + height + padded_channels, right_depth), np.float32)
    wide[:channels, : rows * padded_channels] = np.tile(padded_eye, (1, rows))
    wide[channels : channels + height, : rows * padded_channels] = np.kron(
        np.eye(rows), np.ones((channels, padded_channels))
    )
    wide[channels + height :, :channels] = padded_eye.T
    spread = np.repeat(np.eye(channels, dtype=np.float32), modes_x, 0)
    same = np.tile(np.repeat(np.eye(modes_x, dtype=np.float32), FIELDS, 1), (channels, 1))
    spread = np.concatenate([spread, same], 1)
    place = np.tile(np.eye(FIELDS, dtype=np.float32), (1, modes_x))

    def shape(*dims, dtype=F32):
        return jax.ShapeDtypeStruct(dims, dtype)

    cells_count = rows * brick_y * total_z
    field = shape(rows, brick_y, total_z)
    edge = [shape(rows, EDGE, total_z)] * (2 if two_sided else 1)

    swap_core = xor_pairs(core_count, 1)
    got = [lax.ppermute(array, "gz", swap_core) for array in (pressure, previous, material)]
    sending = shape(rows, brick_y, total_z, dtype=BF16)
    half = (rows, brick_y, brick_z)
    fetched = call(
        fetch_body,
        [shape(*half), shape(*half), shape(brick_x, brick_y, brick_z, dtype=jnp.int32), shape(2 * stiffness.shape[0], 8, 128)],
        [HBM] * 6, [pltpu.SMEM(stiffness.shape, F32)] * 3 + [pltpu.SemaphoreType.DMA((6,))], moved=cells_count * 8
    )(*here(stiffness, density, nonlinear, pressure, previous, material))
    fetched, got = lax.optimization_barrier((fetched, got))
    current, before, ratio, bend, sent, cells, *edge_values = call(
        lambda *refs: assemble_body(len(edge), *refs),
        [field] * 4 + [sending, shape(brick_x, brick_y, total_z, dtype=jnp.int32)] + edge, [VMEM] * 7,
        moved=cells_count * 36
    )(*fetched, *got)

    weights = (
        stiffness, density, mode_weight.transpose(0, 2, 1, 3), lift_weight, lift_bias.reshape(1, channels),
        local_weight, spread, place, owner, turn, wide,
    )
    mixing, pointwise, lift_table, offset = call(
        prepare_body,
        [shape(height, 2 * coupled, dtype=BF16), shape(height, right_depth, dtype=BF16),
         shape(padded_channels, 8), shape(height, 1)],
        [HBM] * 11, room(*weights[:9], turn[0], wide), flops=2_000_000_000, moved=4_000_000,
    )(*here(*weights))

    part = lambda fields, dtype: shape(fields, modes_x // 2, modes_y, width, dtype=dtype)

    def spectrum(body, outs, inputs, lines, specs=None, scratch=()):
        return call(
            body, outs, specs or [HBM] + [VMEM] * (inputs + 2),
            [pltpu.VMEM((4 * brick_y, lines * width), BF16), pltpu.VMEM((modes_y, lines * width), F32), *scratch],
            flops=cells_count * 256 * lines, moved=cells_count * 2 * lines,
        )

    stages = [(axis, count, 2 ** (bit + 1) - 1) for axis, count in (("gy", column_count), ("gx", cycle_count))
              for bit in range((count - 1).bit_length())]
    swap = lambda value: lax.ppermute(value, "gz", swap_core)

    def exchange(value, axis, count, distance):
        return lax.ppermute(value.astype(BF16), axis, xor_pairs(count, distance))

    tables = (twiddle_x, stiffness, density, forward_z, forward_y)
    early, forward_z, forward_y = spectrum(
        materials_body,
        [part(2, F32)] + [jax.ShapeDtypeStruct(table.shape, table.dtype) for table in (forward_z, forward_y)],
        1, 2 * brick_x, [HBM] * 5 + [VMEM], room(*tables[:3])[:3] + [pltpu.SemaphoreType.DMA((5,))],
    )(*here(*tables), cells)
    twiddles = here(twiddle_x)
    twiddle_room = room(twiddle_x)

    for repeat in range(STEPS):
        last = repeat == STEPS - 1
        far = lax.ppermute(sent, ("gx", "gy", "gz"), row_pairs(cycle_count, column_count))
        mate = swap(current)
        halos = [lax.ppermute(edge_values[0], "gy", xor_pairs(column_count, 1))]
        if two_sided:
            halos.append(lax.ppermute(edge_values[1], "gy", odd_pairs(column_count)))
        if repeat == 0:
            far, early = lax.optimization_barrier((far, early))
        if last:
            prior = spectrum(prior_body, shape(modes_x // 2, modes_y, width), 2, brick_x, None, twiddle_room)(
                *twiddles, current, mate, forward_z, forward_y
            )
            far, prior = lax.optimization_barrier((far, prior))
            prior_mate = mate
        outs = [field] + ([] if last else [sending] + edge)
        body = lambda *refs, last=last: step_body(two_sided, last, *refs)
        new, *others = call(
            body, outs, [VMEM] * (6 + len(halos)),
            [pltpu.VMEM((brick_y + 2 * EDGE, total_z), F32)], flops=cells_count * 60, moved=cells_count * 28,
        )(current, before, ratio, bend, mate, far, *halos)
        if not last:
            sent, *edge_values = others
        current, before = new, current

    total, sent = spectrum(wave_body, [part(FIELDS, F32), part(1, BF16)], 3, rows, None, twiddle_room)(
        *twiddles, current, prior, early, forward_z, forward_y
    )
    total = total + jnp.pad(swap(sent).astype(F32), ((0, FIELDS - 1), (0, 0), (0, 0), (0, 0)))
    wave_other = swap(current)
    group = 8
    steps = brick_y // group
    whole = lambda array: pl.BlockSpec(array.shape, lambda i: (0,) * len(array.shape))

    def pointwise_part(start, held=()):
        slab = lambda count: pl.BlockSpec((count, group, total_z), lambda i: (0, i + start, 0))
        return pl.pallas_call(
            pointwise_body,
            grid=(steps // 2,),
            out_shape=shape(height, brick_y, total_z),
            in_specs=[HBM] * 2 + [slab(rows)] * 4 + [slab(brick_x), whole(lift_table), whole(pointwise), whole(offset)]
            + [pl.BlockSpec(memory_space=pl.ANY)] * len(held),
            out_specs=pl.BlockSpec((height, group, total_z), lambda i: (0, i + start, 0)),
            input_output_aliases={10: 0} if held else {},
            scratch_shapes=[pltpu.VMEM((group, right_depth, total_z), BF16)] + room(stiffness, density),
            compiler_params=pltpu.CompilerParams(vmem_limit_bytes=16 * 1024 * 1024),
            cost_estimate=pl.CostEstimate(flops=cells_count * 20000, bytes_accessed=cells_count * 50, transcendentals=0),
        )(*here(stiffness, density), current, before, wave_other, prior_mate, cells, lift_table, pointwise, offset, *held)

    for index, stage in enumerate(stages):
        arrived = exchange(total, *stage)
        if index == 0:
            arrived, mixing, pointwise, lift_table, offset = lax.optimization_barrier(
                (arrived, mixing, pointwise, lift_table, offset)
            )
        if index == len(stages) - 2:
            local = pointwise_part(0)
            wave = call(join_body, shape(*pressure.shape), [VMEM] * 2, moved=cells_count * 12)(current, wave_other)
            arrived, local, wave = lax.optimization_barrier((arrived, local, wave))
        if index == len(stages) - 1:
            local = pointwise_part(steps // 2, (local,))
            repeats = np.repeat(np.eye(height), 8, 0).astype(ml_dtypes.bfloat16)
            wide_mixing = call(
                widen_body, shape(height * 8, 16 * coupled, dtype=BF16), [VMEM] * 2, flops=1_000_000_000, moved=2_000_000
            )(mixing, repeats)
            arrived, local, wide_mixing = lax.optimization_barrier((arrived, local, wide_mixing))
        total = total + arrived.astype(F32)
    other = swap(total.astype(BF16))
    batch = min(32, brick_y)
    scoped = 10 * 2**20 + 20 * height * 16 * coupled + 4 * (brick_y * coupled * width + 6 * batch * coupled * total_z)
    features = pl.pallas_call(
        output_body,
        grid=(brick_y // batch,),
        out_shape=shape(rows, channels, brick_y, total_z, dtype=BF16),
        in_specs=[VMEM, VMEM,
                  VMEM, VMEM, VMEM, VMEM],
        out_specs=pl.BlockSpec((rows, channels, batch, total_z), lambda i: (0, 0, i, 0)),
        scratch_shapes=[
            pltpu.VMEM((brick_y, coupled, width), F32),
            pltpu.VMEM((batch * 2 * coupled, total_z), BF16),
        ],
        compiler_params=pltpu.CompilerParams(vmem_limit_bytes=scoped),
        cost_estimate=pl.CostEstimate(flops=cells_count * 2000, bytes_accessed=cells_count * 60, transcendentals=cells_count * 20),
    )(total, other, local, wide_mixing, inverse_y, inverse_z)
    features = features.transpose(0, 2, 1, 3)
    return (wave, features)


def solution(mesh):
    placed = (
        P(("grp", "gx"), "gy", "gz"),
        P(("grp", "gx"), "gy", "gz"),
        P(("grp", "gx"), "gy", "gz"),
        P(),
        P(),
        P(),
        P(),
        P(),
        P(),
        P(),
    )
    return jax.shard_map(
        per_device,
        mesh=mesh,
        in_specs=placed,
        out_specs=(P(("grp", "gx"), "gy", "gz"), P(("grp", "gx", "gz"), "gy", None, None)),
        check_vma=False,
    )
```

```python
import math

import numpy as np
import jax
import jax.numpy as jnp
from jax import lax
from jax.experimental import pallas as pl
from jax.experimental.pallas import tpu as pltpu
from jax.sharding import PartitionSpec as P
import ml_dtypes

STEPS = 4
FIELDS = 4
REACH = 4
EDGE = 8
stencil_taps = (-205.0 / 72.0, 8.0 / 5.0, -1.0 / 5.0, 8.0 / 315.0, -1.0 / 560.0)
F32 = jnp.float32
BF16 = jnp.bfloat16
HIGHEST = lax.Precision.HIGHEST

VMEM = pl.BlockSpec(memory_space=pltpu.VMEM)
SMEM = pl.BlockSpec(memory_space=pltpu.SMEM)
HBM = pl.BlockSpec(memory_space=pltpu.HBM)


def rounded(table):
    return table.astype(ml_dtypes.bfloat16)


def kept_modes(length, mode_count):
    position = np.arange(mode_count)
    return np.where(position < mode_count // 2, position, length - mode_count + position)


def cos_sin(source, target, length):
    product = (source[:, None] * target[None, :]) % length
    phases = np.float32(2.0 * math.pi / length) * product.astype(np.float32)
    return rounded(np.cos(phases)), rounded(np.sin(phases))


def call(body, outs, in_specs, scratch=(), flops=0, moved=0, room_bytes=16 * 1024 * 1024):
    return pl.pallas_call(
        body,
        out_shape=outs,
        in_specs=in_specs,
        out_specs=jax.tree.map(lambda _: VMEM, outs),
        scratch_shapes=list(scratch),
        compiler_params=pltpu.CompilerParams(vmem_limit_bytes=room_bytes),
        cost_estimate=pl.CostEstimate(flops=flops, bytes_accessed=moved, transcendentals=0),
    )


def begin(sources, targets, semaphores):
    copies = [
        pltpu.make_async_copy(source, target, semaphores.at[index])
        for index, (source, target) in enumerate(zip(sources, targets))
    ]
    for copy in copies:
        copy.start()
    return copies


def here(*arrays):
    return [pltpu.with_memory_space_constraint(jnp.asarray(array), pltpu.HBM) for array in arrays]


def room(*arrays):
    return [(pltpu.SMEM if array.ndim == 1 else pltpu.VMEM)(array.shape, array.dtype) for array in arrays] + [
        pltpu.SemaphoreType.DMA((len(arrays),))
    ]


def high_low(value):
    high = value.astype(BF16)
    return high, (value - high.astype(F32)).astype(BF16)


def turned(value, half, sign):
    lane = lax.broadcasted_iota(jnp.int32, value.shape, value.ndim - 1)
    swapped = pltpu.roll(value, half, value.ndim - 1)
    return jnp.where(lane < half, sign * swapped, -sign * swapped)


def looked_up(material, table, entries):
    result = jnp.full(material.shape, table(0), F32)
    for entry in range(1, entries):
        result = jnp.where(material == entry, table(entry), result)
    return result


def middle(table):
    total = table[0]
    for entry in range(1, table.shape[0]):
        total = total + table[entry]
    return total * (1.0 / table.shape[0])


def edges(value_of, outs, row_parity, brick_y):
    for position, out in enumerate(outs):
        upper = row_parity == position
        out[...] = jnp.where(upper, value_of(brick_y - EDGE, brick_y), value_of(0, EDGE))


def slot():
    return (lax.axis_index("gz") + lax.axis_index("gx")) % 2


def fetch_body(*refs):
    tables_in, own_in = refs[:3], refs[3:6]
    p_out, q_out, m_out = refs[6:9]
    tables_out = refs[9]
    tables, semaphores = refs[10:13], refs[13]
    rows = p_out.shape[0]
    start = slot() * rows
    sources = [source.at[pl.ds(start, rows)] for source in own_in[:2]] + [own_in[2]]
    copies = begin(list(tables_in) + sources, list(tables) + [p_out, q_out, m_out], semaphores)
    for copy in copies:
        copy.wait()
    stiffness, density, nonlinear = tables
    for entry in range(stiffness.shape[0]):
        tables_out[2 * entry] = jnp.full(tables_out.shape[1:], stiffness[entry] / density[entry], F32)
        tables_out[2 * entry + 1] = jnp.full(tables_out.shape[1:], nonlinear[entry], F32)


def assemble_body(count, *refs):
    own, tables, got = refs[:3], refs[3], refs[4:7]
    p_out, q_out, ratio, bend, sent, cells = refs[7:13]
    edge_outs = refs[13 : 13 + count]
    core, column = lax.axis_index("gz"), lax.axis_index("gy")
    rows, brick_y, depth = p_out.shape
    start = slot() * rows
    entries = tables.shape[0] // 2

    def whole(mine, other):
        return jnp.concatenate(
            [jnp.where(core == 0, mine, other), jnp.where(core == 0, other, mine)], axis=-1
        )

    def chosen(cell, place):
        result = jnp.broadcast_to(tables[place, 0:1, 0:1], cell.shape)
        for entry in range(1, entries):
            result = jnp.where(cell == entry, jnp.broadcast_to(tables[2 * entry + place, 0:1, 0:1], cell.shape), result)
        return result

    for row in range(cells.shape[0]):
        cells[row] = whole(own[2][row], got[2][row])
    for row in range(rows):
        value = whole(own[0][row], got[0][start + row])
        p_out[row] = value
        sent[row] = value.astype(BF16)
        q_out[row] = whole(own[1][row], got[1][start + row])
        cell = cells[start + row]
        ratio[row] = chosen(cell, 0)
        bend[row] = chosen(cell, 1)
    edges(lambda a, b: p_out[:, a:b, :], edge_outs, column % 2, brick_y)


def step_body(two_sided, last, p_ref, q_ref, ratio, bend, mate, far, *rest):
    count = 2 if two_sided else 1
    halos = rest[:count]
    new_ref = rest[count]
    sent = None if last else rest[count + 1]
    edge_outs = rest[count + 2 : -1]
    padded = rest[-1]
    place = slot()
    parity = lax.axis_index("gy") % 2
    rows, brick_y, depth = p_ref.shape
    lane = lax.broadcasted_iota(jnp.int32, (brick_y, depth), 1)
    zero_edge = jnp.zeros((EDGE, depth), F32)

    cycle = lax.axis_index("gx")
    outside = cycle == jnp.where(place == 0, 0, lax.axis_size("gx") - 1)

    def line(index):
        if 0 <= index < rows:
            return p_ref[index]
        at = index % rows
        beyond = jnp.where(outside, 0.0, far[at].astype(F32))
        return jnp.where(place == (0 if index < 0 else 1), beyond, mate[at])

    for row in range(rows):
        first = halos[0][row]
        second = halos[1][row] if two_sided else zero_edge
        center = p_ref[row]
        padded[0:EDGE, :] = jnp.where(parity == 0, second, first)
        padded[EDGE : EDGE + brick_y, :] = center
        padded[EDGE + brick_y :, :] = jnp.where(parity == 0, first, second)
        total = (3.0 * stencil_taps[0]) * center
        for offset in range(1, REACH + 1):
            low, high = EDGE - offset, EDGE + offset
            pair = padded[low : low + brick_y, :] + padded[high : high + brick_y, :]
            pair = pair + (line(row - offset) + line(row + offset))
            pair = pair + jnp.where(lane >= offset, pltpu.roll(center, offset, 1), 0.0)
            pair = pair + jnp.where(
                lane < depth - offset, pltpu.roll(center, depth - offset, 1), 0.0
            )
            total = total + stencil_taps[offset] * pair
        change = center - q_ref[row]
        value = (center + change) + ratio[row] * total + bend[row] * change * change
        new_ref[row] = value
        if not last:
            sent[row] = value.astype(BF16)
    if not last:
        edges(lambda a, b: new_ref[:, a:b, :], edge_outs, parity, brick_y)


def transformed(sources, first, twiddle_x, table_z, table_y, lines, grid, late=()):
    column = lax.axis_index("gy")
    brick_y = lines.shape[0] // 4
    modes_y = grid.shape[0]
    width = table_z.shape[1]
    half = width // 2
    for field, rows in enumerate(sources):
        for row, load in enumerate(rows):
            high, low = high_low(load())
            modes = jnp.dot(high, table_z[...], preferred_element_type=F32)
            modes = modes + jnp.dot(low, table_z[...], preferred_element_type=F32)
            back = turned(modes, half, 1.0)
            high, low = high_low(modes)
            back_high, back_low = high_low(back)
            lanes = slice((field * len(rows) + row) * width, (field * len(rows) + row + 1) * width)
            for index, part in enumerate((high, back_high, low, back_low)):
                lines[index * brick_y : (index + 1) * brick_y, lanes] = part
    grid[...] = jnp.dot(table_y[column], lines[...], preferred_element_type=F32)
    for copy in late:
        copy.wait()

    def at_mode(field, modes_x):
        count = len(sources[field])
        values = [
            grid[:, (field * count + row) * width : (field * count + row + 1) * width] for row in range(count)
        ]
        backs = [turned(value, half, 1.0) for value in values]

        def summed(mode):
            total = jnp.zeros((modes_y, width), F32)
            for row in range(count):
                at = ((first + row) * modes_x + mode) * 2
                total = total + twiddle_x[at] * values[row] + twiddle_x[at + 1] * backs[row]
            return total

        return summed

    return at_mode


def materials_body(*refs):
    sources, cells, keep, table_z, table_y, lines, grid = refs[:5], *refs[5:11]
    twiddle_x, stiffness, density, semaphores = refs[11:15]
    copies = begin(sources, (twiddle_x, stiffness, density, table_z, table_y), semaphores)
    for copy in copies:
        copy.wait()
    half_x = keep.shape[1]
    entries = stiffness.shape[0]
    rows = cells.shape[0]
    sources = []
    for table in (stiffness, density):
        center = middle(table)
        sources.append([
            lambda row=row, table=table, center=center: looked_up(cells[row], lambda e: table[e] - center, entries)
            for row in range(rows)
        ])
    at_mode = transformed(sources, lax.axis_index("gx") * rows, twiddle_x, table_z, table_y, lines, grid)
    core = lax.axis_index("gz")
    for field in range(2):
        summed = at_mode(field, 2 * half_x)

        @pl.loop(0, half_x)
        def _(mode):
            keep[field, mode] = summed(core * half_x + mode)


def prior_body(twiddles, own, mate, table_z, table_y, keep, lines, grid, twiddle_x, semaphores):
    copies = begin((twiddles,), (twiddle_x,), semaphores)
    half_x = keep.shape[0]
    rows = own.shape[0]
    place = slot()
    sources = [
        (lambda row=row: jnp.where(place == 0, own[row], mate[row])) for row in range(rows)
    ] + [(lambda row=row: jnp.where(place == 0, mate[row], own[row])) for row in range(rows)]
    at_mode = transformed([sources], lax.axis_index("gx") * (2 * rows), twiddle_x, table_z, table_y, lines, grid, copies)
    core = lax.axis_index("gz")
    summed = at_mode(0, 2 * half_x)

    @pl.loop(0, half_x)
    def _(mode):
        keep[mode] = summed(core * half_x + mode)


def wave_body(twiddles, own, prior, early, table_z, table_y, keep, send, lines, grid, twiddle_x, semaphores):
    copies = begin((twiddles,), (twiddle_x,), semaphores)
    half_x = keep.shape[1]
    rows = own.shape[0]
    first = (lax.axis_index("gx") * 2 + slot()) * rows
    sources = [(lambda row=row: own[row]) for row in range(rows)]
    at_mode = transformed([sources], first, twiddle_x, table_z, table_y, lines, grid, copies)
    core = lax.axis_index("gz")
    summed = at_mode(0, 2 * half_x)
    keep[1] = prior[...]
    keep[2:4] = early[...]

    @pl.loop(0, half_x)
    def _(mode):
        keep[0, mode] = summed(core * half_x + mode)
        send[0, mode] = summed((1 - core) * half_x + mode).astype(BF16)


def prepare_body(*refs):
    sources, outs, targets, semaphores = refs[:11], refs[11:15], refs[15:26], refs[26]
    mixing, pointwise, lift_table, offset = outs
    block = lax.axis_index("gx") * 2 + lax.axis_index("gz")
    copies = begin([*sources[:9], sources[9].at[block], sources[10]], targets, semaphores)
    for copy in copies:
        copy.wait()
    stiffness, density, mode_ref, lift_ref, bias_ref, local_ref, spread_ref, place_ref, owner_ref, turn_ref, wide_ref = targets
    half = place_ref.shape[1]
    channels = lift_ref.shape[1]
    spread = owner_ref[...]

    def dot(a, b, dims=((1,), (0,))):
        return lax.dot_general(a, b, (dims, ((), ())), precision=HIGHEST, preferred_element_type=F32)

    across = ((1,), (1,))
    lifted = dot(dot(spread_ref[:, :channels], lift_ref[...], across), place_ref[...])
    lifted = lifted * spread_ref[:, channels : channels + half]
    flat = [mode_ref[index].reshape(-1, channels) for index in range(2)]
    real, imag = [dot(dot(spread, values, across), lifted) for values in flat]
    cosine = turn_ref[0]
    sine = turn_ref[1]
    coupled = jnp.concatenate([cosine * real - sine * imag, -(cosine * imag + sine * real)], axis=1)
    mixing[...] = coupled.astype(BF16)
    constant = dot(spread, mode_ref[0, :, 0, :], across)
    bias = bias_ref[...] + middle(stiffness) * lift_ref[2:3, :] + middle(density) * lift_ref[3:4, :]
    offset[...] = jnp.sum(constant * bias, axis=1, keepdims=True)
    height = spread.shape[0]
    widest = wide_ref[0:channels, :]
    repeated = dot(dot(spread, local_ref[...].astype(F32), across), widest)
    pointwise[...] = (repeated * wide_ref[channels : channels + height, :]).astype(BF16)
    padded = wide_ref[channels + height :, 0:channels]
    lift_table[:, 0:FIELDS] = dot(padded, lift_ref[...], across)
    lift_table[:, FIELDS : FIELDS + 1] = dot(padded, bias_ref[...], across)
    lift_table[:, FIELDS + 1 :] = jnp.zeros_like(lift_table[:, FIELDS + 1 :])


def widen_body(mixing, repeat_ref, out):
    rows, span = repeat_ref.shape[0], mixing.shape[1]
    count = rows // mixing.shape[0]
    values = jnp.dot(repeat_ref[...], mixing[...], preferred_element_type=F32)
    column = lax.broadcasted_iota(jnp.int32, (rows, span), 0) % count
    parts = [jnp.where(column == index, values, 0.0) for index in range(count)]
    out[...] = jnp.concatenate(parts, axis=1).astype(BF16)


def pointwise_body(stiffness_in, density_in, p_ref, q_ref, p_mate, q_mate, cells, lift_ref, left, offset, *rest):
    out, right, stiffness, density, semaphores = rest[-5:]
    rows, group, depth = p_ref.shape
    padded_channels = lift_ref.shape[0]
    height = rows * padded_channels
    entries = stiffness.shape[0]
    core = lax.axis_index("gz")
    own = slot() == core

    @pl.when(pl.program_id(0) == 0)
    def _():
        right[...] = jnp.zeros_like(right)
        for copy in begin((stiffness_in, density_in), (stiffness, density), semaphores):
            copy.wait()

    weights = [lift_ref[:, index : index + 1] for index in range(FIELDS + 1)]
    values = []
    for row in range(rows):
        cell = cells[core * rows + row]
        values.append((
            jnp.where(own, p_ref[row], p_mate[row]),
            jnp.where(own, q_ref[row], q_mate[row]),
            looked_up(cell, lambda e: stiffness[e], entries),
            looked_up(cell, lambda e: density[e], entries),
        ))
    for y in range(group):
        lifted = []
        for row in range(rows):
            total = jnp.broadcast_to(weights[FIELDS], (padded_channels, depth))
            for value, weight in zip(values[row], weights):
                total = total + value[y : y + 1, :] * weight
            lifted.append(total)
        right[y, 0:height, :] = jnp.concatenate(lifted, axis=0).astype(BF16)
        out[:, y, :] = jnp.dot(left[...], right[y], preferred_element_type=F32) + offset[...]


def join_body(own, other, wave_out):
    core = lax.axis_index("gz")
    rows, _, depth = own.shape
    half = depth // 2
    place = slot()
    for row in range(rows):
        for ref, start in ((own, place * rows), (other, (1 - place) * rows)):
            wave_out[start + row] = jnp.where(core == 0, ref[row, :, :half], ref[row, :, half:])


def back_columns(spectra, left_y, modes):
    fields, half_x, _, width = spectra.shape
    chunk = min(8, half_x)
    for field in range(fields):
        for start in range(0, half_x, chunk):
            values = [spectra[field, mode].astype(F32) for mode in range(start, start + chunk)]
            stacked = jnp.concatenate([
                jnp.concatenate([value.astype(BF16) for value in values], axis=1),
                jnp.concatenate([turned(value, width // 2, -1.0).astype(BF16) for value in values], axis=1),
            ], axis=0)
            result = jnp.dot(left_y, stacked, preferred_element_type=F32)
            for mode in range(start, start + chunk):
                lanes = slice((mode - start) * width, (mode - start + 1) * width)
                modes[:, mode * fields + field, :] = result[:, lanes]


def own_half_body(mine, table_y, table_z, out, modes):
    back_columns(mine, table_y[lax.axis_index("gy")], modes)
    lines = modes[...].reshape(out.shape[0], modes.shape[2]).astype(BF16)
    out[...] = jnp.dot(lines, table_z[...], preferred_element_type=F32).astype(BF16)


def output_body(
    waves_own, other, local, left, table_y, table_z, features, modes, right,
):
    step = pl.program_id(0)
    core, column = lax.axis_index("gz"), lax.axis_index("gy")
    half_x, modes_y, width = other.shape[1:]
    rows, channels, group, depth = features.shape
    coupled = 2 * FIELDS * half_x
    half_rows = FIELDS * half_x

    @pl.when(step == 0)
    def _():
        back_columns(other, table_y[column], modes)

    base = pl.multiple_of(step * group, group)
    lines = modes[pl.ds(base, group)].reshape(group * half_rows, width).astype(BF16)
    waves = jnp.dot(lines, table_z[...], preferred_element_type=F32).astype(BF16)
    own = waves_own[pl.ds(pl.multiple_of(base * half_rows, group * half_rows), group * half_rows), :]
    count = left.shape[1] // (2 * coupled)
    for y in range(group):
        lines = slice(y * half_rows, (y + 1) * half_rows)
        for values, place in ((own, core), (waves, 1 - core)):
            for part in range(2):
                at = pl.multiple_of(y * 2 * coupled + part * coupled + place * half_rows, half_rows)
                right[pl.ds(at, half_rows), :] = values[lines, part * depth : (part + 1) * depth]
    for first in range(0, group, 2 * count):
        results = []
        for start in (first * 2 * coupled, (first + count) * 2 * coupled):
            results.append(jnp.dot(
                left[...], right[start : start + count * 2 * coupled, :], preferred_element_type=F32
            ))
        for row in range(rows):
            for channel in range(channels):
                at = row * channels + channel
                total = jnp.concatenate([result[at * count : (at + 1) * count] for result in results], axis=0)
                total = total + local[at, pl.ds(base + first, 2 * count), :]
                scale = math.sqrt(2.0 / math.pi)
                inner = total * (scale + (scale * 0.044715) * (total * total))
                part = 0.5 * total
                total = part + part * jnp.tanh(inner)
                features[row, channel, first : first + 2 * count, :] = total.astype(BF16)


def xor_pairs(count, distance):
    return [(index, index ^ distance) for index in range(count)]


def odd_pairs(count):
    pairs = [(index, index + 1) for index in range(1, count - 1, 2)]
    return pairs + [(target, source) for source, target in pairs]


def row_pairs(cycles, columns):
    place = lambda cycle, column, core: (cycle * columns + column) * 2 + core
    pairs = []
    for column in range(columns):
        for cycle in range(cycles - 1):
            one, two = place(cycle, column, 1 - cycle % 2), place(cycle + 1, column, 1 - cycle % 2)
            pairs += [(one, two), (two, one)]
        for cycle, core in ((0, 0), (cycles - 1, 1 - (cycles - 1) % 2)):
            pairs.append((place(cycle, column, core), place(cycle, column ^ 1, core)))
    return pairs


def per_device(
    pressure,
    previous,
    material,
    stiffness,
    density,
    nonlinear,
    lift_weight,
    lift_bias,
    mode_weight,
    local_weight,
):
    brick_x, brick_y, brick_z = pressure.shape
    cycle_count = lax.axis_size("gx")
    column_count = lax.axis_size("gy")
    core_count = lax.axis_size("gz")
    total_x = brick_x * cycle_count
    total_y = brick_y * column_count
    total_z = brick_z * core_count
    modes_x = total_x // 4
    modes_y = total_y // 4
    modes_z = total_z // 4
    width = 2 * modes_z
    channels = lift_bias.shape[0]
    rows = brick_x // core_count
    assert core_count == 2 and rows >= REACH
    blocks = cycle_count * core_count
    padded_channels = -(-channels // 8) * 8
    height = rows * channels
    coupled = FIELDS * modes_x
    right_depth = -(-rows * padded_channels // 128) * 128
    two_sided = column_count > 2

    kept_first = kept_modes(total_x, modes_x)
    kept_second = kept_modes(total_y, modes_y)
    kept_third = np.arange(modes_z)
    cz, sz = cos_sin(np.arange(total_z), kept_third, total_z)
    forward_z = np.concatenate([cz, -sz], 1)
    weight = np.where(kept_third == 0, 1.0, 2.0) / (total_x * total_y * total_z)
    wc, ws = [rounded((t.astype(np.float32) * weight).T.astype(np.float32)) for t in (cz, sz)]
    inverse_z = np.concatenate(
        [np.concatenate([wc, ws], 1), np.concatenate([-ws.astype(np.float32), wc.astype(np.float32)], 1)], 0
    )
    inverse_z = rounded(inverse_z)
    cy, sy = cos_sin(kept_second, np.arange(total_y), total_y)
    cy3, sy3 = [t.reshape(modes_y, column_count, brick_y).transpose(1, 0, 2) for t in (cy, sy)]
    forward_y = np.concatenate([cy3, sy3, cy3, sy3], 2)
    cy3, sy3 = [t.transpose(0, 2, 1) for t in (cy3, sy3)]
    inverse_y = np.concatenate([cy3, sy3], 2)
    cx, sx = [t.astype(np.float32) for t in cos_sin(np.arange(total_x), kept_first, total_x)]
    twiddle_x = np.stack([cx, sx], -1).reshape(-1)
    owner = np.tile(np.eye(channels, dtype=np.float32), (rows, 1))
    turn = np.zeros((blocks, 2, height, coupled), np.float32)
    for source, table in enumerate((cx, sx)):
        turn[:, source] = np.repeat(
            np.repeat(table.reshape(blocks, rows, modes_x), channels, 1), FIELDS, 2
        )
    padded_eye = np.eye(channels, padded_channels, dtype=np.float32)
    wide = np.zeros((channels + height + padded_channels, right_depth), np.float32)
    wide[:channels, : rows * padded_channels] = np.tile(padded_eye, (1, rows))
    wide[channels : channels + height, : rows * padded_channels] = np.kron(
        np.eye(rows), np.ones((channels, padded_channels))
    )
    wide[channels + height :, :channels] = padded_eye.T
    spread = np.repeat(np.eye(channels, dtype=np.float32), modes_x, 0)
    same = np.tile(np.repeat(np.eye(modes_x, dtype=np.float32), FIELDS, 1), (channels, 1))
    spread = np.concatenate([spread, same], 1)
    place = np.tile(np.eye(FIELDS, dtype=np.float32), (1, modes_x))

    def shape(*dims, dtype=F32):
        return jax.ShapeDtypeStruct(dims, dtype)

    cells_count = rows * brick_y * total_z
    field = shape(rows, brick_y, total_z)
    edge = [shape(rows, EDGE, total_z)] * (2 if two_sided else 1)

    swap_core = xor_pairs(core_count, 1)
    got = [lax.ppermute(array, "gz", swap_core) for array in (pressure, previous, material)]
    sending = shape(rows, brick_y, total_z, dtype=BF16)
    half = (rows, brick_y, brick_z)
    fetched = call(
        fetch_body,
        [shape(*half), shape(*half), shape(brick_x, brick_y, brick_z, dtype=jnp.int32), shape(2 * stiffness.shape[0], 8, 128)],
        [HBM] * 6, [pltpu.SMEM(stiffness.shape, F32)] * 3 + [pltpu.SemaphoreType.DMA((6,))], moved=cells_count * 8
    )(*here(stiffness, density, nonlinear, pressure, previous, material))
    fetched, got = lax.optimization_barrier((fetched, got))
    current, before, ratio, bend, sent, cells, *edge_values = call(
        lambda *refs: assemble_body(len(edge), *refs),
        [field] * 4 + [sending, shape(brick_x, brick_y, total_z, dtype=jnp.int32)] + edge, [VMEM] * 7,
        moved=cells_count * 36
    )(*fetched, *got)

    weights = (
        stiffness, density, mode_weight.transpose(0, 2, 1, 3), lift_weight, lift_bias.reshape(1, channels),
        local_weight, spread, place, owner, turn, wide,
    )
    mixing, pointwise, lift_table, offset = call(
        prepare_body,
        [shape(height, 2 * coupled, dtype=BF16), shape(height, right_depth, dtype=BF16),
         shape(padded_channels, 8), shape(height, 1)],
        [HBM] * 11, room(*weights[:9], turn[0], wide), flops=2_000_000_000, moved=4_000_000,
    )(*here(*weights))

    part = lambda fields, dtype: shape(fields, modes_x // 2, modes_y, width, dtype=dtype)

    def spectrum(body, outs, inputs, lines, specs=None, scratch=()):
        return call(
            body, outs, specs or [HBM] + [VMEM] * (inputs + 2),
            [pltpu.VMEM((4 * brick_y, lines * width), BF16), pltpu.VMEM((modes_y, lines * width), F32), *scratch],
            flops=cells_count * 256 * lines, moved=cells_count * 2 * lines,
        )

    stages = [(axis, count, 2 ** (bit + 1) - 1) for axis, count in (("gy", column_count), ("gx", cycle_count))
              for bit in range((count - 1).bit_length())]
    swap = lambda value: lax.ppermute(value, "gz", swap_core)

    def exchange(value, axis, count, distance):
        return lax.ppermute(value.astype(BF16), axis, xor_pairs(count, distance))

    tables = (twiddle_x, stiffness, density, forward_z, forward_y)
    early, forward_z, forward_y = spectrum(
        materials_body,
        [part(2, F32)] + [jax.ShapeDtypeStruct(table.shape, table.dtype) for table in (forward_z, forward_y)],
        1, 2 * brick_x, [HBM] * 5 + [VMEM], room(*tables[:3])[:3] + [pltpu.SemaphoreType.DMA((5,))],
    )(*here(*tables), cells)
    twiddles = here(twiddle_x)
    twiddle_room = room(twiddle_x)

    for repeat in range(STEPS):
        last = repeat == STEPS - 1
        far = lax.ppermute(sent, ("gx", "gy", "gz"), row_pairs(cycle_count, column_count))
        mate = swap(current)
        halos = [lax.ppermute(edge_values[0], "gy", xor_pairs(column_count, 1))]
        if two_sided:
            halos.append(lax.ppermute(edge_values[1], "gy", odd_pairs(column_count)))
        if repeat == 0:
            far, early = lax.optimization_barrier((far, early))
        if last:
            prior = spectrum(prior_body, shape(modes_x // 2, modes_y, width), 2, brick_x, None, twiddle_room)(
                *twiddles, current, mate, forward_z, forward_y
            )
            far, prior = lax.optimization_barrier((far, prior))
            prior_mate = mate
        outs = [field] + ([] if last else [sending] + edge)
        body = lambda *refs, last=last: step_body(two_sided, last, *refs)
        new, *others = call(
            body, outs, [VMEM] * (6 + len(halos)),
            [pltpu.VMEM((brick_y + 2 * EDGE, total_z), F32)], flops=cells_count * 60, moved=cells_count * 28,
        )(current, before, ratio, bend, mate, far, *halos)
        if not last:
            sent, *edge_values = others
        current, before = new, current

    total, sent = spectrum(wave_body, [part(FIELDS, F32), part(1, BF16)], 3, rows, None, twiddle_room)(
        *twiddles, current, prior, early, forward_z, forward_y
    )
    total = total + jnp.pad(swap(sent).astype(F32), ((0, FIELDS - 1), (0, 0), (0, 0), (0, 0)))
    wave_other = swap(current)
    group = 8
    steps = brick_y // group
    whole = lambda array: pl.BlockSpec(array.shape, lambda i: (0,) * len(array.shape))

    def pointwise_part(start, held=()):
        slab = lambda count: pl.BlockSpec((count, group, total_z), lambda i: (0, i + start, 0))
        return pl.pallas_call(
            pointwise_body,
            grid=(steps // 2,),
            out_shape=shape(height, brick_y, total_z),
            in_specs=[HBM] * 2 + [slab(rows)] * 4 + [slab(brick_x), whole(lift_table), whole(pointwise), whole(offset)]
            + [pl.BlockSpec(memory_space=pl.ANY)] * len(held),
            out_specs=pl.BlockSpec((height, group, total_z), lambda i: (0, i + start, 0)),
            input_output_aliases={10: 0} if held else {},
            scratch_shapes=[pltpu.VMEM((group, right_depth, total_z), BF16)] + room(stiffness, density),
            compiler_params=pltpu.CompilerParams(vmem_limit_bytes=16 * 1024 * 1024),
            cost_estimate=pl.CostEstimate(flops=cells_count * 20000, bytes_accessed=cells_count * 50, transcendentals=0),
        )(*here(stiffness, density), current, before, wave_other, prior_mate, cells, lift_table, pointwise, offset, *held)

    for index, stage in enumerate(stages):
        arrived = exchange(total, *stage)
        if index == 0:
            arrived, mixing, pointwise, lift_table, offset = lax.optimization_barrier(
                (arrived, mixing, pointwise, lift_table, offset)
            )
        if index == len(stages) - 2:
            local = pointwise_part(0)
            wave = call(join_body, shape(*pressure.shape), [VMEM] * 2, moved=cells_count * 12)(current, wave_other)
            arrived, local, wave = lax.optimization_barrier((arrived, local, wave))
        if index == len(stages) - 1:
            local = pointwise_part(steps // 2, (local,))
            repeats = np.repeat(np.eye(height), 8, 0).astype(ml_dtypes.bfloat16)
            wide_mixing = call(
                widen_body, shape(height * 8, 16 * coupled, dtype=BF16), [VMEM] * 2, flops=1_000_000_000, moved=2_000_000
            )(mixing, repeats)
            arrived, local, wide_mixing = lax.optimization_barrier((arrived, local, wide_mixing))
        total = total + arrived.astype(F32)
    other = swap(total.astype(BF16))
    batch = min(32, brick_y)
    scoped = 10 * 2**20 + 20 * height * 16 * coupled + 4 * (brick_y * coupled * width + 6 * batch * coupled * total_z)
    waves_own = call(
        own_half_body, shape(brick_y * coupled // 2, 2 * total_z, dtype=BF16), [VMEM] * 3,
        [pltpu.VMEM((brick_y, coupled // 2, width), F32)], flops=1_000_000_000, moved=2_000_000, room_bytes=scoped,
    )(total, inverse_y, inverse_z)
    other, waves_own = lax.optimization_barrier((other, waves_own))
    features = pl.pallas_call(
        output_body,
        grid=(brick_y // batch,),
        out_shape=shape(rows, channels, brick_y, total_z, dtype=BF16),
        in_specs=[VMEM, VMEM,
                  VMEM, VMEM, VMEM, VMEM],
        out_specs=pl.BlockSpec((rows, channels, batch, total_z), lambda i: (0, 0, i, 0)),
        scratch_shapes=[
            pltpu.VMEM((brick_y, coupled // 2, width), F32),
            pltpu.VMEM((batch * 2 * coupled, total_z), BF16),
        ],
        compiler_params=pltpu.CompilerParams(vmem_limit_bytes=scoped),
        cost_estimate=pl.CostEstimate(flops=cells_count * 2000, bytes_accessed=cells_count * 60, transcendentals=cells_count * 20),
    )(waves_own, other, local, wide_mixing, inverse_y, inverse_z)
    features = features.transpose(0, 2, 1, 3)
    return (wave, features)


def solution(mesh):
    placed = (
        P(("grp", "gx"), "gy", "gz"),
        P(("grp", "gx"), "gy", "gz"),
        P(("grp", "gx"), "gy", "gz"),
        P(),
        P(),
        P(),
        P(),
        P(),
        P(),
        P(),
    )
    return jax.shard_map(
        per_device,
        mesh=mesh,
        in_specs=placed,
        out_specs=(P(("grp", "gx"), "gy", "gz"), P(("grp", "gx", "gz"), "gy", None, None)),
        check_vma=False,
    )
```

```python
import math

import numpy as np
import jax
import jax.numpy as jnp
from jax import lax
from jax.experimental import pallas as pl
from jax.experimental.pallas import tpu as pltpu
from jax.sharding import PartitionSpec as P
import ml_dtypes

STEPS = 4
FIELDS = 4
REACH = 4
EDGE = 8
stencil_taps = (-205.0 / 72.0, 8.0 / 5.0, -1.0 / 5.0, 8.0 / 315.0, -1.0 / 560.0)
F32 = jnp.float32
BF16 = jnp.bfloat16
HIGHEST = lax.Precision.HIGHEST

VMEM = pl.BlockSpec(memory_space=pltpu.VMEM)
SMEM = pl.BlockSpec(memory_space=pltpu.SMEM)
HBM = pl.BlockSpec(memory_space=pltpu.HBM)


def rounded(table):
    return table.astype(ml_dtypes.bfloat16)


def kept_modes(length, mode_count):
    position = np.arange(mode_count)
    return np.where(position < mode_count // 2, position, length - mode_count + position)


def cos_sin(source, target, length):
    product = (source[:, None] * target[None, :]) % length
    phases = np.float32(2.0 * math.pi / length) * product.astype(np.float32)
    return rounded(np.cos(phases)), rounded(np.sin(phases))


def call(body, outs, in_specs, scratch=(), flops=0, moved=0, room_bytes=16 * 1024 * 1024):
    return pl.pallas_call(
        body,
        out_shape=outs,
        in_specs=in_specs,
        out_specs=jax.tree.map(lambda _: VMEM, outs),
        scratch_shapes=list(scratch),
        compiler_params=pltpu.CompilerParams(vmem_limit_bytes=room_bytes),
        cost_estimate=pl.CostEstimate(flops=flops, bytes_accessed=moved, transcendentals=0),
    )


def begin(sources, targets, semaphores):
    copies = [
        pltpu.make_async_copy(source, target, semaphores.at[index])
        for index, (source, target) in enumerate(zip(sources, targets))
    ]
    for copy in copies:
        copy.start()
    return copies


def here(*arrays):
    return [pltpu.with_memory_space_constraint(jnp.asarray(array), pltpu.HBM) for array in arrays]


def room(*arrays):
    return [(pltpu.SMEM if array.ndim == 1 else pltpu.VMEM)(array.shape, array.dtype) for array in arrays] + [
        pltpu.SemaphoreType.DMA((len(arrays),))
    ]


def high_low(value):
    high = value.astype(BF16)
    return high, (value - high.astype(F32)).astype(BF16)


def turned(value, half, sign):
    lane = lax.broadcasted_iota(jnp.int32, value.shape, value.ndim - 1)
    swapped = pltpu.roll(value, half, value.ndim - 1)
    return jnp.where(lane < half, sign * swapped, -sign * swapped)


def looked_up(material, table, entries):
    result = jnp.full(material.shape, table(0), F32)
    for entry in range(1, entries):
        result = jnp.where(material == entry, table(entry), result)
    return result


def middle(table):
    total = table[0]
    for entry in range(1, table.shape[0]):
        total = total + table[entry]
    return total * (1.0 / table.shape[0])


def edges(value_of, outs, row_parity, brick_y):
    for position, out in enumerate(outs):
        upper = row_parity == position
        out[...] = jnp.where(upper, value_of(brick_y - EDGE, brick_y), value_of(0, EDGE)).astype(BF16)


def slot():
    return (lax.axis_index("gz") + lax.axis_index("gx")) % 2


def fetch_body(*refs):
    tables_in, own_in = refs[:3], refs[3:6]
    p_out, q_out, m_out = refs[6:9]
    tables_out = refs[9]
    tables, semaphores = refs[10:13], refs[13]
    rows = p_out.shape[0]
    start = slot() * rows
    sources = [source.at[pl.ds(start, rows)] for source in own_in[:2]] + [own_in[2]]
    copies = begin(list(tables_in) + sources, list(tables) + [p_out, q_out, m_out], semaphores)
    for copy in copies:
        copy.wait()
    stiffness, density, nonlinear = tables
    for entry in range(stiffness.shape[0]):
        tables_out[2 * entry] = jnp.full(tables_out.shape[1:], stiffness[entry] / density[entry], F32)
        tables_out[2 * entry + 1] = jnp.full(tables_out.shape[1:], nonlinear[entry], F32)


def assemble_body(count, *refs):
    own, tables, got = refs[:3], refs[3], refs[4:7]
    p_out, q_out, ratio, bend, sent, cells = refs[7:13]
    edge_outs = refs[13 : 13 + count]
    core, column = lax.axis_index("gz"), lax.axis_index("gy")
    rows, brick_y, depth = p_out.shape
    start = slot() * rows
    entries = tables.shape[0] // 2

    def whole(mine, other):
        return jnp.concatenate(
            [jnp.where(core == 0, mine, other), jnp.where(core == 0, other, mine)], axis=-1
        )

    def chosen(cell, place):
        result = jnp.broadcast_to(tables[place, 0:1, 0:1], cell.shape)
        for entry in range(1, entries):
            result = jnp.where(cell == entry, jnp.broadcast_to(tables[2 * entry + place, 0:1, 0:1], cell.shape), result)
        return result

    for row in range(cells.shape[0]):
        cells[row] = whole(own[2][row], got[2][row])
    for row in range(rows):
        value = whole(own[0][row], got[0][start + row])
        p_out[row] = value
        sent[row] = value.astype(BF16)
        q_out[row] = whole(own[1][row], got[1][start + row])
        cell = cells[start + row]
        ratio[row] = chosen(cell, 0)
        bend[row] = chosen(cell, 1)
    edges(lambda a, b: p_out[:, a:b, :], edge_outs, column % 2, brick_y)


def step_body(two_sided, last, p_ref, q_ref, ratio, bend, mate, far, *rest):
    count = 2 if two_sided else 1
    halos = rest[:count]
    new_ref = rest[count]
    sent = None if last else rest[count + 1]
    edge_outs = rest[count + 2 : -1]
    padded = rest[-1]
    place = slot()
    parity = lax.axis_index("gy") % 2
    rows, brick_y, depth = p_ref.shape
    lane = lax.broadcasted_iota(jnp.int32, (brick_y, depth), 1)
    zero_edge = jnp.zeros((EDGE, depth), F32)

    cycle = lax.axis_index("gx")
    outside = cycle == jnp.where(place == 0, 0, lax.axis_size("gx") - 1)

    def line(index):
        if 0 <= index < rows:
            return p_ref[index]
        at = index % rows
        beyond = jnp.where(outside, 0.0, far[at].astype(F32))
        return jnp.where(place == (0 if index < 0 else 1), beyond, mate[at])

    for row in range(rows):
        first = halos[0][row].astype(F32)
        second = halos[1][row].astype(F32) if two_sided else zero_edge
        center = p_ref[row]
        padded[0:EDGE, :] = jnp.where(parity == 0, second, first)
        padded[EDGE : EDGE + brick_y, :] = center
        padded[EDGE + brick_y :, :] = jnp.where(parity == 0, first, second)
        total = (3.0 * stencil_taps[0]) * center
        for offset in range(1, REACH + 1):
            low, high = EDGE - offset, EDGE + offset
            pair = padded[low : low + brick_y, :] + padded[high : high + brick_y, :]
            pair = pair + (line(row - offset) + line(row + offset))
            pair = pair + jnp.where(lane >= offset, pltpu.roll(center, offset, 1), 0.0)
            pair = pair + jnp.where(
                lane < depth - offset, pltpu.roll(center, depth - offset, 1), 0.0
            )
            total = total + stencil_taps[offset] * pair
        change = center - q_ref[row]
        value = (center + change) + ratio[row] * total + bend[row] * change * change
        new_ref[row] = value
        if not last:
            sent[row] = value.astype(BF16)
    if not last:
        edges(lambda a, b: new_ref[:, a:b, :], edge_outs, parity, brick_y)


def transformed(sources, first, twiddle_x, table_z, table_y, lines, grid, late=()):
    column = lax.axis_index("gy")
    brick_y = lines.shape[0] // 4
    modes_y = grid.shape[0]
    width = table_z.shape[1]
    half = width // 2
    for field, rows in enumerate(sources):
        for row, load in enumerate(rows):
            high, low = high_low(load())
            modes = jnp.dot(high, table_z[...], preferred_element_type=F32)
            modes = modes + jnp.dot(low, table_z[...], preferred_element_type=F32)
            back = turned(modes, half, 1.0)
            high, low = high_low(modes)
            back_high, back_low = high_low(back)
            lanes = slice((field * len(rows) + row) * width, (field * len(rows) + row + 1) * width)
            for index, part in enumerate((high, back_high, low, back_low)):
                lines[index * brick_y : (index + 1) * brick_y, lanes] = part
    grid[...] = jnp.dot(table_y[column], lines[...], preferred_element_type=F32)
    for copy in late:
        copy.wait()

    def at_mode(field, modes_x):
        count = len(sources[field])
        values = [
            grid[:, (field * count + row) * width : (field * count + row + 1) * width] for row in range(count)
        ]
        backs = [turned(value, half, 1.0) for value in values]

        def summed(mode):
            total = jnp.zeros((modes_y, width), F32)
            for row in range(count):
                at = ((first + row) * modes_x + mode) * 2
                total = total + twiddle_x[at] * values[row] + twiddle_x[at + 1] * backs[row]
            return total

        return summed

    return at_mode


def materials_body(*refs):
    sources, cells, keep, table_z, table_y, lines, grid = refs[:5], *refs[5:11]
    twiddle_x, stiffness, density, semaphores = refs[11:15]
    copies = begin(sources, (twiddle_x, stiffness, density, table_z, table_y), semaphores)
    for copy in copies:
        copy.wait()
    half_x = keep.shape[1]
    entries = stiffness.shape[0]
    rows = cells.shape[0]
    sources = []
    for table in (stiffness, density):
        center = middle(table)
        sources.append([
            lambda row=row, table=table, center=center: looked_up(cells[row], lambda e: table[e] - center, entries)
            for row in range(rows)
        ])
    at_mode = transformed(sources, lax.axis_index("gx") * rows, twiddle_x, table_z, table_y, lines, grid)
    core = lax.axis_index("gz")
    for field in range(2):
        summed = at_mode(field, 2 * half_x)

        @pl.loop(0, half_x)
        def _(mode):
            keep[field, mode] = summed(core * half_x + mode)


def prior_body(twiddles, own, mate, table_z, table_y, keep, lines, grid, twiddle_x, semaphores):
    copies = begin((twiddles,), (twiddle_x,), semaphores)
    half_x = keep.shape[0]
    rows = own.shape[0]
    place = slot()
    sources = [
        (lambda row=row: jnp.where(place == 0, own[row], mate[row])) for row in range(rows)
    ] + [(lambda row=row: jnp.where(place == 0, mate[row], own[row])) for row in range(rows)]
    at_mode = transformed([sources], lax.axis_index("gx") * (2 * rows), twiddle_x, table_z, table_y, lines, grid, copies)
    core = lax.axis_index("gz")
    summed = at_mode(0, 2 * half_x)

    @pl.loop(0, half_x)
    def _(mode):
        keep[mode] = summed(core * half_x + mode)


def wave_body(twiddles, own, prior, early, table_z, table_y, keep, send, lines, grid, twiddle_x, semaphores):
    copies = begin((twiddles,), (twiddle_x,), semaphores)
    half_x = keep.shape[1]
    rows = own.shape[0]
    first = (lax.axis_index("gx") * 2 + slot()) * rows
    sources = [(lambda row=row: own[row]) for row in range(rows)]
    at_mode = transformed([sources], first, twiddle_x, table_z, table_y, lines, grid, copies)
    core = lax.axis_index("gz")
    summed = at_mode(0, 2 * half_x)
    keep[1] = prior[...]
    keep[2:4] = early[...]

    @pl.loop(0, half_x)
    def _(mode):
        keep[0, mode] = summed(core * half_x + mode)
        send[0, mode] = summed((1 - core) * half_x + mode).astype(BF16)


def prepare_body(*refs):
    sources, outs, targets, semaphores = refs[:11], refs[11:15], refs[15:26], refs[26]
    mixing, pointwise, lift_table, offset = outs
    block = lax.axis_index("gx") * 2 + lax.axis_index("gz")
    copies = begin([*sources[:9], sources[9].at[block], sources[10]], targets, semaphores)
    for copy in copies:
        copy.wait()
    stiffness, density, mode_ref, lift_ref, bias_ref, local_ref, spread_ref, place_ref, owner_ref, turn_ref, wide_ref = targets
    half = place_ref.shape[1]
    channels = lift_ref.shape[1]
    spread = owner_ref[...]

    def dot(a, b, dims=((1,), (0,))):
        return lax.dot_general(a, b, (dims, ((), ())), precision=HIGHEST, preferred_element_type=F32)

    across = ((1,), (1,))
    lifted = dot(dot(spread_ref[:, :channels], lift_ref[...], across), place_ref[...])
    lifted = lifted * spread_ref[:, channels : channels + half]
    flat = [mode_ref[index].reshape(-1, channels) for index in range(2)]
    real, imag = [dot(dot(spread, values, across), lifted) for values in flat]
    cosine = turn_ref[0]
    sine = turn_ref[1]
    coupled = jnp.concatenate([cosine * real - sine * imag, -(cosine * imag + sine * real)], axis=1)
    mixing[...] = coupled.astype(BF16)
    constant = dot(spread, mode_ref[0, :, 0, :], across)
    bias = bias_ref[...] + middle(stiffness) * lift_ref[2:3, :] + middle(density) * lift_ref[3:4, :]
    offset[...] = jnp.sum(constant * bias, axis=1, keepdims=True)
    height = spread.shape[0]
    widest = wide_ref[0:channels, :]
    repeated = dot(dot(spread, local_ref[...].astype(F32), across), widest)
    pointwise[...] = (repeated * wide_ref[channels : channels + height, :]).astype(BF16)
    padded = wide_ref[channels + height :, 0:channels]
    lift_table[:, 0:FIELDS] = dot(padded, lift_ref[...], across)
    lift_table[:, FIELDS : FIELDS + 1] = dot(padded, bias_ref[...], across)
    lift_table[:, FIELDS + 1 :] = jnp.zeros_like(lift_table[:, FIELDS + 1 :])


def widen_body(mixing, repeat_ref, out):
    rows, span = repeat_ref.shape[0], mixing.shape[1]
    count = rows // mixing.shape[0]
    values = jnp.dot(repeat_ref[...], mixing[...], preferred_element_type=F32)
    column = lax.broadcasted_iota(jnp.int32, (rows, span), 0) % count
    parts = [jnp.where(column == index, values, 0.0) for index in range(count)]
    out[...] = jnp.concatenate(parts, axis=1).astype(BF16)


def pointwise_body(stiffness_in, density_in, p_ref, q_ref, p_mate, q_mate, cells, lift_ref, left, offset, *rest):
    out, right, stiffness, density, semaphores = rest[-5:]
    rows, group, depth = p_ref.shape
    padded_channels = lift_ref.shape[0]
    height = rows * padded_channels
    entries = stiffness.shape[0]
    core = lax.axis_index("gz")
    own = slot() == core

    @pl.when(pl.program_id(0) == 0)
    def _():
        right[...] = jnp.zeros_like(right)
        for copy in begin((stiffness_in, density_in), (stiffness, density), semaphores):
            copy.wait()

    weights = [lift_ref[:, index : index + 1] for index in range(FIELDS + 1)]
    values = []
    for row in range(rows):
        cell = cells[core * rows + row]
        values.append((
            jnp.where(own, p_ref[row], p_mate[row]),
            jnp.where(own, q_ref[row], q_mate[row]),
            looked_up(cell, lambda e: stiffness[e], entries),
            looked_up(cell, lambda e: density[e], entries),
        ))
    for y in range(group):
        lifted = []
        for row in range(rows):
            total = jnp.broadcast_to(weights[FIELDS], (padded_channels, depth))
            for value, weight in zip(values[row], weights):
                total = total + value[y : y + 1, :] * weight
            lifted.append(total)
        right[y, 0:height, :] = jnp.concatenate(lifted, axis=0).astype(BF16)
        out[:, y, :] = jnp.dot(left[...], right[y], preferred_element_type=F32) + offset[...]


def join_body(own, other, wave_out):
    core = lax.axis_index("gz")
    rows, _, depth = own.shape
    half = depth // 2
    place = slot()
    for row in range(rows):
        for ref, start in ((own, place * rows), (other, (1 - place) * rows)):
            wave_out[start + row] = jnp.where(core == 0, ref[row, :, :half], ref[row, :, half:])


def back_columns(spectra, left_y, modes):
    fields, half_x, _, width = spectra.shape
    chunk = min(8, half_x)
    for field in range(fields):
        for start in range(0, half_x, chunk):
            values = [spectra[field, mode].astype(F32) for mode in range(start, start + chunk)]
            stacked = jnp.concatenate([
                jnp.concatenate([value.astype(BF16) for value in values], axis=1),
                jnp.concatenate([turned(value, width // 2, -1.0).astype(BF16) for value in values], axis=1),
            ], axis=0)
            result = jnp.dot(left_y, stacked, preferred_element_type=F32)
            for mode in range(start, start + chunk):
                lanes = slice((mode - start) * width, (mode - start + 1) * width)
                modes[:, mode * fields + field, :] = result[:, lanes]


def own_half_body(mine, table_y, table_z, out, modes):
    back_columns(mine, table_y[lax.axis_index("gy")], modes)
    lines = modes[...].reshape(out.shape[0], modes.shape[2]).astype(BF16)
    out[...] = jnp.dot(lines, table_z[...], preferred_element_type=F32).astype(BF16)


def output_body(
    waves_own, other, local, left, table_y, table_z, features, modes, right,
):
    step = pl.program_id(0)
    core, column = lax.axis_index("gz"), lax.axis_index("gy")
    half_x, modes_y, width = other.shape[1:]
    rows, channels, group, depth = features.shape
    coupled = 2 * FIELDS * half_x
    half_rows = FIELDS * half_x

    @pl.when(step == 0)
    def _():
        back_columns(other, table_y[column], modes)

    base = pl.multiple_of(step * group, group)
    lines = modes[pl.ds(base, group)].reshape(group * half_rows, width).astype(BF16)
    waves = jnp.dot(lines, table_z[...], preferred_element_type=F32).astype(BF16)
    own = waves_own[pl.ds(pl.multiple_of(base * half_rows, group * half_rows), group * half_rows), :]
    count = left.shape[1] // (2 * coupled)
    for y in range(group):
        lines = slice(y * half_rows, (y + 1) * half_rows)
        for values, place in ((own, core), (waves, 1 - core)):
            for part in range(2):
                at = pl.multiple_of(y * 2 * coupled + part * coupled + place * half_rows, half_rows)
                right[pl.ds(at, half_rows), :] = values[lines, part * depth : (part + 1) * depth]
    for first in range(0, group, 2 * count):
        results = []
        for start in (first * 2 * coupled, (first + count) * 2 * coupled):
            results.append(jnp.dot(
                left[...], right[start : start + count * 2 * coupled, :], preferred_element_type=F32
            ))
        for row in range(rows):
            for channel in range(channels):
                at = row * channels + channel
                total = jnp.concatenate([result[at * count : (at + 1) * count] for result in results], axis=0)
                total = total + local[at, pl.ds(base + first, 2 * count), :]
                scale = math.sqrt(2.0 / math.pi)
                inner = total * (scale + (scale * 0.044715) * (total * total))
                part = 0.5 * total
                total = part + part * jnp.tanh(inner)
                features[row, channel, first : first + 2 * count, :] = total.astype(BF16)


def xor_pairs(count, distance):
    return [(index, index ^ distance) for index in range(count)]


def odd_pairs(count):
    pairs = [(index, index + 1) for index in range(1, count - 1, 2)]
    return pairs + [(target, source) for source, target in pairs]


def row_pairs(cycles, columns):
    place = lambda cycle, column, core: (cycle * columns + column) * 2 + core
    pairs = []
    for column in range(columns):
        for cycle in range(cycles - 1):
            one, two = place(cycle, column, 1 - cycle % 2), place(cycle + 1, column, 1 - cycle % 2)
            pairs += [(one, two), (two, one)]
        for cycle, core in ((0, 0), (cycles - 1, 1 - (cycles - 1) % 2)):
            pairs.append((place(cycle, column, core), place(cycle, column ^ 1, core)))
    return pairs


def per_device(
    pressure,
    previous,
    material,
    stiffness,
    density,
    nonlinear,
    lift_weight,
    lift_bias,
    mode_weight,
    local_weight,
):
    brick_x, brick_y, brick_z = pressure.shape
    cycle_count = lax.axis_size("gx")
    column_count = lax.axis_size("gy")
    core_count = lax.axis_size("gz")
    total_x = brick_x * cycle_count
    total_y = brick_y * column_count
    total_z = brick_z * core_count
    modes_x = total_x // 4
    modes_y = total_y // 4
    modes_z = total_z // 4
    width = 2 * modes_z
    channels = lift_bias.shape[0]
    rows = brick_x // core_count
    assert core_count == 2 and rows >= REACH
    blocks = cycle_count * core_count
    padded_channels = -(-channels // 8) * 8
    height = rows * channels
    coupled = FIELDS * modes_x
    right_depth = -(-rows * padded_channels // 128) * 128
    two_sided = column_count > 2

    kept_first = kept_modes(total_x, modes_x)
    kept_second = kept_modes(total_y, modes_y)
    kept_third = np.arange(modes_z)
    cz, sz = cos_sin(np.arange(total_z), kept_third, total_z)
    forward_z = np.concatenate([cz, -sz], 1)
    weight = np.where(kept_third == 0, 1.0, 2.0) / (total_x * total_y * total_z)
    wc, ws = [rounded((t.astype(np.float32) * weight).T.astype(np.float32)) for t in (cz, sz)]
    inverse_z = np.concatenate(
        [np.concatenate([wc, ws], 1), np.concatenate([-ws.astype(np.float32), wc.astype(np.float32)], 1)], 0
    )
    inverse_z = rounded(inverse_z)
    cy, sy = cos_sin(kept_second, np.arange(total_y), total_y)
    cy3, sy3 = [t.reshape(modes_y, column_count, brick_y).transpose(1, 0, 2) for t in (cy, sy)]
    forward_y = np.concatenate([cy3, sy3, cy3, sy3], 2)
    cy3, sy3 = [t.transpose(0, 2, 1) for t in (cy3, sy3)]
    inverse_y = np.concatenate([cy3, sy3], 2)
    cx, sx = [t.astype(np.float32) for t in cos_sin(np.arange(total_x), kept_first, total_x)]
    twiddle_x = np.stack([cx, sx], -1).reshape(-1)
    owner = np.tile(np.eye(channels, dtype=np.float32), (rows, 1))
    turn = np.zeros((blocks, 2, height, coupled), np.float32)
    for source, table in enumerate((cx, sx)):
        turn[:, source] = np.repeat(
            np.repeat(table.reshape(blocks, rows, modes_x), channels, 1), FIELDS, 2
        )
    padded_eye = np.eye(channels, padded_channels, dtype=np.float32)
    wide = np.zeros((channels + height + padded_channels, right_depth), np.float32)
    wide[:channels, : rows * padded_channels] = np.tile(padded_eye, (1, rows))
    wide[channels : channels + height, : rows * padded_channels] = np.kron(
        np.eye(rows), np.ones((channels, padded_channels))
    )
    wide[channels + height :, :channels] = padded_eye.T
    spread = np.repeat(np.eye(channels, dtype=np.float32), modes_x, 0)
    same = np.tile(np.repeat(np.eye(modes_x, dtype=np.float32), FIELDS, 1), (channels, 1))
    spread = np.concatenate([spread, same], 1)
    place = np.tile(np.eye(FIELDS, dtype=np.float32), (1, modes_x))

    def shape(*dims, dtype=F32):
        return jax.ShapeDtypeStruct(dims, dtype)

    cells_count = rows * brick_y * total_z
    field = shape(rows, brick_y, total_z)
    edge = [shape(rows, EDGE, total_z, dtype=BF16)] * (2 if two_sided else 1)

    swap_core = xor_pairs(core_count, 1)
    got = [lax.ppermute(array, "gz", swap_core) for array in (pressure, previous, material)]
    sending = shape(rows, brick_y, total_z, dtype=BF16)
    half = (rows, brick_y, brick_z)
    fetched = call(
        fetch_body,
        [shape(*half), shape(*half), shape(brick_x, brick_y, brick_z, dtype=jnp.int32), shape(2 * stiffness.shape[0], 8, 128)],
        [HBM] * 6, [pltpu.SMEM(stiffness.shape, F32)] * 3 + [pltpu.SemaphoreType.DMA((6,))], moved=cells_count * 8
    )(*here(stiffness, density, nonlinear, pressure, previous, material))
    fetched, got = lax.optimization_barrier((fetched, got))
    current, before, ratio, bend, sent, cells, *edge_values = call(
        lambda *refs: assemble_body(len(edge), *refs),
        [field] * 4 + [sending, shape(brick_x, brick_y, total_z, dtype=jnp.int32)] + edge, [VMEM] * 7,
        moved=cells_count * 36
    )(*fetched, *got)

    weights = (
        stiffness, density, mode_weight.transpose(0, 2, 1, 3), lift_weight, lift_bias.reshape(1, channels),
        local_weight, spread, place, owner, turn, wide,
    )
    mixing, pointwise, lift_table, offset = call(
        prepare_body,
        [shape(height, 2 * coupled, dtype=BF16), shape(height, right_depth, dtype=BF16),
         shape(padded_channels, 8), shape(height, 1)],
        [HBM] * 11, room(*weights[:9], turn[0], wide), flops=2_000_000_000, moved=4_000_000,
    )(*here(*weights))

    part = lambda fields, dtype: shape(fields, modes_x // 2, modes_y, width, dtype=dtype)

    def spectrum(body, outs, inputs, lines, specs=None, scratch=()):
        return call(
            body, outs, specs or [HBM] + [VMEM] * (inputs + 2),
            [pltpu.VMEM((4 * brick_y, lines * width), BF16), pltpu.VMEM((modes_y, lines * width), F32), *scratch],
            flops=cells_count * 256 * lines, moved=cells_count * 2 * lines,
        )

    stages = [(axis, count, 2 ** (bit + 1) - 1) for axis, count in (("gy", column_count), ("gx", cycle_count))
              for bit in range((count - 1).bit_length())]
    swap = lambda value: lax.ppermute(value, "gz", swap_core)

    def exchange(value, axis, count, distance):
        return lax.ppermute(value.astype(BF16), axis, xor_pairs(count, distance))

    tables = (twiddle_x, stiffness, density, forward_z, forward_y)
    early, forward_z, forward_y = spectrum(
        materials_body,
        [part(2, F32)] + [jax.ShapeDtypeStruct(table.shape, table.dtype) for table in (forward_z, forward_y)],
        1, 2 * brick_x, [HBM] * 5 + [VMEM], room(*tables[:3])[:3] + [pltpu.SemaphoreType.DMA((5,))],
    )(*here(*tables), cells)
    twiddles = here(twiddle_x)
    twiddle_room = room(twiddle_x)

    for repeat in range(STEPS):
        last = repeat == STEPS - 1
        far = lax.ppermute(sent, ("gx", "gy", "gz"), row_pairs(cycle_count, column_count))
        mate = swap(current)
        halos = [lax.ppermute(edge_values[0], "gy", xor_pairs(column_count, 1))]
        if two_sided:
            halos.append(lax.ppermute(edge_values[1], "gy", odd_pairs(column_count)))
        if repeat == 0:
            far, early = lax.optimization_barrier((far, early))
        if last:
            prior = spectrum(prior_body, shape(modes_x // 2, modes_y, width), 2, brick_x, None, twiddle_room)(
                *twiddles, current, mate, forward_z, forward_y
            )
            far, prior = lax.optimization_barrier((far, prior))
            prior_mate = mate
        outs = [field] + ([] if last else [sending] + edge)
        body = lambda *refs, last=last: step_body(two_sided, last, *refs)
        new, *others = call(
            body, outs, [VMEM] * (6 + len(halos)),
            [pltpu.VMEM((brick_y + 2 * EDGE, total_z), F32)], flops=cells_count * 60, moved=cells_count * 28,
        )(current, before, ratio, bend, mate, far, *halos)
        if not last:
            sent, *edge_values = others
        current, before = new, current

    total, sent = spectrum(wave_body, [part(FIELDS, F32), part(1, BF16)], 3, rows, None, twiddle_room)(
        *twiddles, current, prior, early, forward_z, forward_y
    )
    total = total + jnp.pad(swap(sent).astype(F32), ((0, FIELDS - 1), (0, 0), (0, 0), (0, 0)))
    wave_other = swap(current)
    group = 8
    steps = brick_y // group
    whole = lambda array: pl.BlockSpec(array.shape, lambda i: (0,) * len(array.shape))

    def pointwise_part(start, held=()):
        slab = lambda count: pl.BlockSpec((count, group, total_z), lambda i: (0, i + start, 0))
        return pl.pallas_call(
            pointwise_body,
            grid=(steps // 2,),
            out_shape=shape(height, brick_y, total_z),
            in_specs=[HBM] * 2 + [slab(rows)] * 4 + [slab(brick_x), whole(lift_table), whole(pointwise), whole(offset)]
            + [pl.BlockSpec(memory_space=pl.ANY)] * len(held),
            out_specs=pl.BlockSpec((height, group, total_z), lambda i: (0, i + start, 0)),
            input_output_aliases={10: 0} if held else {},
            scratch_shapes=[pltpu.VMEM((group, right_depth, total_z), BF16)] + room(stiffness, density),
            compiler_params=pltpu.CompilerParams(vmem_limit_bytes=16 * 1024 * 1024),
            cost_estimate=pl.CostEstimate(flops=cells_count * 20000, bytes_accessed=cells_count * 50, transcendentals=0),
        )(*here(stiffness, density), current, before, wave_other, prior_mate, cells, lift_table, pointwise, offset, *held)

    for index, stage in enumerate(stages):
        arrived = exchange(total, *stage)
        if index == 0:
            arrived, mixing, pointwise, lift_table, offset = lax.optimization_barrier(
                (arrived, mixing, pointwise, lift_table, offset)
            )
        if index == len(stages) - 2:
            local = pointwise_part(0)
            wave = call(join_body, shape(*pressure.shape), [VMEM] * 2, moved=cells_count * 12)(current, wave_other)
            arrived, local, wave = lax.optimization_barrier((arrived, local, wave))
        if index == len(stages) - 1:
            local = pointwise_part(steps // 2, (local,))
            repeats = np.repeat(np.eye(height), 8, 0).astype(ml_dtypes.bfloat16)
            wide_mixing = call(
                widen_body, shape(height * 8, 16 * coupled, dtype=BF16), [VMEM] * 2, flops=1_000_000_000, moved=2_000_000
            )(mixing, repeats)
            arrived, local, wide_mixing = lax.optimization_barrier((arrived, local, wide_mixing))
        total = total + arrived.astype(F32)
    other = swap(total.astype(BF16))
    batch = min(32, brick_y)
    scoped = 10 * 2**20 + 20 * height * 16 * coupled + 4 * (brick_y * coupled * width + 6 * batch * coupled * total_z)
    waves_own = call(
        own_half_body, shape(brick_y * coupled // 2, 2 * total_z, dtype=BF16), [VMEM] * 3,
        [pltpu.VMEM((brick_y, coupled // 2, width), F32)], flops=1_000_000_000, moved=2_000_000, room_bytes=scoped,
    )(total, inverse_y, inverse_z)
    other, waves_own = lax.optimization_barrier((other, waves_own))
    features = pl.pallas_call(
        output_body,
        grid=(brick_y // batch,),
        out_shape=shape(rows, channels, brick_y, total_z, dtype=BF16),
        in_specs=[VMEM, VMEM,
                  VMEM, VMEM, VMEM, VMEM],
        out_specs=pl.BlockSpec((rows, channels, batch, total_z), lambda i: (0, 0, i, 0)),
        scratch_shapes=[
            pltpu.VMEM((brick_y, coupled // 2, width), F32),
            pltpu.VMEM((batch * 2 * coupled, total_z), BF16),
        ],
        compiler_params=pltpu.CompilerParams(vmem_limit_bytes=scoped),
        cost_estimate=pl.CostEstimate(flops=cells_count * 2000, bytes_accessed=cells_count * 60, transcendentals=cells_count * 20),
    )(waves_own, other, local, wide_mixing, inverse_y, inverse_z)
    features = features.transpose(0, 2, 1, 3)
    return (wave, features)


def solution(mesh):
    placed = (
        P(("grp", "gx"), "gy", "gz"),
        P(("grp", "gx"), "gy", "gz"),
        P(("grp", "gx"), "gy", "gz"),
        P(),
        P(),
        P(),
        P(),
        P(),
        P(),
        P(),
    )
    return jax.shard_map(
        per_device,
        mesh=mesh,
        in_specs=placed,
        out_specs=(P(("grp", "gx"), "gy", "gz"), P(("grp", "gx", "gz"), "gy", None, None)),
        check_vma=False,
    )
```
